256 devices in a mesh: grp: 4 (over y), dev: 64 (over x, z, core).
Axes of the slice: x: 4, y: 4, z: 8, core: 2. Of those that a mesh axis runs over, the one named last changes fastest.
Arguments:
- stiffness: bfloat16 [4096, 64, 704], P(('grp', 'dev')), may hold values from -6 to 6
- prolongator: bfloat16 [4096, 4096], P(('grp', 'dev')), may hold values from -0.75 to 0.75
- columns: int32 [4096, 11], P(('grp', 'dev')), may hold values from -1 to 271, as said below
- fetch_rows: int32 [16384, 4], P(('grp', 'dev')), may hold values from 0 to 15, as said below
- send_order: int32 [256, 8], P(('grp', 'dev')), may hold values from 0 to 7, each once within a row
- partner_slot: int32 [256, 8], P(('grp', 'dev')), may hold values from 0 to 7, each once within a row
Outputs:
- coarse_blocks: bfloat16 [2048, 64, 1408], P(('grp', 'dev'))
- coarse_columns: int32 [2048, 22], P(('grp', 'dev'))
The draws below stay inside these ranges and needn't reach their ends.
Inputs may be any that keep to these rules, and one draw needn't show every extreme that they name: `columns`: slot 0 of each row is the row itself; a row's used slots come first and padding (-1) fills the rest of its tile. `fetch_rows`: each row holds 4 distinct rows. `send_order`: each row is a permutation; exactly 2 followers of a device go to each group. `partner_slot`: each row is a permutation.
All inputs are finite; a program needn't handle non-finite values.
Results may differ from the reference program's by a relative error of at most 0.0054.
Values may be sent and summed in bfloat16 or wider, within the bound.
No kernel may reach another device: no remote copies, remote signals or barrier semaphores. Data moves between devices by JAX's collectives and lax.ppermute only.
A program may use at most 64 MiB of HBM per device.

```python
import jax
import jax.numpy as jnp
from jax import lax

BLK = 64
K = 11
C = 4
ROWS_DEV = 16
HALF = 8
NFINE = 4096
NCOARSE = 2048
N_GRP = 4
N_DEV = 64


def draw_columns(key, part):
    key_top = jax.random.fold_in(key, 11)
    key_count = jax.random.fold_in(key, 12)
    key_cols = jax.random.fold_in(key, 13)
    lowest = max(2, K // 4)
    device_top = jax.random.randint(key_top, (N_GRP * N_DEV,), lowest, K + 1)
    row_top = jnp.repeat(device_top, ROWS_DEV)
    counts = jax.random.randint(key_count, (NFINE,), 1, K + 1)
    counts = jnp.minimum(counts, row_top)
    picks = jax.random.randint(key_cols, (NFINE, K), 0, ROWS_DEV + N_DEV * C)
    own_rows = jnp.arange(NFINE, dtype=jnp.int32) % ROWS_DEV
    slot_index = jnp.arange(K, dtype=jnp.int32)[None, :]
    picks = jnp.where(slot_index == 0, own_rows[:, None], picks)
    return jnp.where(slot_index < counts[:, None], picks, -1).astype(jnp.int32)


def draw_fetch_rows(key, part):
    total = N_GRP * N_DEV * N_DEV
    keys = jax.random.split(jax.random.fold_in(key, 21), total)

    def one_row(row_key):
        return jax.random.permutation(row_key, ROWS_DEV)[:C]
    return jax.vmap(one_row)(keys).astype(jnp.int32)


def shard_levels(stream_key, extent, shards, smallest, high):
    level, own = 1.0, jax.random.fold_in(stream_key, 6)
    for axis_at, parts in shards:
        heights = jnp.exp(jax.random.uniform(jax.random.fold_in(own, axis_at), (parts,), jnp.float32, smallest / len(shards), high / len(shards)))
        level = level * jnp.repeat(heights, extent[axis_at] // parts).reshape([-1 if axis == axis_at else 1 for axis in range(len(extent))])
    return level


def normal_values(stream_key, shape, deviation, most, cuts=(), held_as=jnp.bfloat16):
    array = jax.random.normal(stream_key, shape, jnp.float32) * deviation
    if len(cuts) > 0:
        array = shard_levels(stream_key, shape, cuts, -0.22, 0.18) * array
    return jnp.clip(array, min=-most, max=most).astype(held_as)


def setup_inputs(seed: int = 0) -> dict:
    streams_of = jax.random.split(jax.random.key(seed), 7)
    return {
        "stiffness": normal_values(streams_of[0], (NFINE, BLK, K * BLK), 1.0, 6.0, ((0, 256),)),
        "prolongator": normal_values(streams_of[1], (NFINE, BLK * BLK), BLK ** -0.5, 0.75, ((0, 256),)),
        "columns": draw_columns(jax.random.fold_in(streams_of[6], 71), 0),
        "fetch_rows": draw_fetch_rows(jax.random.fold_in(streams_of[6], 71), 0),
        "send_order": jax.vmap(lambda own: jax.random.permutation(own, HALF))(jax.random.split(streams_of[4], (N_GRP * N_DEV))).reshape((N_GRP * N_DEV, HALF)).astype(jnp.int32),
        "partner_slot": jax.vmap(lambda own: jax.random.permutation(own, HALF))(jax.random.split(streams_of[5], (N_GRP * N_DEV))).reshape((N_GRP * N_DEV, HALF)).astype(jnp.int32),
    }


def reference(stiffness, prolongator, columns, fetch_rows, send_order, partner_slot):
    lead_count = ROWS_DEV // 2
    per_group = lead_count // N_GRP
    fine_index = jnp.arange(NFINE, dtype=jnp.int32)
    device_of = fine_index // ROWS_DEV
    local_row = fine_index % ROWS_DEV
    coarse_index = jnp.arange(NCOARSE, dtype=jnp.int32)
    owner_device = coarse_index // lead_count
    leader_slot = coarse_index % lead_count
    target_group = owner_device // N_DEV
    member = owner_device % N_DEV
    position = partner_slot[owner_device, leader_slot]
    source = (position // per_group) * N_DEV + member
    follower = send_order[source, target_group * per_group + position % per_group]
    partner_row = (source * ROWS_DEV + lead_count + follower).astype(jnp.int32)
    leader_row = (owner_device * ROWS_DEV + leader_slot).astype(jnp.int32)
    coarse_label = (device_of * lead_count + local_row).astype(jnp.int32)
    coarse_label = coarse_label.at[partner_row].set(coarse_index)
    group_of = device_of // N_DEV
    ghost_index = jnp.maximum(columns - ROWS_DEV, 0)
    peer_dev = ghost_index // C
    ghost_slot = ghost_index % C
    fetched = fetch_rows[device_of[:, None] * N_DEV + peer_dev, ghost_slot]
    remote = (group_of[:, None] * N_DEV + peer_dev) * ROWS_DEV + fetched
    global_col = jnp.where(columns < 0, -1, jnp.where(columns < ROWS_DEV, device_of[:, None] * ROWS_DEV + columns, remote)).astype(jnp.int32)
    column_label = jnp.where(global_col < 0, -1, coarse_label[jnp.maximum(global_col, 0)]).astype(jnp.int32)
    hp = lax.Precision.HIGHEST

    def restrict_rows(row_index):
        count_rows = row_index.shape[0]
        stiff_tiles = stiffness[row_index].astype(jnp.float32).reshape(count_rows, BLK, K, BLK)
        global_cols = global_col[row_index]
        present = (global_cols >= 0).astype(jnp.float32)
        picked = prolongator[jnp.maximum(global_cols, 0)].astype(jnp.float32).reshape(count_rows, K, BLK, BLK)
        picked = picked * present[:, :, None, None]
        applied = jnp.einsum('iakb,ikbc->ikac', stiff_tiles, picked, precision=hp).astype(jnp.bfloat16)
        own_block = prolongator[row_index].astype(jnp.float32).reshape(count_rows, BLK, BLK)
        return jnp.einsum('iac,ikad->ikcd', own_block, applied.astype(jnp.float32), precision=hp).astype(jnp.bfloat16)

    def per_device(device_number):
        lead_rows = lax.dynamic_slice_in_dim(leader_row, device_number * lead_count, lead_count)
        part_rows = lax.dynamic_slice_in_dim(partner_row, device_number * lead_count, lead_count)
        blocks = jnp.concatenate([restrict_rows(lead_rows), restrict_rows(part_rows)], axis=1)
        labels = jnp.concatenate([column_label[lead_rows], column_label[part_rows]], axis=1)
        matches = (labels[:, :, None] == labels[:, None, :]).astype(jnp.float32)
        merged = jnp.einsum('nst,ntcd->ncsd', matches, blocks.astype(jnp.float32), precision=hp)
        merged = merged.astype(jnp.bfloat16).reshape(lead_count, BLK, 2 * K * BLK)
        return merged, labels

    merged, labels = lax.map(per_device, jnp.arange(N_GRP * N_DEV, dtype=jnp.int32))
    return merged.reshape(NCOARSE, BLK, 2 * K * BLK), labels.reshape(NCOARSE, 2 * K)
```

```python
import jax
import jax.numpy as jnp
from jax import lax
from jax.experimental import pallas as pl
from jax.experimental.pallas import tpu as pltpu
from jax.sharding import Mesh, PartitionSpec as P

BLK = 64
K = 11
C = 4
ROWS = 16
HALF = 8
NG, NX, NZ, NC = 4, 4, 8, 2
N_DEV = NX * NZ * NC
LANES = 128
SLOTS = 12
WIDE = SLOTS * BLK
TABLE = N_DEV * C
CHUNKS = 1
CK = 32 // CHUNKS
AXES = ("grp", "x", "z", "core")

VMEM = pl.BlockSpec(memory_space=pltpu.VMEM)
SMEM = pl.BlockSpec(memory_space=pltpu.SMEM)
LIMIT = pltpu.CompilerParams(vmem_limit_bytes=40 * 1024 * 1024)


def low_lanes(shape):
    return lax.broadcasted_iota(jnp.int32, shape, 1) < BLK


def products_kernel(p_ref, a_ref, perm_ref, y_ref):
    def row(i, carry):
        y = lax.dot_general(
            p_ref[i], a_ref[i], (((0,), (0,)), ((), ())), preferred_element_type=jnp.float32
        )
        y = jnp.concatenate([y, jnp.zeros((BLK, BLK), jnp.float32)], axis=1)
        y = jnp.where(i < HALF, y, pltpu.roll(y, BLK, 1)).astype(jnp.bfloat16)
        for t in range(WIDE // LANES):
            span = slice(t * LANES, (t + 1) * LANES)
            y_ref[i, :, span] = jnp.dot(
                y[:, span], perm_ref[...], preferred_element_type=jnp.float32
            ).astype(jnp.bfloat16)
        return carry

    lax.fori_loop(0, ROWS, row, 0)


def products(blocks, stiffness, perm):
    return pl.pallas_call(
        products_kernel,
        out_shape=jax.ShapeDtypeStruct((ROWS, BLK, WIDE), jnp.bfloat16),
        compiler_params=LIMIT,
        cost_estimate=pl.CostEstimate(
            flops=2 * ROWS * BLK * BLK * WIDE * 3, bytes_accessed=3_200_000, transcendentals=0
        ),
        name="products",
    )(blocks, stiffness, perm)


def select_kernel(wanted_ref, place_ref, *refs):
    held, outs = refs[:NZ], refs[NZ:]
    x, z, c = place_ref[1], place_ref[2], place_ref[3]
    for b in range(NX * NC):
        target = ((x + b // NC) & (NX - 1)) * NC + (c ^ (b % NC))
        for s in range(NZ):
            home = ((z - s) & (NZ - 1)) * C
            for m in range(C):
                outs[b][home + m] = held[s][wanted_ref[target, home + m]]


def select(wanted, place, held):
    shape = jax.ShapeDtypeStruct((NZ * C, CK, LANES), jnp.bfloat16)
    return pl.pallas_call(
        select_kernel,
        out_shape=[shape] * (NX * NC),
        in_specs=[SMEM, SMEM] + [VMEM] * NZ,
        out_specs=[VMEM] * (NX * NC),
        compiler_params=LIMIT,
        name="select",
    )(wanted, place, *held)


def fill(table, own_ref, parts):
    n = NX * NC
    for h in range(CHUNKS):
        for b in range(n):
            table[b * NZ * C:(b + 1) * NZ * C, h * CK:(h + 1) * CK] = parts[h * n + b][...]
    table[TABLE:TABLE + ROWS] = own_ref[...]
    table[TABLE + ROWS] = jnp.zeros((32, LANES), jnp.bfloat16)


def row_tiles(i, table, at_ref, y_ref, emit):
    low = low_lanes((32, LANES))
    zero = jnp.zeros((32, LANES), jnp.bfloat16)
    for t in range(SLOTS // 2):
        a = table[at_ref[i, 2 * t]]
        b = table[at_ref[i, 2 * t + 1]]
        rhs = jnp.concatenate([
            jnp.where(low, a, zero),
            jnp.where(low, pltpu.roll(a, BLK, 1), zero),
            jnp.where(low, zero, pltpu.roll(b, BLK, 1)),
            jnp.where(low, zero, b),
        ], axis=0)
        span = slice(t * LANES, (t + 1) * LANES)
        emit(span, jnp.dot(
            y_ref[i, :, span], rhs, preferred_element_type=jnp.float32
        ).astype(jnp.bfloat16))


def follower_kernel(at_ref, place_ref, send_ref, own_ref, y_ref, *refs):
    n = NX * NC * CHUNKS
    parts, outs, table = refs[:n], refs[n:n + NG], refs[n + NG]
    fill(table, own_ref, parts)
    for s in range(NG):
        target = (place_ref[0] + s) & (NG - 1)
        for q in range(2):
            row = HALF + send_ref[0, target * 2 + q]

            def emit(span, value, s=s, q=q):
                outs[s][q, :, span] = value

            row_tiles(row, table, at_ref, y_ref, emit)


def leader_kernel(at_ref, own_ref, y_ref, *refs):
    n = NX * NC * CHUNKS
    parts, out, table = refs[:n], refs[n], refs[n + 1]
    fill(table, own_ref, parts)

    def row(i, carry):
        def emit(span, value):
            out[i, :, span] = value

        row_tiles(i, table, at_ref, y_ref, emit)
        return carry

    lax.fori_loop(0, HALF, row, 0)


SCRATCH = [pltpu.VMEM((TABLE + ROWS + 1, 32, LANES), jnp.bfloat16)]
ROW_COST = pl.CostEstimate(flops=2 * 8 * 6 * BLK * LANES * LANES, bytes_accessed=5_000_000, transcendentals=0)


def followers(at, place, send, own, y, parts):
    shape = jax.ShapeDtypeStruct((2, BLK, WIDE), jnp.bfloat16)
    return pl.pallas_call(
        follower_kernel,
        out_shape=[shape] * NG,
        in_specs=[SMEM] * 3 + [VMEM] * (2 + len(parts)),
        out_specs=[VMEM] * NG,
        scratch_shapes=SCRATCH,
        compiler_params=LIMIT,
        cost_estimate=ROW_COST,
        name="followers",
    )(at, place, send, own, y, *parts)


def leaders(at, own, y, parts):
    return pl.pallas_call(
        leader_kernel,
        out_shape=jax.ShapeDtypeStruct((HALF, BLK, WIDE), jnp.bfloat16),
        in_specs=[SMEM] + [VMEM] * (2 + len(parts)),
        out_specs=VMEM,
        scratch_shapes=SCRATCH,
        compiler_params=LIMIT,
        cost_estimate=ROW_COST,
        name="leaders",
    )(at, own, y, *parts)


def merge_kernel(place_ref, slots_ref, match_ref, extra_ref, lead_ref, *refs):
    parts, out, follow, work = refs[:NG], refs[NG], refs[NG + 1], refs[NG + 2]
    for s in range(NG):
        follow[2 * s:2 * s + 2] = parts[s][...]
    low = low_lanes((BLK, LANES))
    tiles = SLOTS // 2

    def row(n, carry):
        spot = slots_ref[0, n]
        f = ((place_ref[0] - (spot >> 1)) & (NG - 1)) * 2 + (spot & 1)

        def lead(t):
            return lead_ref[n, :, t * LANES:(t + 1) * LANES]

        def part(t):
            return follow[f, :, t * LANES:(t + 1) * LANES]

        first, second = lead(0).astype(jnp.float32), part(0).astype(jnp.float32)
        out[n, :, 0:LANES] = (first + pltpu.roll(second, BLK, 1)).astype(jnp.bfloat16)
        middle = lead(tiles - 1).astype(jnp.float32) + second
        middle = middle + jnp.where(low, 0.0, pltpu.roll(first, BLK, 1))
        out[n, :, 5 * LANES:6 * LANES] = middle.astype(jnp.bfloat16)
        for t in range(1, tiles - 1):
            out[n, :, t * LANES:(t + 1) * LANES] = lead(t)
        for t in range(1, tiles):
            out[n, :, (5 + t) * LANES:(6 + t) * LANES] = part(t)

        @pl.when(extra_ref[0, n] != 0)
        def _():
            for t in range(tiles):
                work[t] = lead(t).astype(jnp.float32)
                work[tiles + t] = part(t).astype(jnp.float32)
            for s in range(2 * K):
                mask = match_ref[n, s]

                @pl.when(mask != 0)
                def _(s=s, mask=mask):
                    def term(t, total):
                        spot = jnp.where(t < K, t, t + 2)
                        block = work[spot >> 1]
                        turned = pltpu.roll(block, BLK, 1)
                        same = jnp.broadcast_to((spot & 1) == (s & 1), block.shape)
                        taken = jnp.broadcast_to(((mask >> t) & 1) == 1, block.shape)
                        return total + jnp.where(taken, jnp.where(same, block, turned), 0.0)

                    total = lax.fori_loop(0, 2 * K, term, jnp.zeros((BLK, LANES), jnp.float32))
                    span = slice((s // 2) * LANES, (s // 2 + 1) * LANES)
                    keep = low if s % 2 == 0 else jnp.logical_not(low)
                    out[n, :, span] = jnp.where(
                        keep, total, out[n, :, span].astype(jnp.float32)
                    ).astype(jnp.bfloat16)

        return carry

    lax.fori_loop(0, HALF, row, 0)


def merge(place, slots, match, extra, lead, parts):
    return pl.pallas_call(
        merge_kernel,
        out_shape=jax.ShapeDtypeStruct((HALF, BLK, 2 * K * BLK), jnp.bfloat16),
        in_specs=[SMEM] * 4 + [VMEM] * (1 + NG),
        scratch_shapes=[
            pltpu.VMEM((2 * NG, BLK, WIDE), jnp.bfloat16),
            pltpu.VMEM((SLOTS, BLK, LANES), jnp.float32),
        ],
        compiler_params=LIMIT,
        name="merge",
    )(place, slots, match, extra, lead, *parts)


def shift(value, axis, size, by):
    if by == 0:
        return value
    return lax.ppermute(value, axis, [(i, (i + by) % size) for i in range(size)])


def cross(value, b):
    by, flip = b // NC, b % NC
    pairs = [
        (x * NC + c, ((x + by) % NX) * NC + (c ^ flip)) for x in range(NX) for c in range(NC)
    ]
    return lax.ppermute(value, ("x", "core"), pairs)


def per_device(stiffness, prolongator, columns, fetch_rows, send_order, partner_slot):
    g, x, z, c = (lax.axis_index(name) for name in AXES)
    device = x * (NZ * NC) + z * NC + c
    place = jnp.stack([g, x, z, c]).astype(jnp.int32)
    own = prolongator.reshape(ROWS, 32, LANES)

    held = []
    for h in range(CHUNKS):
        piece = own[:, h * CK:(h + 1) * CK]
        got = {0: piece}
        for s in (4, 3, 5, 2, 6, 1, 7):
            got[s] = shift(piece, "z", NZ, s)
        held.append([got[s] for s in range(NZ)])

    lists = fetch_rows.reshape(NX, NZ, NC, C).transpose(0, 2, 1, 3).reshape(NX * NC, NZ * C)
    wanted = lax.all_to_all(lists, ("x", "core"), split_axis=0, concat_axis=0, tiled=True)

    sending, slots = send_order[0], partner_slot[0]
    eight = jnp.arange(HALF, dtype=jnp.int32)
    codes = jnp.sum(jnp.where(slots[:, None] == eight[None, :], (g * HALF + eight)[:, None], 0), axis=0)
    returned = lax.all_to_all(codes, "grp", split_axis=0, concat_axis=0, tiled=True)
    follower_codes = jnp.sum(jnp.where(sending[:, None] == eight[None, :], returned[:, None], 0), axis=0)
    peer_codes = lax.all_to_all(
        jnp.broadcast_to(follower_codes[None, :], (N_DEV, HALF)),
        ("x", "z", "core"), split_axis=0, concat_axis=0, tiled=True,
    )
    picked = jnp.sum(
        jnp.where(fetch_rows[:, :, None] - HALF == eight, peer_codes[:, None, :], 0), axis=2
    )
    ghost_codes = jnp.where(fetch_rows < HALF, g * HALF + fetch_rows, picked)
    peers = jnp.arange(N_DEV, dtype=jnp.int32)[:, None]
    ghost_labels = (((ghost_codes >> 3) * N_DEV + peers) * HALF + (ghost_codes & 7)).reshape(-1)
    own_codes = jnp.concatenate([g * HALF + eight, follower_codes])
    own_labels = ((own_codes >> 3) * N_DEV + device) * HALF + (own_codes & 7)
    label_table = jnp.concatenate([own_labels, ghost_labels])
    present = columns >= 0
    taken = jnp.take(label_table, jnp.maximum(columns, 0), mode="clip")
    column_labels = jnp.where(present, taken, -1).astype(jnp.int32)
    follower_labels = jnp.take(column_labels[HALF:], sending, axis=0, mode="clip")
    arrived_labels = lax.all_to_all(follower_labels, "grp", split_axis=0, concat_axis=0, tiled=True)
    partner_labels = jnp.take(arrived_labels, slots, axis=0, mode="clip")
    labels = jnp.concatenate([column_labels[:HALF], partner_labels], axis=1)

    every = jnp.arange(2 * K, dtype=jnp.int32)
    same = (labels[:, :, None] == labels[:, None, :]) & (labels >= 0)[:, :, None]
    match = jnp.sum(jnp.where(same, 1 << every[None, None, :], 0), axis=2).astype(jnp.int32)
    alone = jnp.where((every == 0) | (every == K), 1 | (1 << K), 1 << every)
    match = jnp.where(match == alone[None, :], 0, match)
    extra = jnp.max(jnp.where(match != 0, 1, 0), axis=1).astype(jnp.int32)[None, :]

    ghost = columns - ROWS
    peer = ghost >> 2
    way = ((x - (peer >> 4)) & (NX - 1)) * NC + (c ^ (peer & 1))
    at = way * (NZ * C) + ((peer >> 1) & (NZ - 1)) * C + (ghost & 3)
    at = jnp.where(columns < ROWS, TABLE + columns, at)
    at = jnp.where(present, at, TABLE + ROWS).astype(jnp.int32)
    none = jnp.full((HALF, 1), TABLE + ROWS, jnp.int32)
    at = jnp.concatenate([
        jnp.concatenate([at[:HALF], none], axis=1),
        jnp.concatenate([none, at[HALF:]], axis=1),
    ])

    lane = jnp.arange(LANES, dtype=jnp.int32)
    inner = lane & (BLK - 1)
    source = (lane & BLK) + jnp.where(inner < 32, 2 * inner, 2 * (inner - 32) + 1)
    perm = (lane[:, None] == source[None, :]).astype(jnp.bfloat16)
    y = products(prolongator.reshape(ROWS, BLK, BLK), stiffness, perm)

    parts = []
    for h in range(CHUNKS):
        chosen = select(wanted, place, held[h])
        parts.append(chosen[0])
        for b in range(1, NX * NC):
            parts.append(cross(chosen[b], b))

    sent = followers(at, place, send_order, own, y, parts)
    arrived = [sent[0]] + [shift(sent[s], "grp", NG, s) for s in range(1, NG)]
    lead = leaders(at, own, y, parts)
    merged = merge(place, partner_slot, match, extra, lead, arrived)
    return (merged, labels)


def solution(mesh):
    grid = Mesh(mesh.devices.reshape(NG, NX, NZ, NC), AXES)
    return jax.shard_map(
        per_device,
        mesh=grid,
        in_specs=(
            P(AXES, None, None),
            P(AXES, None),
            P(AXES, None),
            P(AXES, None),
            P(AXES, None),
            P(AXES, None),
        ),
        out_specs=(P(AXES, None, None), P(AXES, None)),
        check_vma=False,
    )
```

```python
import jax
import jax.numpy as jnp
from jax import lax
from jax.experimental import pallas as pl
from jax.experimental.pallas import tpu as pltpu
from jax.sharding import Mesh, PartitionSpec as P

BLK = 64
K = 11
C = 4
ROWS = 16
HALF = 8
NG, NX, NZ, NC = 4, 4, 8, 2
N_DEV = NX * NZ * NC
LANES = 128
SLOTS = 12
WIDE = SLOTS * BLK
TABLE = N_DEV * C
CHUNKS = 1
CK = 32 // CHUNKS
AXES = ("grp", "x", "z", "core")

VMEM = pl.BlockSpec(memory_space=pltpu.VMEM)
SMEM = pl.BlockSpec(memory_space=pltpu.SMEM)
LIMIT = pltpu.CompilerParams(vmem_limit_bytes=40 * 1024 * 1024)


def low_lanes(shape):
    return lax.broadcasted_iota(jnp.int32, shape, 1) < BLK


def products_kernel(p_ref, a_ref, perm_ref, y_ref):
    def row(i, carry):
        y = lax.dot_general(
            p_ref[i], a_ref[i], (((0,), (0,)), ((), ())), preferred_element_type=jnp.float32
        )
        y = jnp.concatenate([y, jnp.zeros((BLK, BLK), jnp.float32)], axis=1)
        y = jnp.where(i < HALF, y, pltpu.roll(y, BLK, 1)).astype(jnp.bfloat16)
        for t in range(WIDE // LANES):
            span = slice(t * LANES, (t + 1) * LANES)
            y_ref[i, :, span] = jnp.dot(
                y[:, span], perm_ref[...], preferred_element_type=jnp.float32
            ).astype(jnp.bfloat16)
        return carry

    lax.fori_loop(0, ROWS, row, 0, unroll=4)


def products(blocks, stiffness, perm):
    return pl.pallas_call(
        products_kernel,
        out_shape=jax.ShapeDtypeStruct((ROWS, BLK, WIDE), jnp.bfloat16),
        compiler_params=LIMIT,
        cost_estimate=pl.CostEstimate(
            flops=2 * ROWS * BLK * BLK * WIDE * 3, bytes_accessed=3_200_000, transcendentals=0
        ),
        name="products",
    )(blocks, stiffness, perm)


def select_kernel(wanted_ref, place_ref, *refs):
    held, outs = refs[:NZ], refs[NZ:]
    x, z, c = place_ref[1], place_ref[2], place_ref[3]
    for b in range(NX * NC):
        target = ((x + b // NC) & (NX - 1)) * NC + (c ^ (b % NC))
        for s in range(NZ):
            home = ((z - s) & (NZ - 1)) * C
            for m in range(C):
                outs[b][home + m] = held[s][wanted_ref[target, home + m]]


def select(wanted, place, held):
    shape = jax.ShapeDtypeStruct((NZ * C, CK, LANES), jnp.bfloat16)
    return pl.pallas_call(
        select_kernel,
        out_shape=[shape] * (NX * NC),
        in_specs=[SMEM, SMEM] + [VMEM] * NZ,
        out_specs=[VMEM] * (NX * NC),
        compiler_params=LIMIT,
        name="select",
    )(wanted, place, *held)


def fill(table, own_ref, parts):
    n = NX * NC
    for h in range(CHUNKS):
        for b in range(n):
            table[b * NZ * C:(b + 1) * NZ * C, h * CK:(h + 1) * CK] = parts[h * n + b][...]
    table[TABLE:TABLE + ROWS] = own_ref[...]
    table[TABLE + ROWS] = jnp.zeros((32, LANES), jnp.bfloat16)


def row_tiles(i, table, at_ref, y_ref, emit):
    low = low_lanes((32, LANES))
    zero = jnp.zeros((32, LANES), jnp.bfloat16)
    for t in range(SLOTS // 2):
        a = table[at_ref[i, 2 * t]]
        b = table[at_ref[i, 2 * t + 1]]
        rhs = jnp.concatenate([
            jnp.where(low, a, zero),
            jnp.where(low, pltpu.roll(a, BLK, 1), zero),
            jnp.where(low, zero, pltpu.roll(b, BLK, 1)),
            jnp.where(low, zero, b),
        ], axis=0)
        span = slice(t * LANES, (t + 1) * LANES)
        emit(span, jnp.dot(
            y_ref[i, :, span], rhs, preferred_element_type=jnp.float32
        ).astype(jnp.bfloat16))


def follower_kernel(at_ref, place_ref, send_ref, own_ref, y_ref, *refs):
    n = NX * NC * CHUNKS
    parts, outs, table = refs[:n], refs[n:n + NG], refs[n + NG]
    fill(table, own_ref, parts)
    for s in range(NG):
        target = (place_ref[0] + s) & (NG - 1)
        for q in range(2):
            row = HALF + send_ref[0, target * 2 + q]

            def emit(span, value, s=s, q=q):
                outs[s][q, :, span] = value

            row_tiles(row, table, at_ref, y_ref, emit)


def leader_kernel(at_ref, own_ref, y_ref, *refs):
    n = NX * NC * CHUNKS
    parts, out, table = refs[:n], refs[n], refs[n + 1]
    fill(table, own_ref, parts)

    def row(i, carry):
        def emit(span, value):
            out[i, :, span] = value

        row_tiles(i, table, at_ref, y_ref, emit)
        return carry

    lax.fori_loop(0, HALF, row, 0)


SCRATCH = [pltpu.VMEM((TABLE + ROWS + 1, 32, LANES), jnp.bfloat16)]
ROW_COST = pl.CostEstimate(flops=2 * 8 * 6 * BLK * LANES * LANES, bytes_accessed=5_000_000, transcendentals=0)


def followers(at, place, send, own, y, parts):
    shape = jax.ShapeDtypeStruct((2, BLK, WIDE), jnp.bfloat16)
    return pl.pallas_call(
        follower_kernel,
        out_shape=[shape] * NG,
        in_specs=[SMEM] * 3 + [VMEM] * (2 + len(parts)),
        out_specs=[VMEM] * NG,
        scratch_shapes=SCRATCH,
        compiler_params=LIMIT,
        cost_estimate=ROW_COST,
        name="followers",
    )(at, place, send, own, y, *parts)


def leaders(at, own, y, parts):
    return pl.pallas_call(
        leader_kernel,
        out_shape=jax.ShapeDtypeStruct((HALF, BLK, WIDE), jnp.bfloat16),
        in_specs=[SMEM] + [VMEM] * (2 + len(parts)),
        out_specs=VMEM,
        scratch_shapes=SCRATCH,
        compiler_params=LIMIT,
        cost_estimate=ROW_COST,
        name="leaders",
    )(at, own, y, *parts)


def places_kernel(place_ref, columns_ref, fetch_ref, codes_ref, mine_ref, send_ref, at_ref, lead_ref, follow_ref):
    g, x, z, c = (place_ref[i] for i in range(4))
    device = x * (NZ * NC) + z * NC + c

    def slot(i, k):
        column = columns_ref[i, k]
        ghost = jnp.maximum(column - ROWS, 0)
        peer, m = ghost >> 2, ghost & 3
        px, pz, pc = peer >> 4, (peer >> 1) & (NZ - 1), peer & 1
        way = ((x - px) & (NX - 1)) * NC + (c ^ pc)
        local = column < ROWS
        at = jnp.where(local, TABLE + column, way * (NZ * C) + pz * C + m)
        row = jnp.where(local, jnp.maximum(column, 0), fetch_ref[peer, m])
        late = jnp.maximum(row - HALF, 0)
        code = jnp.where(local, mine_ref[late], codes_ref[px * NC + pc, pz * HALF + late])
        code = jnp.where(row < HALF, g * HALF + row, code)
        owner = jnp.where(local, device, peer)
        label = ((code >> 3) * N_DEV + owner) * HALF + (code & 7)
        present = column >= 0
        return jnp.where(present, at, TABLE + ROWS), jnp.where(present, label, -1)

    def row(i, carry):
        follower = send_ref[0, i] + HALF
        at_ref[i, K] = TABLE + ROWS
        at_ref[follower, 0] = TABLE + ROWS
        for k in range(K):
            at_ref[i, k], lead_ref[i, k] = slot(i, k)
            at_ref[follower, k + 1], follow_ref[i, k] = slot(follower, k)
        return carry

    lax.fori_loop(0, HALF, row, 0)


def places(place, columns, fetch, codes, mine, send):
    labels = jax.ShapeDtypeStruct((HALF, K), jnp.int32)
    return pl.pallas_call(
        places_kernel,
        out_shape=[jax.ShapeDtypeStruct((ROWS, SLOTS), jnp.int32), labels, labels],
        in_specs=[SMEM] * 6,
        out_specs=[SMEM] * 3,
        name="places",
    )(place, columns, fetch, codes, mine, send)


def chains_kernel(slots_ref, lead_ref, arrived_ref, labels_ref, next_ref, work_ref):
    lane = lax.broadcasted_iota(jnp.int32, (HALF, LANES), 1)
    work_ref[...] = jnp.full((HALF, LANES), -1, jnp.int32)
    work_ref[:, 0:K] = lead_ref[...]
    for l in range(HALF):
        work_ref[l:l + 1, K:2 * K] = arrived_ref[pl.ds(slots_ref[0, l], 1), :]
    labels = work_ref[...]
    labels_ref[...] = work_ref[:, 0:2 * K]
    twice = jnp.where(lane < 2 * K, labels, pltpu.roll(labels, 2 * K, 1))
    steps = jnp.full((HALF, LANES), 2 * K, jnp.int32)
    for d in range(2 * K - 1, 0, -1):
        steps = jnp.where(pltpu.roll(twice, LANES - d, 1) == labels, d, steps)
    steps = jnp.where((lane < 2 * K) & (labels >= 0), steps, 2 * K)
    usual = jnp.where((lane == 0) | (lane == K), K, 2 * K)
    odd = jnp.max(jnp.where(steps != usual, 1, 0), axis=1, keepdims=True)
    next_ref[...] = jnp.where(lane == 2 * K, odd, steps)


def chains(slots, lead, arrived):
    return pl.pallas_call(
        chains_kernel,
        out_shape=[
            jax.ShapeDtypeStruct((HALF, 2 * K), jnp.int32),
            jax.ShapeDtypeStruct((HALF, LANES), jnp.int32),
        ],
        in_specs=[SMEM, VMEM, VMEM],
        out_specs=[VMEM, VMEM],
        scratch_shapes=[pltpu.VMEM((HALF, LANES), jnp.int32)],
        name="chains",
    )(slots, lead, arrived)


def merge_kernel(place_ref, slots_ref, next_ref, lead_ref, *refs):
    parts, out, tiles, stage, sems = refs[:NG], refs[NG], refs[NG + 1], refs[NG + 2], refs[NG + 3]
    per = SLOTS // 2
    for t in range(per):
        span = slice(t * LANES, (t + 1) * LANES)
        for n in range(HALF):
            tiles[n * per + t] = lead_ref[n, :, span]
        for s in range(NG):
            for q in range(2):
                tiles[(HALF + 2 * s + q) * per + t] = parts[s][q, :, span]
    low = low_lanes((BLK, LANES))

    def save(n):
        return pltpu.make_async_copy(stage.at[n], out.at[n], sems.at[n])

    for n in range(HALF):
        spot = slots_ref[0, n]
        f = (HALF + ((place_ref[0] - (spot >> 1)) & (NG - 1)) * 2 + (spot & 1)) * per
        l = n * per
        first, second = tiles[l].astype(jnp.float32), tiles[f].astype(jnp.float32)
        stage[n, :, 0:LANES] = (first + pltpu.roll(second, BLK, 1)).astype(jnp.bfloat16)
        middle = tiles[l + per - 1].astype(jnp.float32) + second
        middle = middle + jnp.where(low, 0.0, pltpu.roll(first, BLK, 1))
        stage[n, :, 5 * LANES:6 * LANES] = middle.astype(jnp.bfloat16)
        for t in range(1, per - 1):
            stage[n, :, t * LANES:(t + 1) * LANES] = tiles[l + t]
        for t in range(1, per):
            stage[n, :, (5 + t) * LANES:(6 + t) * LANES] = tiles[f + t]

        @pl.when(next_ref[n, 2 * K] != 0)
        def _(n=n, f=f, l=l):
            plain = (next_ref[n, 0] == K) & (next_ref[n, K] == K)
            for s in range(2 * K):
                step = next_ref[n, s]
                skip = plain if s in (0, K) else step == 2 * K

                @pl.when(jnp.logical_not(skip))
                def _(s=s, step=step):
                    def block(t):
                        spot = jnp.where(t < K, t, t - K + 1)
                        value = tiles[jnp.where(t < K, l, f) + (spot >> 1)].astype(jnp.float32)
                        same = jnp.broadcast_to((spot & 1) == (place & 1), value.shape)
                        return jnp.where(same, value, pltpu.roll(value, BLK, 1))

                    place = s if s < K else s - K + 1

                    def more(carry):
                        return carry[0] != s

                    def add(carry):
                        t, total = carry
                        after = t + next_ref[n, t]
                        after = jnp.where(after >= 2 * K, after - 2 * K, after)
                        return after, total + block(t)

                    after = s + step
                    after = jnp.where(after >= 2 * K, after - 2 * K, after)
                    _, total = lax.while_loop(more, add, (after, block(jnp.int32(s))))
                    span = slice((s // 2) * LANES, (s // 2 + 1) * LANES)
                    keep = low if s % 2 == 0 else jnp.logical_not(low)
                    stage[n, :, span] = jnp.where(
                        keep, total, stage[n, :, span].astype(jnp.float32)
                    ).astype(jnp.bfloat16)

        save(n).start()
    for n in range(HALF):
        save(n).wait()


def merge(place, slots, after, lead, parts):
    return pl.pallas_call(
        merge_kernel,
        out_shape=jax.ShapeDtypeStruct((HALF, BLK, 2 * K * BLK), jnp.bfloat16),
        in_specs=[SMEM] * 3 + [VMEM] * (1 + NG),
        out_specs=pl.BlockSpec(memory_space=pl.ANY),
        scratch_shapes=[
            pltpu.VMEM((2 * HALF * SLOTS // 2, BLK, LANES), jnp.bfloat16),
            pltpu.VMEM((HALF, BLK, 2 * K * BLK), jnp.bfloat16),
            pltpu.SemaphoreType.DMA((HALF,)),
        ],
        compiler_params=LIMIT,
        name="merge",
    )(place, slots, after, lead, *parts)


def shift(value, axis, size, by):
    if by == 0:
        return value
    return lax.ppermute(value, axis, [(i, (i + by) % size) for i in range(size)])


def cross(value, b):
    by, flip = b // NC, b % NC
    pairs = [
        (x * NC + c, ((x + by) % NX) * NC + (c ^ flip)) for x in range(NX) for c in range(NC)
    ]
    return lax.ppermute(value, ("x", "core"), pairs)


def per_device(stiffness, prolongator, columns, fetch_rows, send_order, partner_slot):
    g, x, z, c = (lax.axis_index(name) for name in AXES)
    device = x * (NZ * NC) + z * NC + c
    place = jnp.stack([g, x, z, c]).astype(jnp.int32)
    own = prolongator.reshape(ROWS, 32, LANES)

    held = []
    for h in range(CHUNKS):
        piece = own[:, h * CK:(h + 1) * CK]
        got = {0: piece}
        for s in (4, 2, 6, 1, 7):
            got[s] = shift(piece, "z", NZ, s)
        got[5] = shift(got[4], "z", NZ, 1)
        got[3] = shift(got[4], "z", NZ, NZ - 1)
        held.append([got[s] for s in range(NZ)])

    lists = fetch_rows.reshape(NX, NZ, NC, C).transpose(0, 2, 1, 3).reshape(NX * NC, NZ * C)
    wanted = lax.all_to_all(lists, ("x", "core"), split_axis=0, concat_axis=0, tiled=True)

    sending, slots = send_order[0], partner_slot[0]
    eight = jnp.arange(HALF, dtype=jnp.int32)
    codes = jnp.sum(jnp.where(slots[:, None] == eight[None, :], (g * HALF + eight)[:, None], 0), axis=0)
    returned = lax.all_to_all(codes, "grp", split_axis=0, concat_axis=0, tiled=True)
    mine = jnp.sum(jnp.where(sending[:, None] == eight[None, :], returned[:, None], 0), axis=0)
    line = lax.all_to_all(
        jnp.broadcast_to(mine[None, :], (NZ, HALF)), "z", split_axis=0, concat_axis=0, tiled=True
    )
    plane = lax.all_to_all(
        jnp.broadcast_to(line.reshape(1, NZ * HALF), (NX * NC, NZ * HALF)),
        ("x", "core"), split_axis=0, concat_axis=0, tiled=True,
    )
    at, lead_labels, follower_labels = places(place, columns, fetch_rows, plane, mine, send_order)
    arrived_labels = lax.all_to_all(follower_labels, "grp", split_axis=0, concat_axis=0, tiled=True)
    labels, after = chains(partner_slot, lead_labels, arrived_labels)

    lane = jnp.arange(LANES, dtype=jnp.int32)
    inner = lane & (BLK - 1)
    source = (lane & BLK) + jnp.where(inner < 32, 2 * inner, 2 * (inner - 32) + 1)
    perm = (lane[:, None] == source[None, :]).astype(jnp.bfloat16)
    y = products(prolongator.reshape(ROWS, BLK, BLK), stiffness, perm)

    parts = []
    for h in range(CHUNKS):
        chosen = select(wanted, place, held[h])
        parts.append(chosen[0])
        moved = {b: cross(chosen[b], b) for b in (4, 5, 2, 3, 6, 7, 1)}
        parts += [moved[b] for b in range(1, NX * NC)]

    sent = followers(at, place, send_order, own, y, parts)
    arrived = [sent[0]] + [shift(sent[s], "grp", NG, s) for s in range(1, NG)]
    lead = leaders(at, own, y, parts)
    merged = merge(place, partner_slot, after, lead, arrived)
    return (merged, labels)


def solution(mesh):
    grid = Mesh(mesh.devices.reshape(NG, NX, NZ, NC), AXES)
    return jax.shard_map(
        per_device,
        mesh=grid,
        in_specs=(
            P(AXES, None, None),
            P(AXES, None),
            P(AXES, None),
            P(AXES, None),
            P(AXES, None),
            P(AXES, None),
        ),
        out_specs=(P(AXES, None, None), P(AXES, None)),
        check_vma=False,
    )
```

```python
import jax
import jax.numpy as jnp
from jax import lax
from jax.experimental import pallas as pl
from jax.experimental.pallas import tpu as pltpu
from jax.sharding import Mesh, PartitionSpec as P

BLK = 64
K = 11
C = 4
ROWS = 16
HALF = 8
NG, NX, NZ, NC = 4, 4, 8, 2
N_DEV = NX * NZ * NC
LANES = 128
SLOTS = 12
WIDE = SLOTS * BLK
TABLE = N_DEV * C
CHUNKS = 1
CK = 32 // CHUNKS
AXES = ("grp", "x", "z", "core")
ORDER = (1, 2, 4, 5, 6, 3, 7, 0)

VMEM = pl.BlockSpec(memory_space=pltpu.VMEM)
SMEM = pl.BlockSpec(memory_space=pltpu.SMEM)
LIMIT = pltpu.CompilerParams(vmem_limit_bytes=12 * 1024 * 1024)


def low_lanes(shape):
    return lax.broadcasted_iota(jnp.int32, shape, 1) < BLK


def products_kernel(p_ref, a_ref, perm_ref, y_ref):
    def row(i, carry):
        y = lax.dot_general(
            p_ref[i], a_ref[i], (((0,), (0,)), ((), ())), preferred_element_type=jnp.float32
        )
        y = jnp.concatenate([y, jnp.zeros((BLK, BLK), jnp.float32)], axis=1)
        y = jnp.where(i < HALF, y, pltpu.roll(y, BLK, 1)).astype(jnp.bfloat16)
        for t in range(WIDE // LANES):
            span = slice(t * LANES, (t + 1) * LANES)
            y_ref[i, :, span] = jnp.dot(
                y[:, span], perm_ref[...], preferred_element_type=jnp.float32
            ).astype(jnp.bfloat16)
        return carry

    lax.fori_loop(0, ROWS, row, 0, unroll=4)


def products(blocks, stiffness, perm):
    return pl.pallas_call(
        products_kernel,
        out_shape=jax.ShapeDtypeStruct((ROWS, BLK, WIDE), jnp.bfloat16),
        compiler_params=LIMIT,
        cost_estimate=pl.CostEstimate(
            flops=2 * ROWS * BLK * BLK * WIDE * 3, bytes_accessed=3_200_000, transcendentals=0
        ),
        name="products",
    )(blocks, stiffness, perm)


def select_kernel(wanted_ref, place_ref, *refs):
    held, outs = refs[:NZ], refs[NZ:]
    x, z, c = place_ref[1], place_ref[2], place_ref[3]
    for i, b in enumerate(ORDER):
        target = ((x + b // NC) & (NX - 1)) * NC + (c ^ (b % NC))
        for s in range(NZ):
            home = ((z - s) & (NZ - 1)) * C
            for m in range(C):
                outs[i][home + m] = held[s][wanted_ref[target, home + m]]


def select(wanted, place, held):
    shape = jax.ShapeDtypeStruct((NZ * C, CK, LANES), jnp.bfloat16)
    return pl.pallas_call(
        select_kernel,
        out_shape=[shape] * (NX * NC),
        in_specs=[SMEM, SMEM] + [VMEM] * NZ,
        out_specs=[VMEM] * (NX * NC),
        compiler_params=LIMIT,
        name="select",
    )(wanted, place, *held)


def fill(table, own_ref, parts, sems):
    n = NX * NC
    copies = []
    for h in range(CHUNKS):
        for b in range(n):
            spot = table.at[pl.ds(b * NZ * C, NZ * C), pl.ds(h * CK, CK)]
            copies.append(pltpu.make_async_copy(parts[h * n + b], spot, sems.at[h * n + b]))
    for copy in copies:
        copy.start()
    table[TABLE:TABLE + ROWS] = own_ref[...]
    table[TABLE + ROWS] = jnp.zeros((32, LANES), jnp.bfloat16)
    for copy in copies:
        copy.wait()


def row_tiles(i, table, at_ref, y_ref, emit):
    low = low_lanes((32, LANES))
    zero = jnp.zeros((32, LANES), jnp.bfloat16)
    for t in range(SLOTS // 2):
        a = table[at_ref[i, 2 * t]]
        b = table[at_ref[i, 2 * t + 1]]
        rhs = jnp.concatenate([
            jnp.where(low, a, zero),
            jnp.where(low, pltpu.roll(a, BLK, 1), zero),
            jnp.where(low, zero, pltpu.roll(b, BLK, 1)),
            jnp.where(low, zero, b),
        ], axis=0)
        span = slice(t * LANES, (t + 1) * LANES)
        emit(span, jnp.dot(
            y_ref[i, :, span], rhs, preferred_element_type=jnp.float32
        ).astype(jnp.bfloat16))


def follower_kernel(at_ref, place_ref, send_ref, own_ref, y_ref, labels_ref, *refs):
    n = NX * NC * CHUNKS
    parts, outs, table, sems = refs[:n], refs[n:n + NG], refs[n + NG], refs[n + NG + 1]
    fill(table, own_ref, parts, sems)
    for s in range(NG):
        target = (place_ref[0] + s) & (NG - 1)
        for q in range(2):
            spot = target * 2 + q
            row = HALF + send_ref[0, spot]

            def emit(span, value, s=s, q=q):
                outs[s][q, :, span] = value

            row_tiles(row, table, at_ref, y_ref, emit)
            label = labels_ref[pl.ds(spot, 1), :]
            outs[s][q, 0:1, 0:K] = (label >> 4).astype(jnp.float32).astype(jnp.bfloat16)
            outs[s][q, 16:17, 0:K] = (label & 15).astype(jnp.float32).astype(jnp.bfloat16)


def leader_kernel(at_ref, y_ref, table, out):
    def row(i, carry):
        def emit(span, value):
            out[i, :, span] = value

        row_tiles(i, table, at_ref, y_ref, emit)
        return carry

    lax.fori_loop(0, HALF, row, 0)


ROW_COST = pl.CostEstimate(flops=2 * 8 * 6 * BLK * LANES * LANES, bytes_accessed=5_000_000, transcendentals=0)
ANY = pl.BlockSpec(memory_space=pltpu.HBM)


def followers(at, place, send, own, y, labels, parts):
    shape = jax.ShapeDtypeStruct((2, BLK, WIDE), jnp.bfloat16)
    table = jax.ShapeDtypeStruct((TABLE + ROWS + 1, 32, LANES), jnp.bfloat16)
    return pl.pallas_call(
        follower_kernel,
        out_shape=[shape] * NG + [table],
        in_specs=[SMEM] * 3 + [VMEM] * 3 + [ANY] * len(parts),
        out_specs=[VMEM] * (NG + 1),
        scratch_shapes=[pltpu.SemaphoreType.DMA((len(parts),))],
        compiler_params=LIMIT,
        cost_estimate=ROW_COST,
        name="followers",
    )(at, place, send, own, y, labels, *parts)


def leaders(at, y, table):
    return pl.pallas_call(
        leader_kernel,
        out_shape=jax.ShapeDtypeStruct((HALF, BLK, WIDE), jnp.bfloat16),
        in_specs=[SMEM] + [VMEM] * 2,
        out_specs=VMEM,
        compiler_params=LIMIT,
        cost_estimate=ROW_COST,
        name="leaders",
    )(at, y, table)


def label_kernel(place_ref, columns_ref, fetch_ref, codes_ref, mine_ref, send_ref, lead_ref, follow_ref):
    g, x, z, c = (place_ref[i] for i in range(4))
    device = x * (NZ * NC) + z * NC + c

    def slot(i, k):
        column = columns_ref[i, k]
        ghost = jnp.maximum(column - ROWS, 0)
        peer = ghost >> 2
        local = column < ROWS
        row = jnp.where(local, jnp.maximum(column, 0), fetch_ref[peer, ghost & 3])
        late = jnp.maximum(row - HALF, 0)
        group = ((peer >> 4) * NC + (peer & 1)) * HALF
        code = jnp.where(local, mine_ref[late], codes_ref[(peer >> 1) & (NZ - 1), group + late])
        code = jnp.where(row < HALF, g * HALF + row, code)
        label = ((code >> 3) * N_DEV + jnp.where(local, device, peer)) * HALF + (code & 7)
        return jnp.where(column >= 0, label, -1)

    def row(i, carry):
        follower = send_ref[0, i] + HALF
        for k in range(K):
            lead_ref[i, k] = slot(i, k)
            follow_ref[i, k] = slot(follower, k)
        return carry

    lax.fori_loop(0, HALF, row, 0)


def label_rows(place, columns, fetch, codes, mine, send):
    labels = jax.ShapeDtypeStruct((HALF, K), jnp.int32)
    return pl.pallas_call(
        label_kernel,
        out_shape=[labels, labels],
        in_specs=[SMEM] * 6,
        out_specs=[SMEM] * 2,
        name="labels",
    )(place, columns, fetch, codes, mine, send)


def merge_kernel(place_ref, slots_ref, lead_ref, own_labels_ref, *refs):
    parts, out, labels_ref = refs[:NG], refs[NG], refs[NG + 1]
    tiles, stage, sems, digits, work, steps_ref, next_ref, next_sem = refs[NG + 2:]
    per = SLOTS // 2

    lane = lax.broadcasted_iota(jnp.int32, (HALF, LANES), 1)
    for s in range(NG):
        for q in range(2):
            high = parts[s][q, 0:1, 0:LANES].astype(jnp.float32)
            rest = parts[s][q, 16:17, 0:LANES].astype(jnp.float32)
            digits[2 * s + q:2 * s + q + 1, :] = (high * 16.0 + rest).astype(jnp.int32)
    spots = []
    for n in range(HALF):
        spot = slots_ref[0, n]
        spots.append(((place_ref[0] - (spot >> 1)) & (NG - 1)) * 2 + (spot & 1))
        work[n:n + 1, :] = digits[pl.ds(spots[n], 1), :]
    labels = jnp.where(lane < 2 * K, pltpu.roll(work[...], K, 1), -1)
    work[...] = labels
    work[:, 0:K] = own_labels_ref[...]
    labels = work[...]
    labels_ref[...] = work[:, 0:2 * K]
    twice = jnp.where(lane < 2 * K, labels, pltpu.roll(labels, 2 * K, 1))
    steps = jnp.full((HALF, LANES), 2 * K, jnp.int32)
    for d in range(2 * K - 1, 0, -1):
        steps = jnp.where(pltpu.roll(twice, LANES - d, 1) == labels, d, steps)
    steps = jnp.where((lane < 2 * K) & (labels >= 0), steps, 2 * K)
    usual = jnp.where((lane == 0) | (lane == K), K, 2 * K)
    odd = jnp.max(jnp.where(steps != usual, 1, 0), axis=1, keepdims=True)
    steps_ref[...] = jnp.where(lane == 2 * K, odd, steps)
    fetch = pltpu.make_async_copy(steps_ref, next_ref, next_sem)
    fetch.start()

    for t in range(per):
        span = slice(t * LANES, (t + 1) * LANES)
        for n in range(HALF):
            tiles[n * per + t] = lead_ref[n, :, span]
        for s in range(NG):
            for q in range(2):
                tiles[(HALF + 2 * s + q) * per + t] = parts[s][q, :, span]
    low = low_lanes((BLK, LANES))

    for n in range(HALF):
        f, l = (HALF + spots[n]) * per, n * per
        first = tiles[l].astype(jnp.float32)
        second = jnp.where(low, 0.0, tiles[f].astype(jnp.float32))
        tiles[f] = second.astype(jnp.bfloat16)
        stage[n, :, 0:LANES] = (first + pltpu.roll(second, BLK, 1)).astype(jnp.bfloat16)
        middle = tiles[l + per - 1].astype(jnp.float32) + second
        middle = middle + jnp.where(low, 0.0, pltpu.roll(first, BLK, 1))
        stage[n, :, 5 * LANES:6 * LANES] = middle.astype(jnp.bfloat16)
        for t in range(1, per - 1):
            stage[n, :, t * LANES:(t + 1) * LANES] = tiles[l + t]
        for t in range(1, per):
            stage[n, :, (5 + t) * LANES:(6 + t) * LANES] = tiles[f + t]

    def save(n):
        return pltpu.make_async_copy(stage.at[n], out.at[n], sems.at[n])

    fetch.wait()
    for n in range(HALF):
        f, l = (HALF + spots[n]) * per, n * per

        @pl.when(next_ref[n, 2 * K] != 0)
        def _(n=n, f=f, l=l):
            plain = (next_ref[n, 0] == K) & (next_ref[n, K] == K)
            for s in range(2 * K):
                step = next_ref[n, s]
                skip = plain if s in (0, K) else step == 2 * K

                @pl.when(jnp.logical_not(skip))
                def _(s=s, step=step):
                    home = s if s < K else s - K + 1

                    def block(t):
                        spot = jnp.where(t < K, t, t - K + 1)
                        value = tiles[jnp.where(t < K, l, f) + (spot >> 1)].astype(jnp.float32)
                        same = jnp.broadcast_to((spot & 1) == (home & 1), value.shape)
                        return jnp.where(same, value, pltpu.roll(value, BLK, 1))

                    def follow(t, step):
                        after = t + step
                        return jnp.where(after >= 2 * K, after - 2 * K, after)

                    def more(carry):
                        return carry[0] != s

                    def add(carry):
                        t, total = carry
                        return follow(t, next_ref[n, t]), total + block(t)

                    _, total = lax.while_loop(more, add, (follow(s, step), block(jnp.int32(s))))
                    span = slice((s // 2) * LANES, (s // 2 + 1) * LANES)
                    keep = low if s % 2 == 0 else jnp.logical_not(low)
                    stage[n, :, span] = jnp.where(
                        keep, total, stage[n, :, span].astype(jnp.float32)
                    ).astype(jnp.bfloat16)

        save(n).start()
    for n in range(HALF):
        save(n).wait()


def merge(place, slots, lead, own_labels, parts):
    return pl.pallas_call(
        merge_kernel,
        out_shape=[
            jax.ShapeDtypeStruct((HALF, BLK, 2 * K * BLK), jnp.bfloat16),
            jax.ShapeDtypeStruct((HALF, 2 * K), jnp.int32),
        ],
        in_specs=[SMEM] * 2 + [VMEM] * (2 + NG),
        out_specs=[pl.BlockSpec(memory_space=pl.ANY), VMEM],
        scratch_shapes=[
            pltpu.VMEM((2 * HALF * SLOTS // 2, BLK, LANES), jnp.bfloat16),
            pltpu.VMEM((HALF, BLK, 2 * K * BLK), jnp.bfloat16),
            pltpu.SemaphoreType.DMA((HALF,)),
            pltpu.VMEM((HALF, LANES), jnp.int32),
            pltpu.VMEM((HALF, LANES), jnp.int32),
            pltpu.VMEM((HALF, LANES), jnp.int32),
            pltpu.SMEM((HALF, LANES), jnp.int32),
            pltpu.SemaphoreType.DMA,
        ],
        compiler_params=LIMIT,
        name="merge",
    )(place, slots, lead, own_labels, *parts)


def shift(value, axis, size, by):
    if by == 0:
        return value
    return lax.ppermute(value, axis, [(i, (i + by) % size) for i in range(size)])


def cross(value, b):
    if b == 0:
        return value
    by, flip = b // NC, b % NC
    pairs = [
        (x * NC + c, ((x + by) % NX) * NC + (c ^ flip)) for x in range(NX) for c in range(NC)
    ]
    return lax.ppermute(value, ("x", "core"), pairs)


def per_device(stiffness, prolongator, columns, fetch_rows, send_order, partner_slot):
    g, x, z, c = (lax.axis_index(name) for name in AXES)
    device = x * (NZ * NC) + z * NC + c
    place = jnp.stack([g, x, z, c]).astype(jnp.int32)
    own = prolongator.reshape(ROWS, 32, LANES)

    held = []
    for h in range(CHUNKS):
        piece = own[:, h * CK:(h + 1) * CK]
        got = {0: piece}
        for s in (4, 2, 6, 1, 7):
            got[s] = shift(piece, "z", NZ, s)
        got[5] = shift(got[4], "z", NZ, 1)
        got[3] = shift(got[4], "z", NZ, NZ - 1)
        held.append([got[s] for s in range(NZ)])

    sending, slots = send_order[0], partner_slot[0]
    eight = jnp.arange(HALF, dtype=jnp.int32)
    codes = jnp.sum(jnp.where(slots[:, None] == eight[None, :], (g * HALF + eight)[:, None], 0), axis=0)
    returned = lax.all_to_all(codes, "grp", split_axis=0, concat_axis=0, tiled=True)
    mine = jnp.sum(jnp.where(sending[:, None] == eight[None, :], returned[:, None], 0), axis=0)

    lists = fetch_rows.reshape(NX, NZ, NC, C).transpose(0, 2, 1, 3).reshape(NX * NC, NZ * C)
    note = jnp.concatenate([lists, jnp.broadcast_to(mine[None, :], (NX * NC, HALF))], axis=1)
    wanted = lax.all_to_all(note, ("x", "core"), split_axis=0, concat_axis=0, tiled=True)
    plane = wanted[:, NZ * C:].reshape(1, NX * NC * HALF)
    every = lax.all_to_all(
        jnp.broadcast_to(plane, (NZ, NX * NC * HALF)), "z", split_axis=0, concat_axis=0, tiled=True
    )
    lead_labels, follower_labels = label_rows(place, columns, fetch_rows, every, mine, send_order)

    ghost = columns - ROWS
    peer = ghost >> 2
    way = ((x - (peer >> 4)) & (NX - 1)) * NC + (c ^ (peer & 1))
    at = way * (NZ * C) + ((peer >> 1) & (NZ - 1)) * C + (ghost & 3)
    at = jnp.where(columns < ROWS, TABLE + columns, at)
    at = jnp.where(columns >= 0, at, TABLE + ROWS).astype(jnp.int32)
    none = jnp.full((HALF, 1), TABLE + ROWS, jnp.int32)
    at = jnp.concatenate([
        jnp.concatenate([at[:HALF], none], axis=1),
        jnp.concatenate([none, at[HALF:]], axis=1),
    ])

    lane = jnp.arange(LANES, dtype=jnp.int32)
    inner = lane & (BLK - 1)
    source = (lane & BLK) + jnp.where(inner < 32, 2 * inner, 2 * (inner - 32) + 1)
    perm = (lane[:, None] == source[None, :]).astype(jnp.bfloat16)
    y = products(prolongator.reshape(ROWS, BLK, BLK), stiffness, perm)

    parts = []
    for h in range(CHUNKS):
        chosen = select(wanted, place, held[h])
        moved = {b: cross(chosen[i], b) for i, b in enumerate(ORDER)}
        parts += [moved[b] for b in range(NX * NC)]

    *sent, table = followers(at, place, send_order, own, y, follower_labels, parts)
    arrived = [sent[0]] + [shift(sent[s], "grp", NG, s) for s in range(1, NG)]
    lead = leaders(at, y, table)
    return tuple(merge(place, partner_slot, lead, lead_labels, arrived))


def solution(mesh):
    grid = Mesh(mesh.devices.reshape(NG, NX, NZ, NC), AXES)
    return jax.shard_map(
        per_device,
        mesh=grid,
        in_specs=(
            P(AXES, None, None),
            P(AXES, None),
            P(AXES, None),
            P(AXES, None),
            P(AXES, None),
            P(AXES, None),
        ),
        out_specs=(P(AXES, None, None), P(AXES, None)),
        check_vma=False,
    )
```

```python
import jax
import jax.numpy as jnp
from jax import lax
from jax.experimental import pallas as pl
from jax.experimental.pallas import tpu as pltpu
from jax.sharding import Mesh, PartitionSpec as P

BLK = 64
K = 11
C = 4
ROWS = 16
HALF = 8
NG, NX, NZ, NC = 4, 4, 8, 2
N_DEV = NX * NZ * NC
LANES = 128
SLOTS = 12
WIDE = SLOTS * BLK
TABLE = N_DEV * C
CHUNKS = 1
CK = 32 // CHUNKS
AXES = ("grp", "x", "z", "core")
ORDER = (1, 2, 4, 5, 6, 3, 7, 0)

VMEM = pl.BlockSpec(memory_space=pltpu.VMEM)
SMEM = pl.BlockSpec(memory_space=pltpu.SMEM)
HBM = pl.BlockSpec(memory_space=pltpu.HBM)
LIMIT = pltpu.CompilerParams(vmem_limit_bytes=12 * 1024 * 1024)


def low_lanes(shape):
    return lax.broadcasted_iota(jnp.int32, shape, 1) < BLK


def products_kernel(p_ref, a_ref, perm_ref, y_ref):
    def row(i, carry):
        y = lax.dot_general(
            p_ref[i], a_ref[i], (((0,), (0,)), ((), ())), preferred_element_type=jnp.float32
        )
        y = jnp.concatenate([y, jnp.zeros((BLK, BLK), jnp.float32)], axis=1)
        y = jnp.where(i < HALF, y, pltpu.roll(y, BLK, 1)).astype(jnp.bfloat16)
        for t in range(WIDE // LANES):
            span = slice(t * LANES, (t + 1) * LANES)
            y_ref[i, :, span] = jnp.dot(
                y[:, span], perm_ref[...], preferred_element_type=jnp.float32
            ).astype(jnp.bfloat16)
        return carry

    lax.fori_loop(0, ROWS, row, 0, unroll=4)


def products(blocks, stiffness, perm):
    return pl.pallas_call(
        products_kernel,
        out_shape=jax.ShapeDtypeStruct((ROWS, BLK, WIDE), jnp.bfloat16),
        compiler_params=LIMIT,
        cost_estimate=pl.CostEstimate(
            flops=2 * ROWS * BLK * BLK * WIDE * 3, bytes_accessed=3_200_000, transcendentals=0
        ),
        name="products",
    )(blocks, stiffness, perm)


def select_kernel(wanted_ref, *refs):
    n = NX * NC
    held, outs, stage, sems = refs[:NZ], refs[NZ:NZ + n], refs[NZ + n], refs[NZ + n + 1]
    x, z, c = (lax.axis_index(name) for name in AXES[1:])
    copies = []
    for i, b in enumerate(ORDER):
        target = ((x + b // NC) & (NX - 1)) * NC + (c ^ (b % NC))
        for s in range(NZ):
            home = ((z - s) & (NZ - 1)) * C
            for m in range(C):
                stage[i, home + m] = held[s][wanted_ref[target, 0, home + m]]
        copy = pltpu.make_async_copy(stage.at[i], outs[i], sems.at[i])
        copy.start()
        copies.append(copy)
    for copy in copies:
        copy.wait()


def select(wanted, held):
    n = NX * NC
    shape = (NZ * C, CK, LANES)
    return pl.pallas_call(
        select_kernel,
        out_shape=[jax.ShapeDtypeStruct(shape, jnp.bfloat16)] * n,
        in_specs=[SMEM] + [VMEM] * NZ,
        out_specs=[HBM] * n,
        scratch_shapes=[pltpu.VMEM((n,) + shape, jnp.bfloat16), pltpu.SemaphoreType.DMA((n,))],
        compiler_params=LIMIT,
        name="select",
    )(wanted, *held)


def fill(table, own_ref, parts, sems):
    n = NX * NC
    copies = []
    for h in range(CHUNKS):
        for b in range(n):
            spot = table.at[pl.ds(b * NZ * C, NZ * C), pl.ds(h * CK, CK)]
            copies.append(pltpu.make_async_copy(parts[h * n + b], spot, sems.at[h * n + b]))
    for copy in copies:
        copy.start()
    table[TABLE:TABLE + ROWS] = own_ref[...]
    table[TABLE + ROWS] = jnp.zeros((32, LANES), jnp.bfloat16)
    for copy in copies:
        copy.wait()


def row_tiles(i, table, at_ref, y_ref, emit):
    low = low_lanes((32, LANES))
    zero = jnp.zeros((32, LANES), jnp.bfloat16)
    for t in range(SLOTS // 2):
        a = table[at_ref[i, 2 * t]]
        b = table[at_ref[i, 2 * t + 1]]
        rhs = jnp.concatenate([
            jnp.where(low, a, zero),
            jnp.where(low, pltpu.roll(a, BLK, 1), zero),
            jnp.where(low, zero, pltpu.roll(b, BLK, 1)),
            jnp.where(low, zero, b),
        ], axis=0)
        span = slice(t * LANES, (t + 1) * LANES)
        emit(span, jnp.dot(
            y_ref[i, :, span], rhs, preferred_element_type=jnp.float32
        ).astype(jnp.bfloat16))


def follower_kernel(at_ref, send_ref, own_ref, y_ref, labels_ref, *refs):
    n = NX * NC * CHUNKS
    parts, outs, table, sems = refs[:n], refs[n:n + NG], refs[n + NG], refs[n + NG + 1]
    fill(table, own_ref, parts, sems)
    for s in range(NG):
        target = (lax.axis_index(AXES[0]) + s) & (NG - 1)
        for q in range(2):
            spot = target * 2 + q
            row = HALF + send_ref[0, spot]

            def emit(span, value, s=s, q=q):
                outs[s][q, :, span] = value

            row_tiles(row, table, at_ref, y_ref, emit)
            label = labels_ref[pl.ds(spot, 1), :]
            outs[s][q, 0:1, 0:K] = (label >> 4).astype(jnp.float32).astype(jnp.bfloat16)
            outs[s][q, 16:17, 0:K] = (label & 15).astype(jnp.float32).astype(jnp.bfloat16)


def leader_kernel(at_ref, y_ref, table, out):
    def row(i, carry):
        def emit(span, value):
            out[i, :, span] = value

        row_tiles(i, table, at_ref, y_ref, emit)
        return carry

    lax.fori_loop(0, HALF, row, 0)


ROW_COST = pl.CostEstimate(flops=2 * 8 * 6 * BLK * LANES * LANES, bytes_accessed=5_000_000, transcendentals=0)


def followers(at, send, own, y, labels, parts):
    shape = jax.ShapeDtypeStruct((2, BLK, WIDE), jnp.bfloat16)
    table = jax.ShapeDtypeStruct((TABLE + ROWS + 1, 32, LANES), jnp.bfloat16)
    return pl.pallas_call(
        follower_kernel,
        out_shape=[shape] * NG + [table],
        in_specs=[SMEM] * 2 + [VMEM] * 3 + [HBM] * len(parts),
        out_specs=[VMEM] * (NG + 1),
        scratch_shapes=[pltpu.SemaphoreType.DMA((len(parts),))],
        compiler_params=LIMIT,
        cost_estimate=ROW_COST,
        name="followers",
    )(at, send, own, y, labels, *parts)


def leaders(at, y, table):
    return pl.pallas_call(
        leader_kernel,
        out_shape=jax.ShapeDtypeStruct((HALF, BLK, WIDE), jnp.bfloat16),
        in_specs=[SMEM] + [VMEM] * 2,
        out_specs=VMEM,
        compiler_params=LIMIT,
        cost_estimate=ROW_COST,
        name="leaders",
    )(at, y, table)


NOTE = NZ * C + 2 * HALF


def code_kernel(slots_ref, send_ref, codes_ref, order_ref):
    g = lax.axis_index(AXES[0])
    shape = (NG, 1, 2)
    spot = lax.broadcasted_iota(jnp.int32, shape, 0) * 2 + lax.broadcasted_iota(jnp.int32, shape, 2)
    lane = lax.broadcasted_iota(jnp.int32, (1, HALF), 1)
    codes, order = jnp.zeros(shape, jnp.int32), jnp.zeros((1, HALF), jnp.int32)
    for i in range(HALF):
        codes = jnp.where(spot == slots_ref[0, i], g * HALF + i, codes)
        order = jnp.where(lane == send_ref[0, i], i, order)
    codes_ref[...] = codes
    order_ref[...] = order


def code_rows(slots, send):
    return pl.pallas_call(
        code_kernel,
        out_shape=[
            jax.ShapeDtypeStruct((NG, 1, 2), jnp.int32), jax.ShapeDtypeStruct((1, HALF), jnp.int32)
        ],
        in_specs=[SMEM] * 2,
        out_specs=[VMEM] * 2,
        name="codes",
    )(slots, send)


def note_kernel(lists_ref, order_ref, returned_ref, out):
    first = NZ * C
    for d in range(NX * NC):
        out[d, :, 0:first] = lists_ref[d:d + 1, :]
        out[d, :, first:first + HALF] = order_ref[...]
        for t in range(NG):
            out[d, :, first + HALF + 2 * t:first + HALF + 2 * t + 2] = returned_ref[t]


def note_rows(lists, order, returned):
    return pl.pallas_call(
        note_kernel,
        out_shape=jax.ShapeDtypeStruct((NX * NC, 1, NOTE), jnp.int32),
        in_specs=[VMEM] * 3,
        out_specs=VMEM,
        name="note",
    )(lists, order, returned)


def label_kernel(columns_ref, fetch_ref, codes_ref, send_ref, lead_ref, follow_ref):
    g, x, z, c = (lax.axis_index(name) for name in AXES)
    device = x * (NZ * NC) + z * NC + c

    def slot(i, k):
        column = columns_ref[i, k]
        ghost = jnp.maximum(column - ROWS, 0)
        local = column < ROWS
        asked = ghost >> 2
        peer = jnp.where(local, device, asked)
        row = jnp.where(local, jnp.maximum(column, 0), fetch_ref[asked, ghost & 3])
        group = ((peer >> 4) * NC + (peer & 1)) * 2 * HALF
        line = (peer >> 1) & (NZ - 1)
        spot = codes_ref[line, 0, group + jnp.maximum(row - HALF, 0)]
        code = jnp.where(row < HALF, g * HALF + row, codes_ref[line, 0, group + HALF + spot])
        label = ((code >> 3) * N_DEV + peer) * HALF + (code & 7)
        return jnp.where(column >= 0, label, -1)

    def row(i, carry):
        follower = send_ref[0, i] + HALF
        for k in range(K):
            lead_ref[i, k] = slot(i, k)
            follow_ref[i, k] = slot(follower, k)
        return carry

    lax.fori_loop(0, HALF, row, 0)


def label_rows(columns, fetch, codes, send):
    labels = jax.ShapeDtypeStruct((HALF, K), jnp.int32)
    return pl.pallas_call(
        label_kernel,
        out_shape=[labels, labels],
        in_specs=[SMEM] * 4,
        out_specs=[SMEM] * 2,
        name="labels",
    )(columns, fetch, codes, send)


def merge_kernel(slots_ref, lead_ref, own_labels_ref, *refs):
    parts, out, labels_ref = refs[:NG], refs[NG], refs[NG + 1]
    tiles, stage, sems, digits, work, steps_ref, next_ref, next_sem = refs[NG + 2:]
    per = SLOTS // 2

    lane = lax.broadcasted_iota(jnp.int32, (HALF, LANES), 1)
    for s in range(NG):
        for q in range(2):
            high = parts[s][q, 0:1, 0:LANES].astype(jnp.float32)
            rest = parts[s][q, 16:17, 0:LANES].astype(jnp.float32)
            digits[2 * s + q:2 * s + q + 1, :] = (high * 16.0 + rest).astype(jnp.int32)
    spots = []
    for n in range(HALF):
        spot = slots_ref[0, n]
        spots.append(((lax.axis_index(AXES[0]) - (spot >> 1)) & (NG - 1)) * 2 + (spot & 1))
        work[n:n + 1, :] = digits[pl.ds(spots[n], 1), :]
    labels = jnp.where(lane < 2 * K, pltpu.roll(work[...], K, 1), -1)
    work[...] = labels
    work[:, 0:K] = own_labels_ref[...]
    labels = work[...]
    labels_ref[...] = work[:, 0:2 * K]
    twice = jnp.where(lane < 2 * K, labels, pltpu.roll(labels, 2 * K, 1))
    steps = jnp.full((HALF, LANES), 2 * K, jnp.int32)
    for d in range(2 * K - 1, 0, -1):
        steps = jnp.where(pltpu.roll(twice, LANES - d, 1) == labels, d, steps)
    steps = jnp.where((lane < 2 * K) & (labels >= 0), steps, 2 * K)
    usual = jnp.where((lane == 0) | (lane == K), K, 2 * K)
    odd = jnp.max(jnp.where(steps != usual, 1, 0), axis=1, keepdims=True)
    steps_ref[...] = jnp.where(lane == 2 * K, odd, steps)
    fetch = pltpu.make_async_copy(steps_ref, next_ref, next_sem)
    fetch.start()

    for t in range(per):
        span = slice(t * LANES, (t + 1) * LANES)
        for n in range(HALF):
            tiles[n * per + t] = lead_ref[n, :, span]
        for s in range(NG):
            for q in range(2):
                tiles[(HALF + 2 * s + q) * per + t] = parts[s][q, :, span]
    low = low_lanes((BLK, LANES))

    for n in range(HALF):
        f, l = (HALF + spots[n]) * per, n * per
        first = tiles[l].astype(jnp.float32)
        second = jnp.where(low, 0.0, tiles[f].astype(jnp.float32))
        tiles[f] = second.astype(jnp.bfloat16)
        stage[n, :, 0:LANES] = (first + pltpu.roll(second, BLK, 1)).astype(jnp.bfloat16)
        middle = tiles[l + per - 1].astype(jnp.float32) + second
        middle = middle + jnp.where(low, 0.0, pltpu.roll(first, BLK, 1))
        stage[n, :, 5 * LANES:6 * LANES] = middle.astype(jnp.bfloat16)
        for t in range(1, per - 1):
            stage[n, :, t * LANES:(t + 1) * LANES] = tiles[l + t]
        for t in range(1, per):
            stage[n, :, (5 + t) * LANES:(6 + t) * LANES] = tiles[f + t]

    def save(n):
        return pltpu.make_async_copy(stage.at[n], out.at[n], sems.at[n])

    fetch.wait()
    for n in range(HALF):
        f, l = (HALF + spots[n]) * per, n * per

        @pl.when(next_ref[n, 2 * K] != 0)
        def _(n=n, f=f, l=l):
            plain = (next_ref[n, 0] == K) & (next_ref[n, K] == K)
            for s in range(2 * K):
                step = next_ref[n, s]
                skip = plain if s in (0, K) else step == 2 * K

                @pl.when(jnp.logical_not(skip))
                def _(s=s, step=step):
                    home = s if s < K else s - K + 1

                    def block(t):
                        spot = jnp.where(t < K, t, t - K + 1)
                        value = tiles[jnp.where(t < K, l, f) + (spot >> 1)].astype(jnp.float32)
                        same = jnp.broadcast_to((spot & 1) == (home & 1), value.shape)
                        return jnp.where(same, value, pltpu.roll(value, BLK, 1))

                    def follow(t, step):
                        after = t + step
                        return jnp.where(after >= 2 * K, after - 2 * K, after)

                    def more(carry):
                        return carry[0] != s

                    def add(carry):
                        t, total = carry
                        return follow(t, next_ref[n, t]), total + block(t)

                    _, total = lax.while_loop(more, add, (follow(s, step), block(jnp.int32(s))))
                    span = slice((s // 2) * LANES, (s // 2 + 1) * LANES)
                    keep = low if s % 2 == 0 else jnp.logical_not(low)
                    stage[n, :, span] = jnp.where(
                        keep, total, stage[n, :, span].astype(jnp.float32)
                    ).astype(jnp.bfloat16)

        save(n).start()
    for n in range(HALF):
        save(n).wait()


def merge(slots, lead, own_labels, parts):
    return pl.pallas_call(
        merge_kernel,
        out_shape=[
            jax.ShapeDtypeStruct((HALF, BLK, 2 * K * BLK), jnp.bfloat16),
            jax.ShapeDtypeStruct((HALF, 2 * K), jnp.int32),
        ],
        in_specs=[SMEM] + [VMEM] * (2 + NG),
        out_specs=[pl.BlockSpec(memory_space=pl.ANY), VMEM],
        scratch_shapes=[
            pltpu.VMEM((2 * HALF * SLOTS // 2, BLK, LANES), jnp.bfloat16),
            pltpu.VMEM((HALF, BLK, 2 * K * BLK), jnp.bfloat16),
            pltpu.SemaphoreType.DMA((HALF,)),
            pltpu.VMEM((HALF, LANES), jnp.int32),
            pltpu.VMEM((HALF, LANES), jnp.int32),
            pltpu.VMEM((HALF, LANES), jnp.int32),
            pltpu.SMEM((HALF, LANES), jnp.int32),
            pltpu.SemaphoreType.DMA,
        ],
        compiler_params=LIMIT,
        name="merge",
    )(slots, lead, own_labels, *parts)


def shift(value, axis, size, by):
    if by == 0:
        return value
    return lax.ppermute(value, axis, [(i, (i + by) % size) for i in range(size)])


def cross(value, b):
    if b == 0:
        return value
    by, flip = b // NC, b % NC
    pairs = [
        (x * NC + c, ((x + by) % NX) * NC + (c ^ flip)) for x in range(NX) for c in range(NC)
    ]
    return lax.ppermute(value, ("x", "core"), pairs)


def per_device(stiffness, prolongator, columns, fetch_rows, send_order, partner_slot):
    g, x, z, c = (lax.axis_index(name) for name in AXES)
    device = x * (NZ * NC) + z * NC + c
    own = prolongator.reshape(ROWS, 32, LANES)

    held = []
    for h in range(CHUNKS):
        piece = own[:, h * CK:(h + 1) * CK]
        got = {0: piece}
        for s in (4, 2, 6, 1, 7):
            got[s] = shift(piece, "z", NZ, s)
        got[5] = shift(got[4], "z", NZ, 1)
        got[3] = shift(got[4], "z", NZ, NZ - 1)
        held.append([got[s] for s in range(NZ)])

    codes, order = code_rows(partner_slot, send_order)
    returned = lax.all_to_all(codes, "grp", split_axis=0, concat_axis=0, tiled=True)

    lane = jnp.arange(LANES, dtype=jnp.int32)
    inner = lane & (BLK - 1)
    source = (lane & BLK) + jnp.where(inner < 32, 2 * inner, 2 * (inner - 32) + 1)
    perm = (lane[:, None] == source[None, :]).astype(jnp.bfloat16)
    y = products(prolongator.reshape(ROWS, BLK, BLK), stiffness, perm)
    returned, y = lax.optimization_barrier((returned, y))

    lists = fetch_rows.reshape(NX, NZ, NC, C).transpose(0, 2, 1, 3).reshape(NX * NC, NZ * C)
    note = note_rows(lists, order, returned)
    wanted = lax.all_to_all(note, ("x", "core"), split_axis=0, concat_axis=0, tiled=True)
    plane = wanted[:, :, NZ * C:].reshape(1, 1, NX * NC * 2 * HALF)
    every = lax.all_to_all(
        jnp.broadcast_to(plane, (NZ, 1, NX * NC * 2 * HALF)), "z", split_axis=0, concat_axis=0, tiled=True
    )
    lead_labels, follower_labels = label_rows(columns, fetch_rows, every, send_order)

    ghost = columns - ROWS
    peer = ghost >> 2
    way = ((x - (peer >> 4)) & (NX - 1)) * NC + (c ^ (peer & 1))
    at = way * (NZ * C) + ((peer >> 1) & (NZ - 1)) * C + (ghost & 3)
    at = jnp.where(columns < ROWS, TABLE + columns, at)
    at = jnp.where(columns >= 0, at, TABLE + ROWS).astype(jnp.int32)
    none = jnp.full((HALF, 1), TABLE + ROWS, jnp.int32)
    at = jnp.concatenate([
        jnp.concatenate([at[:HALF], none], axis=1),
        jnp.concatenate([none, at[HALF:]], axis=1),
    ])

    parts = []
    for h in range(CHUNKS):
        chosen = select(wanted, held[h])
        moved = {b: cross(chosen[i], b) for i, b in enumerate(ORDER)}
        parts += [pltpu.with_memory_space_constraint(moved[b], pltpu.HBM) for b in range(NX * NC)]

    *sent, table = followers(at, send_order, own, y, follower_labels, parts)
    arrived = [sent[0]] + [shift(sent[s], "grp", NG, s) for s in range(1, NG)]
    lead = leaders(at, y, table)
    return tuple(merge(partner_slot, lead, lead_labels, arrived))


def solution(mesh):
    grid = Mesh(mesh.devices.reshape(NG, NX, NZ, NC), AXES)
    return jax.shard_map(
        per_device,
        mesh=grid,
        in_specs=(
            P(AXES, None, None),
            P(AXES, None),
            P(AXES, None),
            P(AXES, None),
            P(AXES, None),
            P(AXES, None),
        ),
        out_specs=(P(AXES, None, None), P(AXES, None)),
        check_vma=False,
    )
```

```python
import jax
import jax.numpy as jnp
from jax import lax
from jax.experimental import pallas as pl
from jax.experimental.pallas import tpu as pltpu
from jax.sharding import Mesh, PartitionSpec as P

BLK = 64
K = 11
C = 4
ROWS = 16
HALF = 8
NG, NX, NZ, NC = 4, 4, 8, 2
N_DEV = NX * NZ * NC
LANES = 128
SLOTS = 12
WIDE = SLOTS * BLK
TABLE = N_DEV * C
CHUNKS = 1
CK = 32 // CHUNKS
AXES = ("grp", "x", "z", "core")
ORDER = (1, 2, 4, 5, 6, 3, 7, 0)

VMEM = pl.BlockSpec(memory_space=pltpu.VMEM)
SMEM = pl.BlockSpec(memory_space=pltpu.SMEM)
HBM = pl.BlockSpec(memory_space=pltpu.HBM)
LIMIT = pltpu.CompilerParams(vmem_limit_bytes=12 * 1024 * 1024)


def low_lanes(shape):
    return lax.broadcasted_iota(jnp.int32, shape, 1) < BLK


def products_kernel(p_ref, a_ref, perm_ref, y_ref):
    def row(i, carry):
        y = lax.dot_general(
            p_ref[i], a_ref[i], (((0,), (0,)), ((), ())), preferred_element_type=jnp.float32
        )
        y = jnp.concatenate([y, jnp.zeros((BLK, BLK), jnp.float32)], axis=1)
        y = jnp.where(i < HALF, y, pltpu.roll(y, BLK, 1)).astype(jnp.bfloat16)
        for t in range(WIDE // LANES):
            span = slice(t * LANES, (t + 1) * LANES)
            y_ref[i, :, span] = jnp.dot(
                y[:, span], perm_ref[...], preferred_element_type=jnp.float32
            ).astype(jnp.bfloat16)
        return carry

    lax.fori_loop(0, ROWS, row, 0, unroll=4)


def products(blocks, stiffness, perm):
    return pl.pallas_call(
        products_kernel,
        out_shape=jax.ShapeDtypeStruct((ROWS, BLK, WIDE), jnp.bfloat16),
        compiler_params=LIMIT,
        cost_estimate=pl.CostEstimate(
            flops=2 * ROWS * BLK * BLK * WIDE * 3, bytes_accessed=3_200_000, transcendentals=0
        ),
        name="products",
    )(blocks, stiffness, perm)


def select_kernel(wanted_ref, *refs):
    n = NX * NC
    held, outs, stage, sems = refs[:NZ], refs[NZ:NZ + n], refs[NZ + n], refs[NZ + n + 1]
    x, z, c = (lax.axis_index(name) for name in AXES[1:])
    copies = []
    for i, b in enumerate(ORDER):
        target = ((x + b // NC) & (NX - 1)) * NC + (c ^ (b % NC))
        for s in range(NZ):
            home = ((z - s) & (NZ - 1)) * C
            for m in range(C):
                stage[i, home + m] = held[s][wanted_ref[target, 0, home + m]]
        copy = pltpu.make_async_copy(stage.at[i], outs[i], sems.at[i])
        copy.start()
        copies.append(copy)
    for copy in copies:
        copy.wait()


def select(wanted, held):
    n = NX * NC
    shape = (NZ * C, CK, LANES)
    return pl.pallas_call(
        select_kernel,
        out_shape=[jax.ShapeDtypeStruct(shape, jnp.bfloat16)] * n,
        in_specs=[SMEM] + [VMEM] * NZ,
        out_specs=[HBM] * n,
        scratch_shapes=[pltpu.VMEM((n,) + shape, jnp.bfloat16), pltpu.SemaphoreType.DMA((n,))],
        compiler_params=LIMIT,
        name="select",
    )(wanted, *held)


def fill(table, own_ref, parts, sems):
    n = NX * NC
    copies = []
    for h in range(CHUNKS):
        for b in range(n):
            spot = table.at[pl.ds(b * NZ * C, NZ * C), pl.ds(h * CK, CK)]
            copies.append(pltpu.make_async_copy(parts[h * n + b], spot, sems.at[h * n + b]))
    for copy in copies:
        copy.start()
    table[TABLE:TABLE + ROWS] = own_ref[...]
    table[TABLE + ROWS] = jnp.zeros((32, LANES), jnp.bfloat16)
    for copy in copies:
        copy.wait()


def row_tiles(i, table, at_ref, y_ref, emit):
    low = low_lanes((32, LANES))
    zero = jnp.zeros((32, LANES), jnp.bfloat16)
    for t in range(SLOTS // 2):
        a = table[at_ref[i, 2 * t]]
        b = table[at_ref[i, 2 * t + 1]]
        rhs = jnp.concatenate([
            jnp.where(low, a, zero),
            jnp.where(low, pltpu.roll(a, BLK, 1), zero),
            jnp.where(low, zero, pltpu.roll(b, BLK, 1)),
            jnp.where(low, zero, b),
        ], axis=0)
        span = slice(t * LANES, (t + 1) * LANES)
        emit(span, jnp.dot(
            y_ref[i, :, span], rhs, preferred_element_type=jnp.float32
        ).astype(jnp.bfloat16))


def follower_kernel(at_ref, send_ref, own_ref, y_ref, labels_ref, *refs):
    n = NX * NC * CHUNKS
    parts, outs, table, sems = refs[:n], refs[n:n + NG], refs[n + NG], refs[n + NG + 1]
    fill(table, own_ref, parts, sems)
    for s in range(NG):
        target = (lax.axis_index(AXES[0]) + s) & (NG - 1)
        for q in range(2):
            spot = target * 2 + q
            row = HALF + send_ref[0, spot]

            def emit(span, value, s=s, q=q):
                outs[s][q, :, span] = value

            row_tiles(row, table, at_ref, y_ref, emit)
            label = labels_ref[pl.ds(spot, 1), :]
            outs[s][q, 0:1, 0:K] = (label >> 4).astype(jnp.float32).astype(jnp.bfloat16)
            outs[s][q, 16:17, 0:K] = (label & 15).astype(jnp.float32).astype(jnp.bfloat16)


def leader_kernel(at_ref, y_ref, table, out):
    def row(i, carry):
        def emit(span, value):
            out[i, :, span] = value

        row_tiles(i, table, at_ref, y_ref, emit)
        return carry

    lax.fori_loop(0, HALF, row, 0)


ROW_COST = pl.CostEstimate(flops=2 * 8 * 6 * BLK * LANES * LANES, bytes_accessed=5_000_000, transcendentals=0)


def followers(at, send, own, y, labels, parts):
    shape = jax.ShapeDtypeStruct((2, BLK, WIDE), jnp.bfloat16)
    table = jax.ShapeDtypeStruct((TABLE + ROWS + 1, 32, LANES), jnp.bfloat16)
    return pl.pallas_call(
        follower_kernel,
        out_shape=[shape] * NG + [table],
        in_specs=[SMEM] * 2 + [VMEM] * 3 + [HBM] * len(parts),
        out_specs=[VMEM] * (NG + 1),
        scratch_shapes=[pltpu.SemaphoreType.DMA((len(parts),))],
        compiler_params=LIMIT,
        cost_estimate=ROW_COST,
        name="followers",
    )(at, send, own, y, labels, *parts)


def leaders(at, y, table):
    return pl.pallas_call(
        leader_kernel,
        out_shape=jax.ShapeDtypeStruct((HALF, BLK, WIDE), jnp.bfloat16),
        in_specs=[SMEM] + [VMEM] * 2,
        out_specs=VMEM,
        compiler_params=LIMIT,
        cost_estimate=ROW_COST,
        name="leaders",
    )(at, y, table)


NOTE = NZ * C + 2 * HALF


def code_kernel(slots_ref, send_ref, codes_ref, order_ref):
    g = lax.axis_index(AXES[0])
    shape = (NG, 1, 2)
    spot = lax.broadcasted_iota(jnp.int32, shape, 0) * 2 + lax.broadcasted_iota(jnp.int32, shape, 2)
    lane = lax.broadcasted_iota(jnp.int32, (1, HALF), 1)
    codes, order = jnp.zeros(shape, jnp.int32), jnp.zeros((1, HALF), jnp.int32)
    for i in range(HALF):
        codes = jnp.where(spot == slots_ref[0, i], g * HALF + i, codes)
        order = jnp.where(lane == send_ref[0, i], i, order)
    codes_ref[...] = codes
    order_ref[...] = order


def code_rows(slots, send):
    return pl.pallas_call(
        code_kernel,
        out_shape=[
            jax.ShapeDtypeStruct((NG, 1, 2), jnp.int32), jax.ShapeDtypeStruct((1, HALF), jnp.int32)
        ],
        in_specs=[SMEM] * 2,
        out_specs=[VMEM] * 2,
        name="codes",
    )(slots, send)


def note_kernel(lists_ref, order_ref, returned_ref, out):
    first = NZ * C
    for d in range(NX * NC):
        out[d, :, 0:first] = lists_ref[d:d + 1, :]
        out[d, :, first:first + HALF] = order_ref[...]
        for t in range(NG):
            out[d, :, first + HALF + 2 * t:first + HALF + 2 * t + 2] = returned_ref[t]


def note_rows(lists, order, returned):
    return pl.pallas_call(
        note_kernel,
        out_shape=jax.ShapeDtypeStruct((NX * NC, 1, NOTE), jnp.int32),
        in_specs=[VMEM] * 3,
        out_specs=VMEM,
        name="note",
    )(lists, order, returned)


def label_kernel(columns_ref, fetch_ref, codes_ref, send_ref, lead_ref, follow_ref):
    g, x, z, c = (lax.axis_index(name) for name in AXES)
    device = x * (NZ * NC) + z * NC + c

    def slot(i, k):
        column = columns_ref[i, k]
        ghost = jnp.maximum(column - ROWS, 0)
        local = column < ROWS
        asked = ghost >> 2
        peer = jnp.where(local, device, asked)
        row = jnp.where(local, jnp.maximum(column, 0), fetch_ref[asked, ghost & 3])
        group = ((peer >> 4) * NC + (peer & 1)) * 2 * HALF
        line = (peer >> 1) & (NZ - 1)
        spot = codes_ref[line, 0, group + jnp.maximum(row - HALF, 0)]
        code = jnp.where(row < HALF, g * HALF + row, codes_ref[line, 0, group + HALF + spot])
        label = ((code >> 3) * N_DEV + peer) * HALF + (code & 7)
        return jnp.where(column >= 0, label, -1)

    def row(i, carry):
        follower = send_ref[0, i] + HALF
        for k in range(K):
            lead_ref[i, k] = slot(i, k)
            follow_ref[i, k] = slot(follower, k)
        return carry

    lax.fori_loop(0, HALF, row, 0)


def label_rows(columns, fetch, codes, send):
    labels = jax.ShapeDtypeStruct((HALF, K), jnp.int32)
    return pl.pallas_call(
        label_kernel,
        out_shape=[labels, labels],
        in_specs=[SMEM] * 4,
        out_specs=[SMEM] * 2,
        name="labels",
    )(columns, fetch, codes, send)


def merge_kernel(slots_ref, lead_ref, own_labels_ref, *refs):
    parts, out, labels_ref = refs[:NG], refs[NG], refs[NG + 1]
    follow, tiles, stage, sems, digits, work, steps_ref, next_ref, next_sem = refs[NG + 2:]
    per = SLOTS // 2

    lane = lax.broadcasted_iota(jnp.int32, (HALF, LANES), 1)
    for s in range(NG):
        for q in range(2):
            high = parts[s][q, 0:1, 0:LANES].astype(jnp.float32)
            rest = parts[s][q, 16:17, 0:LANES].astype(jnp.float32)
            digits[2 * s + q:2 * s + q + 1, :] = (high * 16.0 + rest).astype(jnp.int32)
    spots = []
    for n in range(HALF):
        spot = slots_ref[0, n]
        spots.append(((lax.axis_index(AXES[0]) - (spot >> 1)) & (NG - 1)) * 2 + (spot & 1))
        work[n:n + 1, :] = digits[pl.ds(spots[n], 1), :]
    labels = jnp.where(lane < 2 * K, pltpu.roll(work[...], K, 1), -1)
    work[...] = labels
    work[:, 0:K] = own_labels_ref[...]
    labels = work[...]
    labels_ref[...] = work[:, 0:2 * K]
    twice = jnp.where(lane < 2 * K, labels, pltpu.roll(labels, 2 * K, 1))
    steps = jnp.full((HALF, LANES), 2 * K, jnp.int32)
    for d in range(2 * K - 1, 0, -1):
        steps = jnp.where(pltpu.roll(twice, LANES - d, 1) == labels, d, steps)
    steps = jnp.where((lane < 2 * K) & (labels >= 0), steps, 2 * K)
    usual = jnp.where((lane == 0) | (lane == K), K, 2 * K)
    odd = jnp.max(jnp.where(steps != usual, 1, 0), axis=1, keepdims=True)
    steps_ref[...] = jnp.where(lane == 2 * K, odd, steps)
    fetch = pltpu.make_async_copy(steps_ref, next_ref, next_sem)
    fetch.start()

    for s in range(NG):
        follow[2 * s:2 * s + 2] = parts[s][...]
    low = low_lanes((BLK, LANES))

    def save(n):
        return pltpu.make_async_copy(stage.at[n], out.at[n], sems.at[n])

    fetch.wait()
    for n in range(HALF):
        f = spots[n]

        def lead(t):
            return lead_ref[n, :, t * LANES:(t + 1) * LANES]

        def part(t):
            return follow[f, :, t * LANES:(t + 1) * LANES]

        first = lead(0).astype(jnp.float32)
        second = jnp.where(low, 0.0, part(0).astype(jnp.float32))
        stage[n, :, 0:LANES] = (first + pltpu.roll(second, BLK, 1)).astype(jnp.bfloat16)
        middle = lead(per - 1).astype(jnp.float32) + second
        middle = middle + jnp.where(low, 0.0, pltpu.roll(first, BLK, 1))
        stage[n, :, 5 * LANES:6 * LANES] = middle.astype(jnp.bfloat16)
        stage[n, :, LANES:5 * LANES] = lead_ref[n, :, LANES:5 * LANES]
        stage[n, :, 6 * LANES:] = follow[f, :, LANES:]

        @pl.when(next_ref[n, 2 * K] != 0)
        def _(n=n, lead=lead, part=part):
            for t in range(per):
                tiles[t] = lead(t).astype(jnp.float32)
                tiles[per + t] = part(t).astype(jnp.float32)
            plain = (next_ref[n, 0] == K) & (next_ref[n, K] == K)
            for s in range(2 * K):
                step = next_ref[n, s]
                skip = plain if s in (0, K) else step == 2 * K

                @pl.when(jnp.logical_not(skip))
                def _(s=s, step=step):
                    home = s if s < K else s + 2

                    def block(t):
                        spot = jnp.where(t < K, t, t + 2)
                        value = tiles[spot >> 1]
                        same = jnp.broadcast_to((spot & 1) == (home & 1), value.shape)
                        return jnp.where(same, value, pltpu.roll(value, BLK, 1))

                    def after(t, step):
                        t = t + step
                        return jnp.where(t >= 2 * K, t - 2 * K, t)

                    def more(carry):
                        return carry[0] != s

                    def add(carry):
                        t, total = carry
                        return after(t, next_ref[n, t]), total + block(t)

                    _, total = lax.while_loop(more, add, (after(s, step), block(jnp.int32(s))))
                    span = slice((s // 2) * LANES, (s // 2 + 1) * LANES)
                    keep = low if s % 2 == 0 else jnp.logical_not(low)
                    stage[n, :, span] = jnp.where(
                        keep, total, stage[n, :, span].astype(jnp.float32)
                    ).astype(jnp.bfloat16)

        save(n).start()
    for n in range(HALF):
        save(n).wait()


def merge(slots, lead, own_labels, parts):
    return pl.pallas_call(
        merge_kernel,
        out_shape=[
            jax.ShapeDtypeStruct((HALF, BLK, 2 * K * BLK), jnp.bfloat16),
            jax.ShapeDtypeStruct((HALF, 2 * K), jnp.int32),
        ],
        in_specs=[SMEM] + [VMEM] * (2 + NG),
        out_specs=[pl.BlockSpec(memory_space=pl.ANY), VMEM],
        scratch_shapes=[
            pltpu.VMEM((2 * NG, BLK, WIDE), jnp.bfloat16),
            pltpu.VMEM((SLOTS, BLK, LANES), jnp.float32),
            pltpu.VMEM((HALF, BLK, 2 * K * BLK), jnp.bfloat16),
            pltpu.SemaphoreType.DMA((HALF,)),
            pltpu.VMEM((HALF, LANES), jnp.int32),
            pltpu.VMEM((HALF, LANES), jnp.int32),
            pltpu.VMEM((HALF, LANES), jnp.int32),
            pltpu.SMEM((HALF, LANES), jnp.int32),
            pltpu.SemaphoreType.DMA,
        ],
        compiler_params=LIMIT,
        name="merge",
    )(slots, lead, own_labels, *parts)


def shift(value, axis, size, by):
    if by == 0:
        return value
    return lax.ppermute(value, axis, [(i, (i + by) % size) for i in range(size)])


def cross(value, b):
    if b == 0:
        return value
    by, flip = b // NC, b % NC
    pairs = [
        (x * NC + c, ((x + by) % NX) * NC + (c ^ flip)) for x in range(NX) for c in range(NC)
    ]
    return lax.ppermute(value, ("x", "core"), pairs)


def per_device(stiffness, prolongator, columns, fetch_rows, send_order, partner_slot):
    g, x, z, c = (lax.axis_index(name) for name in AXES)
    device = x * (NZ * NC) + z * NC + c
    own = prolongator.reshape(ROWS, 32, LANES)

    held = []
    for h in range(CHUNKS):
        piece = own[:, h * CK:(h + 1) * CK]
        got = {0: piece}
        for s in (4, 2, 6, 1, 7):
            got[s] = shift(piece, "z", NZ, s)
        got[5] = shift(got[4], "z", NZ, 1)
        got[3] = shift(got[4], "z", NZ, NZ - 1)
        held.append([got[s] for s in range(NZ)])

    codes, order = code_rows(partner_slot, send_order)
    returned = lax.all_to_all(codes, "grp", split_axis=0, concat_axis=0, tiled=True)

    lane = jnp.arange(LANES, dtype=jnp.int32)
    inner = lane & (BLK - 1)
    source = (lane & BLK) + jnp.where(inner < 32, 2 * inner, 2 * (inner - 32) + 1)
    perm = (lane[:, None] == source[None, :]).astype(jnp.bfloat16)
    y = products(prolongator.reshape(ROWS, BLK, BLK), stiffness, perm)

    lists = fetch_rows.reshape(NX, NZ, NC, C).transpose(0, 2, 1, 3).reshape(NX * NC, NZ * C)
    note = note_rows(lists, order, returned)
    wanted = lax.all_to_all(note, ("x", "core"), split_axis=0, concat_axis=0, tiled=True)
    wanted, y = lax.optimization_barrier((wanted, y))
    plane = wanted[:, :, NZ * C:].reshape(1, 1, NX * NC * 2 * HALF)
    every = lax.all_to_all(
        jnp.broadcast_to(plane, (NZ, 1, NX * NC * 2 * HALF)), "z", split_axis=0, concat_axis=0, tiled=True
    )
    lead_labels, follower_labels = label_rows(columns, fetch_rows, every, send_order)

    ghost = columns - ROWS
    peer = ghost >> 2
    way = ((x - (peer >> 4)) & (NX - 1)) * NC + (c ^ (peer & 1))
    at = way * (NZ * C) + ((peer >> 1) & (NZ - 1)) * C + (ghost & 3)
    at = jnp.where(columns < ROWS, TABLE + columns, at)
    at = jnp.where(columns >= 0, at, TABLE + ROWS).astype(jnp.int32)
    none = jnp.full((HALF, 1), TABLE + ROWS, jnp.int32)
    at = jnp.concatenate([
        jnp.concatenate([at[:HALF], none], axis=1),
        jnp.concatenate([none, at[HALF:]], axis=1),
    ])

    parts = []
    for h in range(CHUNKS):
        chosen = select(wanted, held[h])
        moved = {b: cross(chosen[i], b) for i, b in enumerate(ORDER)}
        parts += [pltpu.with_memory_space_constraint(moved[b], pltpu.HBM) for b in range(NX * NC)]

    *sent, table = followers(at, send_order, own, y, follower_labels, parts)
    arrived = [sent[0]] + [shift(sent[s], "grp", NG, s) for s in range(1, NG)]
    lead = leaders(at, y, table)
    return tuple(merge(partner_slot, lead, lead_labels, arrived))


def solution(mesh):
    grid = Mesh(mesh.devices.reshape(NG, NX, NZ, NC), AXES)
    return jax.shard_map(
        per_device,
        mesh=grid,
        in_specs=(
            P(AXES, None, None),
            P(AXES, None),
            P(AXES, None),
            P(AXES, None),
            P(AXES, None),
            P(AXES, None),
        ),
        out_specs=(P(AXES, None, None), P(AXES, None)),
        check_vma=False,
    )
```

```python
import jax
import jax.numpy as jnp
from jax import lax
from jax.experimental import pallas as pl
from jax.experimental.pallas import tpu as pltpu
from jax.sharding import Mesh, PartitionSpec as P

BLK = 64
K = 11
C = 4
ROWS = 16
HALF = 8
NG, NX, NZ, NC = 4, 4, 8, 2
N_DEV = NX * NZ * NC
LANES = 128
SLOTS = 12
WIDE = SLOTS * BLK
TABLE = N_DEV * C
CHUNKS = 1
CK = 32 // CHUNKS
AXES = ("grp", "x", "z", "core")
ORDER = (1, 2, 4, 5, 6, 3, 7, 0)

VMEM = pl.BlockSpec(memory_space=pltpu.VMEM)
SMEM = pl.BlockSpec(memory_space=pltpu.SMEM)
HBM = pl.BlockSpec(memory_space=pltpu.HBM)
LIMIT = pltpu.CompilerParams(vmem_limit_bytes=12 * 1024 * 1024)


def low_lanes(shape):
    return lax.broadcasted_iota(jnp.int32, shape, 1) < BLK


STEP = 4


def products_kernel(p_ref, perm_ref, a_hbm, y_ref, a_ref, sems):
    def load(h):
        rows = pl.ds(h * STEP, STEP)
        return pltpu.make_async_copy(a_hbm.at[rows], a_ref.at[rows], sems.at[h])

    for h in range(ROWS // STEP):
        load(h).start()
    for h in range(ROWS // STEP):
        load(h).wait()
        for i in range(h * STEP, (h + 1) * STEP):
            y = lax.dot_general(
                p_ref[i], a_ref[i], (((0,), (0,)), ((), ())), preferred_element_type=jnp.float32
            )
            pad = jnp.zeros((BLK, BLK), jnp.float32)
            y = jnp.concatenate([y, pad] if i < HALF else [pad, y], axis=1).astype(jnp.bfloat16)
            for t in range(WIDE // LANES):
                span = slice(t * LANES, (t + 1) * LANES)
                y_ref[i, :, span] = jnp.dot(
                    y[:, span], perm_ref[...], preferred_element_type=jnp.float32
                ).astype(jnp.bfloat16)


def products(blocks, stiffness, perm):
    return pl.pallas_call(
        products_kernel,
        out_shape=jax.ShapeDtypeStruct((ROWS, BLK, WIDE), jnp.bfloat16),
        in_specs=[VMEM, VMEM, HBM],
        out_specs=VMEM,
        scratch_shapes=[
            pltpu.VMEM((ROWS, BLK, K * BLK), jnp.bfloat16),
            pltpu.SemaphoreType.DMA((ROWS // STEP,)),
        ],
        compiler_params=LIMIT,
        cost_estimate=pl.CostEstimate(
            flops=2 * ROWS * BLK * BLK * WIDE * 3, bytes_accessed=3_200_000, transcendentals=0
        ),
        name="products",
    )(blocks, perm, stiffness)


def select_kernel(wanted_ref, *refs):
    n = NX * NC
    held, outs, stage, sems = refs[:NZ], refs[NZ:NZ + n], refs[NZ + n], refs[NZ + n + 1]
    x, z, c = (lax.axis_index(name) for name in AXES[1:])
    copies = []
    for i, b in enumerate(ORDER):
        target = ((x + b // NC) & (NX - 1)) * NC + (c ^ (b % NC))
        for s in range(NZ):
            home = ((z - s) & (NZ - 1)) * C
            for m in range(C):
                stage[i, home + m] = held[s][wanted_ref[target, 0, home + m]]
        copy = pltpu.make_async_copy(stage.at[i], outs[i], sems.at[i])
        copy.start()
        copies.append(copy)
    for copy in copies:
        copy.wait()


def select(wanted, held):
    n = NX * NC
    shape = (NZ * C, CK, LANES)
    return pl.pallas_call(
        select_kernel,
        out_shape=[jax.ShapeDtypeStruct(shape, jnp.bfloat16)] * n,
        in_specs=[SMEM] + [VMEM] * NZ,
        out_specs=[HBM] * n,
        scratch_shapes=[pltpu.VMEM((n,) + shape, jnp.bfloat16), pltpu.SemaphoreType.DMA((n,))],
        compiler_params=LIMIT,
        name="select",
    )(wanted, *held)


def fill(table, own_ref, parts, sems):
    n = NX * NC
    copies = []
    for h in range(CHUNKS):
        for b in range(n):
            spot = table.at[pl.ds(b * NZ * C, NZ * C), pl.ds(h * CK, CK)]
            copies.append(pltpu.make_async_copy(parts[h * n + b], spot, sems.at[h * n + b]))
    for copy in copies:
        copy.start()
    table[TABLE:TABLE + ROWS] = own_ref[...]
    table[TABLE + ROWS] = jnp.zeros((32, LANES), jnp.bfloat16)
    for copy in copies:
        copy.wait()


def row_tiles(i, table, at_ref, y_ref, emit):
    low = low_lanes((32, LANES))
    zero = jnp.zeros((32, LANES), jnp.bfloat16)
    for t in range(SLOTS // 2):
        a = table[at_ref[i, 2 * t]]
        b = table[at_ref[i, 2 * t + 1]]
        rhs = jnp.concatenate([
            jnp.where(low, a, zero),
            jnp.where(low, pltpu.roll(a, BLK, 1), zero),
            jnp.where(low, zero, pltpu.roll(b, BLK, 1)),
            jnp.where(low, zero, b),
        ], axis=0)
        span = slice(t * LANES, (t + 1) * LANES)
        emit(span, jnp.dot(
            y_ref[i, :, span], rhs, preferred_element_type=jnp.float32
        ).astype(jnp.bfloat16))


def label_row(i, address_ref, offset_ref, codes_ref):
    lane = lax.broadcasted_iota(jnp.int32, (1, LANES), 1)
    labels = jnp.full((1, LANES), -1, jnp.int32)
    for k in range(K):
        address = address_ref[i, k]
        spot = jnp.maximum(address, 0)
        code = jnp.where(address < 0, 0, codes_ref[spot >> 6, 0, spot & 63])
        labels = jnp.where(lane == k, offset_ref[i, k] + code, labels)
    return labels


def follower_kernel(at_ref, send_ref, address_ref, offset_ref, codes_ref, own_ref, y_ref, *refs):
    n = NX * NC * CHUNKS
    parts, outs, table, sems = refs[:n], refs[n:n + NG], refs[n + NG], refs[n + NG + 1]
    fill(table, own_ref, parts, sems)
    for s in range(NG):
        target = (lax.axis_index(AXES[0]) + s) & (NG - 1)
        for q in range(2):
            row = HALF + send_ref[0, target * 2 + q]

            def emit(span, value, s=s, q=q):
                outs[s][q, :, span] = value

            row_tiles(row, table, at_ref, y_ref, emit)
            labels = label_row(row, address_ref, offset_ref, codes_ref)[:, 0:BLK]
            outs[s][q, 0:1, 0:BLK] = (labels >> 4).astype(jnp.float32).astype(jnp.bfloat16)
            outs[s][q, 16:17, 0:BLK] = (labels & 15).astype(jnp.float32).astype(jnp.bfloat16)


def leader_kernel(at_ref, address_ref, offset_ref, codes_ref, y_ref, table, out, labels_ref):
    def row(i, carry):
        def emit(span, value):
            out[i, :, span] = value

        row_tiles(i, table, at_ref, y_ref, emit)
        labels_ref[pl.ds(i, 1), :] = label_row(i, address_ref, offset_ref, codes_ref)
        return carry

    lax.fori_loop(0, HALF, row, 0)


ROW_COST = pl.CostEstimate(flops=2 * 8 * 6 * BLK * LANES * LANES, bytes_accessed=5_000_000, transcendentals=0)


def followers(at, send, address, offset, codes, own, y, parts):
    shape = jax.ShapeDtypeStruct((2, BLK, WIDE), jnp.bfloat16)
    table = jax.ShapeDtypeStruct((TABLE + ROWS + 1, 32, LANES), jnp.bfloat16)
    return pl.pallas_call(
        follower_kernel,
        out_shape=[shape] * NG + [table],
        in_specs=[SMEM] * 5 + [VMEM] * 2 + [HBM] * len(parts),
        out_specs=[VMEM] * (NG + 1),
        scratch_shapes=[pltpu.SemaphoreType.DMA((len(parts),))],
        compiler_params=LIMIT,
        cost_estimate=ROW_COST,
        name="followers",
    )(at, send, address, offset, codes, own, y, *parts)


def leaders(at, address, offset, codes, y, table):
    return pl.pallas_call(
        leader_kernel,
        out_shape=[
            jax.ShapeDtypeStruct((HALF, BLK, WIDE), jnp.bfloat16),
            jax.ShapeDtypeStruct((HALF, LANES), jnp.int32),
        ],
        in_specs=[SMEM] * 4 + [VMEM] * 2,
        out_specs=[VMEM] * 2,
        compiler_params=LIMIT,
        cost_estimate=ROW_COST,
        name="leaders",
    )(at, address, offset, codes, y, table)


def code_kernel(slots_ref, codes_ref):
    g = lax.axis_index(AXES[0])
    shape = (NG, 1, 2)
    spot = lax.broadcasted_iota(jnp.int32, shape, 0) * 2 + lax.broadcasted_iota(jnp.int32, shape, 2)
    codes = jnp.zeros(shape, jnp.int32)
    for i in range(HALF):
        codes = jnp.where(spot == slots_ref[0, i], g * (N_DEV * HALF) + i, codes)
    codes_ref[...] = codes


def code_rows(slots):
    return pl.pallas_call(
        code_kernel,
        out_shape=jax.ShapeDtypeStruct((NG, 1, 2), jnp.int32),
        in_specs=[SMEM],
        out_specs=VMEM,
        name="codes",
    )(slots)


def spread_kernel(send_ref, returned_ref, out):
    lane = lax.broadcasted_iota(jnp.int32, (NX * NC, 1, HALF), 2)
    mine = jnp.zeros((NX * NC, 1, HALF), jnp.int32)
    for t in range(NG):
        for q in range(2):
            mine = jnp.where(lane == send_ref[0, 2 * t + q], returned_ref[t, 0, q], mine)
    out[...] = mine


def spread(send, returned):
    return pl.pallas_call(
        spread_kernel,
        out_shape=jax.ShapeDtypeStruct((NX * NC, 1, HALF), jnp.int32),
        in_specs=[SMEM] * 2,
        out_specs=VMEM,
        name="spread",
    )(send, returned)


def plane_kernel(plane_ref, out, row_ref):
    for d in range(NX * NC):
        row_ref[:, d * HALF:(d + 1) * HALF] = plane_ref[d]
    for z in range(NZ):
        out[z] = row_ref[...]


def plane_rows(plane):
    return pl.pallas_call(
        plane_kernel,
        out_shape=jax.ShapeDtypeStruct((NZ, 1, NX * NC * HALF), jnp.int32),
        in_specs=[VMEM],
        out_specs=VMEM,
        scratch_shapes=[pltpu.VMEM((1, NX * NC * HALF), jnp.int32)],
        name="plane",
    )(plane)


def address_kernel(columns_ref, fetch_ref, address_ref, offset_ref):
    g, x, z, c = (lax.axis_index(name) for name in AXES)
    device = x * (NZ * NC) + z * NC + c

    def row(i, carry):
        for k in range(K):
            column = columns_ref[i, k]
            ghost = jnp.maximum(column - ROWS, 0)
            local = column < ROWS
            asked = ghost >> 2
            peer = jnp.where(local, device, asked)
            row = jnp.where(local, jnp.maximum(column, 0), fetch_ref[asked, ghost & 3])
            group = ((peer >> 4) * NC + (peer & 1)) * HALF
            spot = ((peer >> 1) & (NZ - 1)) * (NX * NC * HALF) + group + row - HALF
            late = row >= HALF
            present = column >= 0
            offset = peer * HALF + jnp.where(late, 0, g * (N_DEV * HALF) + row)
            address_ref[i, k] = jnp.where(late & present, spot, -1)
            offset_ref[i, k] = jnp.where(present, offset, -1)
        return carry

    lax.fori_loop(0, ROWS, row, 0)


def addresses(columns, fetch):
    shape = jax.ShapeDtypeStruct((ROWS, K), jnp.int32)
    return pl.pallas_call(
        address_kernel,
        out_shape=[shape, shape],
        in_specs=[SMEM] * 2,
        out_specs=[SMEM] * 2,
        cost_estimate=pl.CostEstimate(flops=1_000_000, bytes_accessed=2_000_000, transcendentals=0),
        name="addresses",
    )(columns, fetch)


def merge_kernel(slots_ref, lead_ref, own_labels_ref, *refs):
    parts, out, labels_ref = refs[:NG], refs[NG], refs[NG + 1]
    follow, tiles, stage, sems, digits, work, steps_ref, next_ref, next_sem = refs[NG + 2:]
    per = SLOTS // 2

    lane = lax.broadcasted_iota(jnp.int32, (HALF, LANES), 1)
    for s in range(NG):
        for q in range(2):
            high = parts[s][q, 0:1, 0:LANES].astype(jnp.float32)
            rest = parts[s][q, 16:17, 0:LANES].astype(jnp.float32)
            digits[2 * s + q:2 * s + q + 1, :] = (high * 16.0 + rest).astype(jnp.int32)
    spots = []
    for n in range(HALF):
        spot = slots_ref[0, n]
        spots.append(((lax.axis_index(AXES[0]) - (spot >> 1)) & (NG - 1)) * 2 + (spot & 1))
        work[n:n + 1, :] = digits[pl.ds(spots[n], 1), :]
    labels = jnp.where(lane < 2 * K, pltpu.roll(work[...], K, 1), -1)
    work[...] = labels
    work[:, 0:K] = own_labels_ref[:, 0:K]
    labels = work[...]
    labels_ref[...] = work[:, 0:2 * K]
    twice = jnp.where(lane < 2 * K, labels, pltpu.roll(labels, 2 * K, 1))
    steps = jnp.full((HALF, LANES), 2 * K, jnp.int32)
    for d in range(2 * K - 1, 0, -1):
        steps = jnp.where(pltpu.roll(twice, LANES - d, 1) == labels, d, steps)
    steps = jnp.where((lane < 2 * K) & (labels >= 0), steps, 2 * K)
    usual = jnp.where((lane == 0) | (lane == K), K, 2 * K)
    odd = jnp.max(jnp.where(steps != usual, 1, 0), axis=1, keepdims=True)
    steps_ref[...] = jnp.where(lane == 2 * K, odd, steps)
    fetch = pltpu.make_async_copy(steps_ref, next_ref, next_sem)
    fetch.start()

    for s in range(NG):
        follow[2 * s:2 * s + 2] = parts[s][...]
    low = low_lanes((BLK, LANES))

    def save(n):
        return pltpu.make_async_copy(stage.at[n], out.at[n], sems.at[n])

    fetch.wait()
    for n in range(HALF):
        f = spots[n]

        def lead(t):
            return lead_ref[n, :, t * LANES:(t + 1) * LANES]

        def part(t):
            return follow[f, :, t * LANES:(t + 1) * LANES]

        first = lead(0).astype(jnp.float32)
        second = jnp.where(low, 0.0, part(0).astype(jnp.float32))
        stage[n, :, 0:LANES] = (first + pltpu.roll(second, BLK, 1)).astype(jnp.bfloat16)
        middle = lead(per - 1).astype(jnp.float32) + second
        middle = middle + jnp.where(low, 0.0, pltpu.roll(first, BLK, 1))
        stage[n, :, 5 * LANES:6 * LANES] = middle.astype(jnp.bfloat16)
        stage[n, :, LANES:5 * LANES] = lead_ref[n, :, LANES:5 * LANES]
        stage[n, :, 6 * LANES:] = follow[f, :, LANES:]

        @pl.when(next_ref[n, 2 * K] != 0)
        def _(n=n, lead=lead, part=part):
            for t in range(per):
                tiles[t] = lead(t).astype(jnp.float32)
                tiles[per + t] = part(t).astype(jnp.float32)
            plain = (next_ref[n, 0] == K) & (next_ref[n, K] == K)
            for s in range(2 * K):
                step = next_ref[n, s]
                skip = plain if s in (0, K) else step == 2 * K

                @pl.when(jnp.logical_not(skip))
                def _(s=s, step=step):
                    home = s if s < K else s + 2

                    def block(t):
                        spot = jnp.where(t < K, t, t + 2)
                        value = tiles[spot >> 1]
                        same = jnp.broadcast_to((spot & 1) == (home & 1), value.shape)
                        return jnp.where(same, value, pltpu.roll(value, BLK, 1))

                    def after(t, step):
                        t = t + step
                        return jnp.where(t >= 2 * K, t - 2 * K, t)

                    def more(carry):
                        return carry[0] != s

                    def add(carry):
                        t, total = carry
                        return after(t, next_ref[n, t]), total + block(t)

                    _, total = lax.while_loop(more, add, (after(s, step), block(jnp.int32(s))))
                    span = slice((s // 2) * LANES, (s // 2 + 1) * LANES)
                    keep = low if s % 2 == 0 else jnp.logical_not(low)
                    stage[n, :, span] = jnp.where(
                        keep, total, stage[n, :, span].astype(jnp.float32)
                    ).astype(jnp.bfloat16)

        save(n).start()
    for n in range(HALF):
        save(n).wait()


def merge(slots, lead, own_labels, parts):
    return pl.pallas_call(
        merge_kernel,
        out_shape=[
            jax.ShapeDtypeStruct((HALF, BLK, 2 * K * BLK), jnp.bfloat16),
            jax.ShapeDtypeStruct((HALF, 2 * K), jnp.int32),
        ],
        in_specs=[SMEM] + [VMEM] * (2 + NG),
        out_specs=[pl.BlockSpec(memory_space=pl.ANY), VMEM],
        scratch_shapes=[
            pltpu.VMEM((2 * NG, BLK, WIDE), jnp.bfloat16),
            pltpu.VMEM((SLOTS, BLK, LANES), jnp.float32),
            pltpu.VMEM((HALF, BLK, 2 * K * BLK), jnp.bfloat16),
            pltpu.SemaphoreType.DMA((HALF,)),
            pltpu.VMEM((HALF, LANES), jnp.int32),
            pltpu.VMEM((HALF, LANES), jnp.int32),
            pltpu.VMEM((HALF, LANES), jnp.int32),
            pltpu.SMEM((HALF, LANES), jnp.int32),
            pltpu.SemaphoreType.DMA,
        ],
        compiler_params=LIMIT,
        name="merge",
    )(slots, lead, own_labels, *parts)


def shift(value, axis, size, by):
    if by == 0:
        return value
    return lax.ppermute(value, axis, [(i, (i + by) % size) for i in range(size)])


def cross(value, b):
    if b == 0:
        return value
    by, flip = b // NC, b % NC
    pairs = [
        (x * NC + c, ((x + by) % NX) * NC + (c ^ flip)) for x in range(NX) for c in range(NC)
    ]
    return lax.ppermute(value, ("x", "core"), pairs)


def per_device(stiffness, prolongator, columns, fetch_rows, send_order, partner_slot):
    g, x, z, c = (lax.axis_index(name) for name in AXES)
    device = x * (NZ * NC) + z * NC + c
    own = prolongator.reshape(ROWS, 32, LANES)

    held = []
    for h in range(CHUNKS):
        piece = own[:, h * CK:(h + 1) * CK]
        got = {0: piece}
        for s in (4, 2, 6, 1, 7):
            got[s] = shift(piece, "z", NZ, s)
        got[5] = shift(got[4], "z", NZ, 1)
        got[3] = shift(got[4], "z", NZ, NZ - 1)
        held.append([got[s] for s in range(NZ)])

    lists = fetch_rows.reshape(NX, NZ, NC, C).transpose(0, 2, 1, 3).reshape(NX * NC, 1, NZ * C)
    wanted = lax.all_to_all(lists, ("x", "core"), split_axis=0, concat_axis=0, tiled=True)

    lane = jnp.arange(LANES, dtype=jnp.int32)
    inner = lane & (BLK - 1)
    source = (lane & BLK) + jnp.where(inner < 32, 2 * inner, 2 * (inner - 32) + 1)
    perm = (lane[:, None] == source[None, :]).astype(jnp.bfloat16)
    y = products(prolongator.reshape(ROWS, BLK, BLK), stiffness, perm)

    returned = lax.all_to_all(code_rows(partner_slot), "grp", split_axis=0, concat_axis=0, tiled=True)
    plane = lax.all_to_all(
        spread(send_order, returned), ("x", "core"), split_axis=0, concat_axis=0, tiled=True
    )
    codes = lax.all_to_all(plane_rows(plane), "z", split_axis=0, concat_axis=0, tiled=True)
    address, offset = addresses(columns, fetch_rows)

    ghost = columns - ROWS
    peer = ghost >> 2
    way = ((x - (peer >> 4)) & (NX - 1)) * NC + (c ^ (peer & 1))
    at = way * (NZ * C) + ((peer >> 1) & (NZ - 1)) * C + (ghost & 3)
    at = jnp.where(columns < ROWS, TABLE + columns, at)
    at = jnp.where(columns >= 0, at, TABLE + ROWS).astype(jnp.int32)
    none = jnp.full((HALF, 1), TABLE + ROWS, jnp.int32)
    at = jnp.concatenate([
        jnp.concatenate([at[:HALF], none], axis=1),
        jnp.concatenate([none, at[HALF:]], axis=1),
    ])

    parts = []
    for h in range(CHUNKS):
        chosen = select(wanted, held[h])
        moved = {b: cross(chosen[i], b) for i, b in enumerate(ORDER)}
        parts += [pltpu.with_memory_space_constraint(moved[b], pltpu.HBM) for b in range(NX * NC)]

    *sent, table = followers(at, send_order, address, offset, codes, own, y, parts)
    arrived = [sent[0]] + [shift(sent[s], "grp", NG, s) for s in range(1, NG)]
    lead, lead_labels = leaders(at, address, offset, codes, y, table)
    return tuple(merge(partner_slot, lead, lead_labels, arrived))


def solution(mesh):
    grid = Mesh(mesh.devices.reshape(NG, NX, NZ, NC), AXES)
    return jax.shard_map(
        per_device,
        mesh=grid,
        in_specs=(
            P(AXES, None, None),
            P(AXES, None),
            P(AXES, None),
            P(AXES, None),
            P(AXES, None),
            P(AXES, None),
        ),
        out_specs=(P(AXES, None, None), P(AXES, None)),
        check_vma=False,
    )
```

```python
import jax
import jax.numpy as jnp
from jax import lax
from jax.experimental import pallas as pl
from jax.experimental.pallas import tpu as pltpu
from jax.sharding import Mesh, PartitionSpec as P

BLK = 64
K = 11
C = 4
ROWS = 16
HALF = 8
NG, NX, NZ, NC = 4, 4, 8, 2
N_DEV = NX * NZ * NC
LANES = 128
SLOTS = 12
WIDE = SLOTS * BLK
TABLE = N_DEV * C
SPOTS, LABELS = 512, 4096
CHUNKS = 1
CK = 32 // CHUNKS
AXES = ("grp", "x", "z", "core")
ORDER = (1, 2, 4, 5, 6, 3, 7, 0)

VMEM = pl.BlockSpec(memory_space=pltpu.VMEM)
SMEM = pl.BlockSpec(memory_space=pltpu.SMEM)
HBM = pl.BlockSpec(memory_space=pltpu.HBM)
LIMIT = pltpu.CompilerParams(vmem_limit_bytes=12 * 1024 * 1024)


def low_lanes(shape):
    return lax.broadcasted_iota(jnp.int32, shape, 1) < BLK


STEP = 4


def products_kernel(p_ref, a_hbm, y_ref, a_ref, work, sems):
    def load(h):
        rows = pl.ds(h * STEP, STEP)
        return pltpu.make_async_copy(a_hbm.at[rows], a_ref.at[rows], sems.at[h])

    for h in range(ROWS // STEP):
        load(h).start()
    row = lax.broadcasted_iota(jnp.int32, (LANES, LANES), 0)
    lane = lax.broadcasted_iota(jnp.int32, (LANES, LANES), 1)
    inner = lane & (BLK - 1)
    source = (lane & BLK) + jnp.where(inner < 32, 2 * inner, 2 * (inner - 32) + 1)
    perm = jnp.where(row == source, 1.0, 0.0).astype(jnp.bfloat16)
    pad = jnp.zeros((BLK, BLK), jnp.float32)
    for h in range(ROWS // STEP):
        load(h).wait()
        for i in range(STEP):
            y = lax.dot_general(
                p_ref[h * STEP + i], a_ref[h * STEP + i], (((0,), (0,)), ((), ())),
                preferred_element_type=jnp.float32,
            )
            y = jnp.concatenate([y, pad] if h * STEP + i < HALF else [pad, y], axis=1)
            work[h, i * BLK:(i + 1) * BLK] = y.astype(jnp.bfloat16)
        for t in range(WIDE // LANES):
            span = slice(t * LANES, (t + 1) * LANES)
            y_ref[h * STEP:(h + 1) * STEP, :, span] = jnp.dot(
                work[h, :, span], perm, preferred_element_type=jnp.float32
            ).astype(jnp.bfloat16).reshape(STEP, BLK, LANES)


def products(blocks, stiffness):
    return pl.pallas_call(
        products_kernel,
        out_shape=jax.ShapeDtypeStruct((ROWS, BLK, WIDE), jnp.bfloat16),
        in_specs=[VMEM, HBM],
        out_specs=VMEM,
        scratch_shapes=[
            pltpu.VMEM((ROWS, BLK, K * BLK), jnp.bfloat16),
            pltpu.VMEM((ROWS // STEP, STEP * BLK, WIDE), jnp.bfloat16),
            pltpu.SemaphoreType.DMA((ROWS // STEP,)),
        ],
        compiler_params=LIMIT,
        cost_estimate=pl.CostEstimate(
            flops=2 * ROWS * BLK * BLK * WIDE * 3, bytes_accessed=3_200_000, transcendentals=0
        ),
        name="products",
    )(blocks, stiffness)


def select_kernel(wanted_ref, *refs):
    n = NX * NC
    held, outs, stage, sems = refs[:NZ], refs[NZ:NZ + n], refs[NZ + n], refs[NZ + n + 1]
    x, z, c = (lax.axis_index(name) for name in AXES[1:])
    copies = []
    for i, b in enumerate(ORDER):
        target = ((x + b // NC) & (NX - 1)) * NC + (c ^ (b % NC))
        for s in range(NZ):
            home = ((z - s) & (NZ - 1)) * C
            for m in range(C):
                stage[i, home + m] = held[s][wanted_ref[target, 0, home + m]]
        copy = pltpu.make_async_copy(stage.at[i], outs[i], sems.at[i])
        copy.start()
        copies.append(copy)
    for copy in copies:
        copy.wait()


def select(wanted, held):
    n = NX * NC
    shape = (NZ * C, CK, LANES)
    return pl.pallas_call(
        select_kernel,
        out_shape=[jax.ShapeDtypeStruct(shape, jnp.bfloat16)] * n,
        in_specs=[SMEM] + [VMEM] * NZ,
        out_specs=[HBM] * n,
        scratch_shapes=[pltpu.VMEM((n,) + shape, jnp.bfloat16), pltpu.SemaphoreType.DMA((n,))],
        compiler_params=LIMIT,
        name="select",
    )(wanted, *held)


def fill(table, own_ref, parts, sems):
    n = NX * NC
    copies = []
    for h in range(CHUNKS):
        for b in range(n):
            spot = table.at[pl.ds(b * NZ * C, NZ * C), pl.ds(h * CK, CK)]
            copies.append(pltpu.make_async_copy(parts[h * n + b], spot, sems.at[h * n + b]))
    for copy in copies:
        copy.start()
    table[TABLE:TABLE + ROWS] = own_ref[...]
    table[TABLE + ROWS] = jnp.zeros((32, LANES), jnp.bfloat16)
    for copy in copies:
        copy.wait()


def row_tiles(i, late, table, slot_ref, y_ref, emit):
    low = low_lanes((32, LANES))
    zero = jnp.zeros((32, LANES), jnp.bfloat16)
    for t in range(SLOTS // 2):
        a, b = (
            table[slot_ref[i, k] & (SPOTS - 1) if 0 <= k < K else TABLE + ROWS]
            for k in (2 * t - late, 2 * t + 1 - late)
        )
        rhs = jnp.concatenate([
            jnp.where(low, a, zero),
            jnp.where(low, pltpu.roll(a, BLK, 1), zero),
            jnp.where(low, zero, pltpu.roll(b, BLK, 1)),
            jnp.where(low, zero, b),
        ], axis=0)
        span = slice(t * LANES, (t + 1) * LANES)
        emit(span, jnp.dot(
            y_ref[i, :, span], rhs, preferred_element_type=jnp.float32
        ).astype(jnp.bfloat16))


def label_row(i, slot_ref, codes_ref):
    lane = lax.broadcasted_iota(jnp.int32, (1, LANES), 1)
    labels = jnp.full((1, LANES), -1, jnp.int32)
    for k in range(K):
        word = slot_ref[i, k]
        address = (word >> 21) - 1
        spot = jnp.maximum(address, 0)
        code = jnp.where(address < 0, 0, codes_ref[spot >> 6, 0, spot & 63])
        offset = ((word >> 9) & (LABELS - 1)) - 1
        labels = jnp.where(lane == k, offset + code, labels)
    return labels


def follower_kernel(slot_ref, send_ref, codes_ref, own_ref, y_ref, *refs):
    n = NX * NC * CHUNKS
    parts, outs, table, sems = refs[:n], refs[n:n + NG], refs[n + NG], refs[n + NG + 1]
    fill(table, own_ref, parts, sems)
    for s in range(NG):
        target = (lax.axis_index(AXES[0]) + s) & (NG - 1)
        for q in range(2):
            row = HALF + send_ref[0, target * 2 + q]

            def emit(span, value, s=s, q=q):
                outs[s][q, :, span] = value

            row_tiles(row, 1, table, slot_ref, y_ref, emit)
            labels = label_row(row, slot_ref, codes_ref)[:, 0:BLK]
            outs[s][q, 0:1, 0:BLK] = (labels >> 4).astype(jnp.float32).astype(jnp.bfloat16)
            outs[s][q, 16:17, 0:BLK] = (labels & 15).astype(jnp.float32).astype(jnp.bfloat16)


def leader_kernel(slot_ref, codes_ref, y_ref, table, out, labels_ref):
    def row(i, carry):
        def emit(span, value):
            out[i, :, span] = value

        row_tiles(i, 0, table, slot_ref, y_ref, emit)
        labels_ref[pl.ds(i, 1), :] = label_row(i, slot_ref, codes_ref)
        return carry

    lax.fori_loop(0, HALF, row, 0)


ROW_COST = pl.CostEstimate(flops=2 * 8 * 6 * BLK * LANES * LANES, bytes_accessed=5_000_000, transcendentals=0)


def followers(slots, send, codes, own, y, parts):
    shape = jax.ShapeDtypeStruct((2, BLK, WIDE), jnp.bfloat16)
    table = jax.ShapeDtypeStruct((TABLE + ROWS + 1, 32, LANES), jnp.bfloat16)
    return pl.pallas_call(
        follower_kernel,
        out_shape=[shape] * NG + [table],
        in_specs=[SMEM] * 3 + [VMEM] * 2 + [HBM] * len(parts),
        out_specs=[VMEM] * (NG + 1),
        scratch_shapes=[pltpu.SemaphoreType.DMA((len(parts),))],
        compiler_params=LIMIT,
        cost_estimate=ROW_COST,
        name="followers",
    )(slots, send, codes, own, y, *parts)


def leaders(slots, codes, y, table):
    return pl.pallas_call(
        leader_kernel,
        out_shape=[
            jax.ShapeDtypeStruct((HALF, BLK, WIDE), jnp.bfloat16),
            jax.ShapeDtypeStruct((HALF, LANES), jnp.int32),
        ],
        in_specs=[SMEM] * 2 + [VMEM] * 2,
        out_specs=[VMEM] * 2,
        compiler_params=LIMIT,
        cost_estimate=ROW_COST,
        name="leaders",
    )(slots, codes, y, table)


def code_kernel(slots_ref, codes_ref):
    g = lax.axis_index(AXES[0])
    shape = (NG, 1, 2)
    spot = lax.broadcasted_iota(jnp.int32, shape, 0) * 2 + lax.broadcasted_iota(jnp.int32, shape, 2)
    codes = jnp.zeros(shape, jnp.int32)
    for i in range(HALF):
        codes = jnp.where(spot == slots_ref[0, i], g * (N_DEV * HALF) + i, codes)
    codes_ref[...] = codes


def code_rows(slots):
    return pl.pallas_call(
        code_kernel,
        out_shape=jax.ShapeDtypeStruct((NG, 1, 2), jnp.int32),
        in_specs=[SMEM],
        out_specs=VMEM,
        name="codes",
    )(slots)


NOTE = NZ * C + HALF


def note_kernel(send_ref, lists_ref, returned_ref, out):
    lane = lax.broadcasted_iota(jnp.int32, (NX * NC, 1, HALF), 2)
    mine = jnp.zeros((NX * NC, 1, HALF), jnp.int32)
    for t in range(NG):
        for q in range(2):
            mine = jnp.where(lane == send_ref[0, 2 * t + q], returned_ref[t:t + 1, :, q:q + 1], mine)
    out[:, :, 0:NZ * C] = lists_ref[...]
    out[:, :, NZ * C:] = mine


def note_rows(send, lists, returned):
    return pl.pallas_call(
        note_kernel,
        out_shape=jax.ShapeDtypeStruct((NX * NC, 1, NOTE), jnp.int32),
        in_specs=[SMEM, VMEM, VMEM],
        out_specs=VMEM,
        name="note",
    )(send, lists, returned)


def plane_kernel(note_ref, out, row_ref):
    for d in range(NX * NC):
        row_ref[:, d * HALF:(d + 1) * HALF] = note_ref[d][:, NZ * C:]
    for z in range(NZ):
        out[z] = row_ref[...]


def plane_rows(note):
    return pl.pallas_call(
        plane_kernel,
        out_shape=jax.ShapeDtypeStruct((NZ, 1, NX * NC * HALF), jnp.int32),
        in_specs=[VMEM],
        out_specs=VMEM,
        scratch_shapes=[pltpu.VMEM((1, NX * NC * HALF), jnp.int32)],
        name="plane",
    )(note)


def slot_kernel(columns_ref, fetch_ref, slot_ref):
    g, x, z, c = (lax.axis_index(name) for name in AXES)
    device = x * (NZ * NC) + z * NC + c

    def row(i, carry):
        for k in range(K):
            column = columns_ref[i, k]
            ghost = jnp.maximum(column - ROWS, 0)
            local = column < ROWS
            asked = ghost >> 2
            peer = jnp.where(local, device, asked)
            row = jnp.where(local, jnp.maximum(column, 0), fetch_ref[asked, ghost & 3])
            px, pz, pc = peer >> 4, (peer >> 1) & (NZ - 1), peer & 1
            way = ((x - px) & (NX - 1)) * NC + (c ^ pc)
            at = jnp.where(local, TABLE + row, way * (NZ * C) + pz * C + (ghost & 3))
            late = row >= HALF
            spot = jnp.where(late, pz * (NX * NC * HALF) + (px * NC + pc) * HALF + row - HALF + 1, 0)
            offset = peer * HALF + 1 + jnp.where(late, 0, g * (N_DEV * HALF) + row)
            word = spot * (LABELS * SPOTS) + offset * SPOTS + at
            slot_ref[i, k] = jnp.where(column >= 0, word, TABLE + ROWS)
        return carry

    lax.fori_loop(0, ROWS, row, 0)


def slot_words(columns, fetch):
    return pl.pallas_call(
        slot_kernel,
        out_shape=jax.ShapeDtypeStruct((ROWS, K), jnp.int32),
        in_specs=[SMEM] * 2,
        out_specs=SMEM,
        cost_estimate=pl.CostEstimate(flops=1_000_000, bytes_accessed=2_000_000, transcendentals=0),
        name="slots",
    )(columns, fetch)


def merge_kernel(slots_ref, lead_ref, own_labels_ref, *refs):
    parts, out, labels_ref = refs[:NG], refs[NG], refs[NG + 1]
    follow, tiles, stage, sems, digits, work, steps_ref, next_ref, next_sem = refs[NG + 2:]
    per = SLOTS // 2

    lane = lax.broadcasted_iota(jnp.int32, (HALF, LANES), 1)
    for s in range(NG):
        for q in range(2):
            high = parts[s][q, 0:1, 0:LANES].astype(jnp.float32)
            rest = parts[s][q, 16:17, 0:LANES].astype(jnp.float32)
            digits[2 * s + q:2 * s + q + 1, :] = (high * 16.0 + rest).astype(jnp.int32)
    spots = []
    for n in range(HALF):
        spot = slots_ref[0, n]
        spots.append(((lax.axis_index(AXES[0]) - (spot >> 1)) & (NG - 1)) * 2 + (spot & 1))
        work[n:n + 1, :] = digits[pl.ds(spots[n], 1), :]
    labels = jnp.where(lane < 2 * K, pltpu.roll(work[...], K, 1), -1)
    work[...] = labels
    work[:, 0:K] = own_labels_ref[:, 0:K]
    labels = work[...]
    labels_ref[...] = work[:, 0:2 * K]
    twice = jnp.where(lane < 2 * K, labels, pltpu.roll(labels, 2 * K, 1))
    steps = jnp.full((HALF, LANES), 2 * K, jnp.int32)
    for d in range(2 * K - 1, 0, -1):
        steps = jnp.where(pltpu.roll(twice, LANES - d, 1) == labels, d, steps)
    steps = jnp.where((lane < 2 * K) & (labels >= 0), steps, 2 * K)
    usual = jnp.where((lane == 0) | (lane == K), K, 2 * K)
    odd = jnp.max(jnp.where(steps != usual, 1, 0), axis=1, keepdims=True)
    steps_ref[...] = jnp.where(lane == 2 * K, odd, steps)
    fetch = pltpu.make_async_copy(steps_ref, next_ref, next_sem)
    fetch.start()

    for s in range(NG):
        follow[2 * s:2 * s + 2] = parts[s][...]
    low = low_lanes((BLK, LANES))

    def save(n):
        return pltpu.make_async_copy(stage.at[n], out.at[n], sems.at[n])

    fetch.wait()
    for n in range(HALF):
        f = spots[n]

        def lead(t):
            return lead_ref[n, :, t * LANES:(t + 1) * LANES]

        def part(t):
            return follow[f, :, t * LANES:(t + 1) * LANES]

        first = lead(0).astype(jnp.float32)
        second = jnp.where(low, 0.0, part(0).astype(jnp.float32))
        stage[n, :, 0:LANES] = (first + pltpu.roll(second, BLK, 1)).astype(jnp.bfloat16)
        middle = lead(per - 1).astype(jnp.float32) + second
        middle = middle + jnp.where(low, 0.0, pltpu.roll(first, BLK, 1))
        stage[n, :, 5 * LANES:6 * LANES] = middle.astype(jnp.bfloat16)
        stage[n, :, LANES:5 * LANES] = lead_ref[n, :, LANES:5 * LANES]
        stage[n, :, 6 * LANES:] = follow[f, :, LANES:]

        @pl.when(next_ref[n, 2 * K] != 0)
        def _(n=n, lead=lead, part=part):
            for t in range(per):
                tiles[t] = lead(t).astype(jnp.float32)
                tiles[per + t] = part(t).astype(jnp.float32)
            plain = (next_ref[n, 0] == K) & (next_ref[n, K] == K)
            for s in range(2 * K):
                step = next_ref[n, s]
                skip = plain if s in (0, K) else step == 2 * K

                @pl.when(jnp.logical_not(skip))
                def _(s=s, step=step):
                    home = s if s < K else s + 2

                    def block(t):
                        spot = jnp.where(t < K, t, t + 2)
                        value = tiles[spot >> 1]
                        same = jnp.broadcast_to((spot & 1) == (home & 1), value.shape)
                        return jnp.where(same, value, pltpu.roll(value, BLK, 1))

                    def after(t, step):
                        t = t + step
                        return jnp.where(t >= 2 * K, t - 2 * K, t)

                    def more(carry):
                        return carry[0] != s

                    def add(carry):
                        t, total = carry
                        return after(t, next_ref[n, t]), total + block(t)

                    _, total = lax.while_loop(more, add, (after(s, step), block(jnp.int32(s))))
                    span = slice((s // 2) * LANES, (s // 2 + 1) * LANES)
                    keep = low if s % 2 == 0 else jnp.logical_not(low)
                    stage[n, :, span] = jnp.where(
                        keep, total, stage[n, :, span].astype(jnp.float32)
                    ).astype(jnp.bfloat16)

        save(n).start()
    for n in range(HALF):
        save(n).wait()


def merge(slots, lead, own_labels, parts):
    return pl.pallas_call(
        merge_kernel,
        out_shape=[
            jax.ShapeDtypeStruct((HALF, BLK, 2 * K * BLK), jnp.bfloat16),
            jax.ShapeDtypeStruct((HALF, 2 * K), jnp.int32),
        ],
        in_specs=[SMEM] + [VMEM] * (2 + NG),
        out_specs=[pl.BlockSpec(memory_space=pl.ANY), VMEM],
        scratch_shapes=[
            pltpu.VMEM((2 * NG, BLK, WIDE), jnp.bfloat16),
            pltpu.VMEM((SLOTS, BLK, LANES), jnp.float32),
            pltpu.VMEM((HALF, BLK, 2 * K * BLK), jnp.bfloat16),
            pltpu.SemaphoreType.DMA((HALF,)),
            pltpu.VMEM((HALF, LANES), jnp.int32),
            pltpu.VMEM((HALF, LANES), jnp.int32),
            pltpu.VMEM((HALF, LANES), jnp.int32),
            pltpu.SMEM((HALF, LANES), jnp.int32),
            pltpu.SemaphoreType.DMA,
        ],
        compiler_params=LIMIT,
        name="merge",
    )(slots, lead, own_labels, *parts)


def shift(value, axis, size, by):
    if by == 0:
        return value
    return lax.ppermute(value, axis, [(i, (i + by) % size) for i in range(size)])


def cross(value, b):
    if b == 0:
        return value
    by, flip = b // NC, b % NC
    pairs = [
        (x * NC + c, ((x + by) % NX) * NC + (c ^ flip)) for x in range(NX) for c in range(NC)
    ]
    return lax.ppermute(value, ("x", "core"), pairs)


def per_device(stiffness, prolongator, columns, fetch_rows, send_order, partner_slot):
    g, x, z, c = (lax.axis_index(name) for name in AXES)
    device = x * (NZ * NC) + z * NC + c
    own = prolongator.reshape(ROWS, 32, LANES)

    held = []
    for h in range(CHUNKS):
        piece = own[:, h * CK:(h + 1) * CK]
        got = {0: piece}
        for s in (4, 2, 6, 1, 7):
            got[s] = shift(piece, "z", NZ, s)
        got[5] = shift(got[4], "z", NZ, 1)
        got[3] = shift(got[4], "z", NZ, NZ - 1)
        held.append([got[s] for s in range(NZ)])

    returned = lax.all_to_all(code_rows(partner_slot), "grp", split_axis=0, concat_axis=0, tiled=True)
    lists = fetch_rows.reshape(NX, NZ, NC, C).transpose(0, 2, 1, 3).reshape(NX * NC, 1, NZ * C)
    note = note_rows(send_order, lists, returned)
    wanted = lax.all_to_all(note, ("x", "core"), split_axis=0, concat_axis=0, tiled=True)
    wanted, words = lax.optimization_barrier((wanted, slot_words(columns, fetch_rows)))
    codes = lax.all_to_all(plane_rows(wanted), "z", split_axis=0, concat_axis=0, tiled=True)
    y = products(prolongator.reshape(ROWS, BLK, BLK), stiffness)

    parts = []
    for h in range(CHUNKS):
        chosen = select(wanted, held[h])
        moved = {b: cross(chosen[i], b) for i, b in enumerate(ORDER)}
        parts += [pltpu.with_memory_space_constraint(moved[b], pltpu.HBM) for b in range(NX * NC)]

    *sent, table = followers(words, send_order, codes, own, y, parts)
    arrived = [sent[0]] + [shift(sent[s], "grp", NG, s) for s in range(1, NG)]
    lead, lead_labels = leaders(words, codes, y, table)
    return tuple(merge(partner_slot, lead, lead_labels, arrived))


def solution(mesh):
    grid = Mesh(mesh.devices.reshape(NG, NX, NZ, NC), AXES)
    return jax.shard_map(
        per_device,
        mesh=grid,
        in_specs=(
            P(AXES, None, None),
            P(AXES, None),
            P(AXES, None),
            P(AXES, None),
            P(AXES, None),
            P(AXES, None),
        ),
        out_specs=(P(AXES, None, None), P(AXES, None)),
        check_vma=False,
    )
```

```python
import jax
import jax.numpy as jnp
from jax import lax
from jax.experimental import pallas as pl
from jax.experimental.pallas import tpu as pltpu
from jax.sharding import Mesh, PartitionSpec as P

BLK = 64
K = 11
C = 4
ROWS = 16
HALF = 8
NG, NX, NZ, NC = 4, 4, 8, 2
N_DEV = NX * NZ * NC
LANES = 128
SLOTS = 12
WIDE = SLOTS * BLK
TABLE = N_DEV * C
SPOTS, LABELS = 512, 4096
CHUNKS = 1
CK = 32 // CHUNKS
AXES = ("grp", "x", "z", "core")
ORDER = (1, 2, 6, 4, 5, 3, 7, 0)

VMEM = pl.BlockSpec(memory_space=pltpu.VMEM)
SMEM = pl.BlockSpec(memory_space=pltpu.SMEM)
HBM = pl.BlockSpec(memory_space=pltpu.HBM)
LIMIT = pltpu.CompilerParams(vmem_limit_bytes=12 * 1024 * 1024)


def low_lanes(shape):
    return lax.broadcasted_iota(jnp.int32, shape, 1) < BLK


STEP = 4


def products_kernel(p_ref, perm_ref, a_hbm, y_ref, a_ref, work, sems):
    def load(h):
        rows = pl.ds(h * STEP, STEP)
        return pltpu.make_async_copy(a_hbm.at[rows], a_ref.at[rows], sems.at[h])

    for h in range(ROWS // STEP):
        load(h).start()
    perm = perm_ref[...]
    pad = jnp.zeros((BLK, BLK), jnp.float32)
    for h in range(ROWS // STEP):
        load(h).wait()
        for i in range(STEP):
            y = lax.dot_general(
                p_ref[h * STEP + i], a_ref[h * STEP + i], (((0,), (0,)), ((), ())),
                preferred_element_type=jnp.float32,
            )
            y = jnp.concatenate([y, pad] if h * STEP + i < HALF else [pad, y], axis=1)
            work[h, i * BLK:(i + 1) * BLK] = y.astype(jnp.bfloat16)
        for t in range(WIDE // LANES):
            span = slice(t * LANES, (t + 1) * LANES)
            y_ref[h * STEP:(h + 1) * STEP, :, span] = jnp.dot(
                work[h, :, span], perm, preferred_element_type=jnp.float32
            ).astype(jnp.bfloat16).reshape(STEP, BLK, LANES)


def products(blocks, perm, stiffness):
    return pl.pallas_call(
        products_kernel,
        out_shape=jax.ShapeDtypeStruct((ROWS, BLK, WIDE), jnp.bfloat16),
        in_specs=[VMEM, VMEM, HBM],
        out_specs=VMEM,
        scratch_shapes=[
            pltpu.VMEM((ROWS, BLK, K * BLK), jnp.bfloat16),
            pltpu.VMEM((ROWS // STEP, STEP * BLK, WIDE), jnp.bfloat16),
            pltpu.SemaphoreType.DMA((ROWS // STEP,)),
        ],
        compiler_params=LIMIT,
        cost_estimate=pl.CostEstimate(
            flops=2 * ROWS * BLK * BLK * WIDE * 3, bytes_accessed=3_200_000, transcendentals=0
        ),
        name="products",
    )(blocks, perm, stiffness)


def select_kernel(wanted_ref, *refs):
    n = NX * NC
    held, outs, stage, sems = refs[:NZ], refs[NZ:NZ + n], refs[NZ + n], refs[NZ + n + 1]
    x, z, c = (lax.axis_index(name) for name in AXES[1:])
    copies = []
    for i, b in enumerate(ORDER):
        target = ((x + b // NC) & (NX - 1)) * NC + (c ^ (b % NC))
        for s in range(NZ):
            home = ((z - s) & (NZ - 1)) * C
            for m in range(C):
                stage[i, home + m] = held[s][wanted_ref[target, 0, home + m]]
        copy = pltpu.make_async_copy(stage.at[i], outs[i], sems.at[i])
        copy.start()
        copies.append(copy)
    for copy in copies:
        copy.wait()


def select(wanted, held):
    n = NX * NC
    shape = (NZ * C, CK, LANES)
    return pl.pallas_call(
        select_kernel,
        out_shape=[jax.ShapeDtypeStruct(shape, jnp.bfloat16)] * n,
        in_specs=[SMEM] + [VMEM] * NZ,
        out_specs=[HBM] * n,
        scratch_shapes=[pltpu.VMEM((n,) + shape, jnp.bfloat16), pltpu.SemaphoreType.DMA((n,))],
        compiler_params=LIMIT,
        name="select",
    )(wanted, *held)


def fill(table, own_ref, parts, sems):
    n = NX * NC
    copies = []
    for h in range(CHUNKS):
        for b in range(n):
            spot = table.at[pl.ds(b * NZ * C, NZ * C), pl.ds(h * CK, CK)]
            copies.append(pltpu.make_async_copy(parts[h * n + b], spot, sems.at[h * n + b]))
    for copy in copies:
        copy.start()
    table[TABLE:TABLE + ROWS] = own_ref[...]
    table[TABLE + ROWS] = jnp.zeros((32, LANES), jnp.bfloat16)
    for copy in copies:
        copy.wait()


def row_tiles(i, late, table, slot_ref, y_ref, emit):
    low = low_lanes((32, LANES))
    zero = jnp.zeros((32, LANES), jnp.bfloat16)
    for t in range(SLOTS // 2):
        a, b = (
            table[slot_ref[i, k] & (SPOTS - 1) if 0 <= k < K else TABLE + ROWS]
            for k in (2 * t - late, 2 * t + 1 - late)
        )
        rhs = jnp.concatenate([
            jnp.where(low, a, zero),
            jnp.where(low, pltpu.roll(a, BLK, 1), zero),
            jnp.where(low, zero, pltpu.roll(b, BLK, 1)),
            jnp.where(low, zero, b),
        ], axis=0)
        span = slice(t * LANES, (t + 1) * LANES)
        emit(span, jnp.dot(
            y_ref[i, :, span], rhs, preferred_element_type=jnp.float32
        ).astype(jnp.bfloat16))


def label_row(i, slot_ref, codes_ref):
    lane = lax.broadcasted_iota(jnp.int32, (1, LANES), 1)
    labels = jnp.full((1, LANES), -1, jnp.int32)
    for k in range(K):
        word = slot_ref[i, k]
        address = (word >> 21) - 1
        spot = jnp.maximum(address, 0)
        code = jnp.where(address < 0, 0, codes_ref[spot >> 6, 0, spot & 63])
        offset = ((word >> 9) & (LABELS - 1)) - 1
        labels = jnp.where(lane == k, offset + code, labels)
    return labels


def follower_kernel(slot_ref, send_ref, codes_ref, own_ref, y_ref, *refs):
    n = NX * NC * CHUNKS
    parts, outs, table, sems = refs[:n], refs[n:n + NG], refs[n + NG], refs[n + NG + 1]
    fill(table, own_ref, parts, sems)
    for s in range(NG):
        target = (lax.axis_index(AXES[0]) + s) & (NG - 1)
        for q in range(2):
            row = HALF + send_ref[0, target * 2 + q]

            def emit(span, value, s=s, q=q):
                outs[s][q, :, span] = value

            row_tiles(row, 1, table, slot_ref, y_ref, emit)
            labels = label_row(row, slot_ref, codes_ref)[:, 0:BLK]
            outs[s][q, 0:1, 0:BLK] = (labels >> 4).astype(jnp.float32).astype(jnp.bfloat16)
            outs[s][q, 16:17, 0:BLK] = (labels & 15).astype(jnp.float32).astype(jnp.bfloat16)


def leader_kernel(slot_ref, codes_ref, y_ref, table, out, labels_ref):
    def row(i, carry):
        def emit(span, value):
            out[i, :, span] = value

        row_tiles(i, 0, table, slot_ref, y_ref, emit)
        labels_ref[pl.ds(i, 1), :] = label_row(i, slot_ref, codes_ref)
        return carry

    lax.fori_loop(0, HALF, row, 0)


ROW_COST = pl.CostEstimate(flops=2 * 8 * 6 * BLK * LANES * LANES, bytes_accessed=5_000_000, transcendentals=0)


def followers(slots, send, codes, own, y, parts):
    shape = jax.ShapeDtypeStruct((2, BLK, WIDE), jnp.bfloat16)
    table = jax.ShapeDtypeStruct((TABLE + ROWS + 1, 32, LANES), jnp.bfloat16)
    return pl.pallas_call(
        follower_kernel,
        out_shape=[shape] * NG + [table],
        in_specs=[SMEM] * 3 + [VMEM] * 2 + [HBM] * len(parts),
        out_specs=[VMEM] * (NG + 1),
        scratch_shapes=[pltpu.SemaphoreType.DMA((len(parts),))],
        compiler_params=LIMIT,
        cost_estimate=ROW_COST,
        name="followers",
    )(slots, send, codes, own, y, *parts)


def leaders(slots, codes, y, table):
    return pl.pallas_call(
        leader_kernel,
        out_shape=[
            jax.ShapeDtypeStruct((HALF, BLK, WIDE), jnp.bfloat16),
            jax.ShapeDtypeStruct((HALF, LANES), jnp.int32),
        ],
        in_specs=[SMEM] * 2 + [VMEM] * 2,
        out_specs=[VMEM] * 2,
        compiler_params=LIMIT,
        cost_estimate=ROW_COST,
        name="leaders",
    )(slots, codes, y, table)


def code_kernel(slots_ref, codes_ref):
    g = lax.axis_index(AXES[0])
    shape = (NG, 1, 2)
    spot = lax.broadcasted_iota(jnp.int32, shape, 0) * 2 + lax.broadcasted_iota(jnp.int32, shape, 2)
    codes = jnp.zeros(shape, jnp.int32)
    for i in range(HALF):
        codes = jnp.where(spot == slots_ref[0, i], g * (N_DEV * HALF) + i, codes)
    codes_ref[...] = codes


def code_rows(slots):
    return pl.pallas_call(
        code_kernel,
        out_shape=jax.ShapeDtypeStruct((NG, 1, 2), jnp.int32),
        in_specs=[SMEM],
        out_specs=VMEM,
        name="codes",
    )(slots)


NOTE = NZ * C + HALF


def note_kernel(send_ref, lists_ref, returned_ref, out):
    lane = lax.broadcasted_iota(jnp.int32, (NX * NC, 1, HALF), 2)
    mine = jnp.zeros((NX * NC, 1, HALF), jnp.int32)
    for t in range(NG):
        for q in range(2):
            mine = jnp.where(lane == send_ref[0, 2 * t + q], returned_ref[t:t + 1, :, q:q + 1], mine)
    out[:, :, 0:NZ * C] = lists_ref[...]
    out[:, :, NZ * C:] = mine


def note_rows(send, lists, returned):
    return pl.pallas_call(
        note_kernel,
        out_shape=jax.ShapeDtypeStruct((NX * NC, 1, NOTE), jnp.int32),
        in_specs=[SMEM, VMEM, VMEM],
        out_specs=VMEM,
        name="note",
    )(send, lists, returned)


def plane_kernel(note_ref, out, row_ref):
    for d in range(NX * NC):
        row_ref[:, d * HALF:(d + 1) * HALF] = note_ref[d][:, NZ * C:]
    for z in range(NZ):
        out[z] = row_ref[...]


def plane_rows(note):
    return pl.pallas_call(
        plane_kernel,
        out_shape=jax.ShapeDtypeStruct((NZ, 1, NX * NC * HALF), jnp.int32),
        in_specs=[VMEM],
        out_specs=VMEM,
        scratch_shapes=[pltpu.VMEM((1, NX * NC * HALF), jnp.int32)],
        name="plane",
    )(note)


def slot_kernel(columns_ref, fetch_ref, slot_ref):
    g, x, z, c = (lax.axis_index(name) for name in AXES)
    device = x * (NZ * NC) + z * NC + c

    def row(i, carry):
        for k in range(K):
            column = columns_ref[i, k]
            ghost = jnp.maximum(column - ROWS, 0)
            local = column < ROWS
            asked = ghost >> 2
            peer = jnp.where(local, device, asked)
            row = jnp.where(local, jnp.maximum(column, 0), fetch_ref[asked, ghost & 3])
            px, pz, pc = peer >> 4, (peer >> 1) & (NZ - 1), peer & 1
            way = ((x - px) & (NX - 1)) * NC + (c ^ pc)
            at = jnp.where(local, TABLE + row, way * (NZ * C) + pz * C + (ghost & 3))
            late = row >= HALF
            spot = jnp.where(late, pz * (NX * NC * HALF) + (px * NC + pc) * HALF + row - HALF + 1, 0)
            offset = peer * HALF + 1 + jnp.where(late, 0, g * (N_DEV * HALF) + row)
            word = spot * (LABELS * SPOTS) + offset * SPOTS + at
            slot_ref[i, k] = jnp.where(column >= 0, word, TABLE + ROWS)
        return carry

    lax.fori_loop(0, ROWS, row, 0)


def slot_words(columns, fetch):
    return pl.pallas_call(
        slot_kernel,
        out_shape=jax.ShapeDtypeStruct((ROWS, K), jnp.int32),
        in_specs=[SMEM] * 2,
        out_specs=SMEM,
        cost_estimate=pl.CostEstimate(flops=1_000_000, bytes_accessed=2_000_000, transcendentals=0),
        name="slots",
    )(columns, fetch)


def merge_kernel(slots_ref, lead_ref, own_labels_ref, *refs):
    parts, out, labels_ref = refs[:NG], refs[NG], refs[NG + 1]
    follow, tiles, stage, sems, digits, work, steps_ref, next_ref, next_sem = refs[NG + 2:]
    per = SLOTS // 2

    lane = lax.broadcasted_iota(jnp.int32, (HALF, LANES), 1)
    for s in range(NG):
        for q in range(2):
            high = parts[s][q, 0:1, 0:LANES].astype(jnp.float32)
            rest = parts[s][q, 16:17, 0:LANES].astype(jnp.float32)
            digits[2 * s + q:2 * s + q + 1, :] = (high * 16.0 + rest).astype(jnp.int32)
    spots = []
    for n in range(HALF):
        spot = slots_ref[0, n]
        spots.append(((lax.axis_index(AXES[0]) - (spot >> 1)) & (NG - 1)) * 2 + (spot & 1))
        work[n:n + 1, :] = digits[pl.ds(spots[n], 1), :]
    labels = jnp.where(lane < 2 * K, pltpu.roll(work[...], K, 1), -1)
    work[...] = labels
    work[:, 0:K] = own_labels_ref[:, 0:K]
    labels = work[...]
    labels_ref[...] = work[:, 0:2 * K]
    twice = jnp.where(lane < 2 * K, labels, pltpu.roll(labels, 2 * K, 1))
    steps = jnp.full((HALF, LANES), 2 * K, jnp.int32)
    for d in range(2 * K - 1, 0, -1):
        steps = jnp.where(pltpu.roll(twice, LANES - d, 1) == labels, d, steps)
    steps = jnp.where((lane < 2 * K) & (labels >= 0), steps, 2 * K)
    usual = jnp.where((lane == 0) | (lane == K), K, 2 * K)
    odd = jnp.max(jnp.where(steps != usual, 1, 0), axis=1, keepdims=True)
    steps_ref[...] = jnp.where(lane == 2 * K, odd, steps)
    fetch = pltpu.make_async_copy(steps_ref, next_ref, next_sem)
    fetch.start()

    for s in range(NG):
        follow[2 * s:2 * s + 2] = parts[s][...]
    low = low_lanes((BLK, LANES))

    def save(n):
        return pltpu.make_async_copy(stage.at[n], out.at[n], sems.at[n])

    fetch.wait()
    for n in range(HALF):
        f = spots[n]

        def lead(t):
            return lead_ref[n, :, t * LANES:(t + 1) * LANES]

        def part(t):
            return follow[f, :, t * LANES:(t + 1) * LANES]

        first = lead(0).astype(jnp.float32)
        second = jnp.where(low, 0.0, part(0).astype(jnp.float32))
        stage[n, :, 0:LANES] = (first + pltpu.roll(second, BLK, 1)).astype(jnp.bfloat16)
        middle = lead(per - 1).astype(jnp.float32) + second
        middle = middle + jnp.where(low, 0.0, pltpu.roll(first, BLK, 1))
        stage[n, :, 5 * LANES:6 * LANES] = middle.astype(jnp.bfloat16)
        stage[n, :, LANES:5 * LANES] = lead_ref[n, :, LANES:5 * LANES]
        stage[n, :, 6 * LANES:] = follow[f, :, LANES:]

        @pl.when(next_ref[n, 2 * K] != 0)
        def _(n=n, lead=lead, part=part):
            for t in range(per):
                tiles[t] = lead(t).astype(jnp.float32)
                tiles[per + t] = part(t).astype(jnp.float32)
            plain = (next_ref[n, 0] == K) & (next_ref[n, K] == K)
            for s in range(2 * K):
                step = next_ref[n, s]
                skip = plain if s in (0, K) else step == 2 * K

                @pl.when(jnp.logical_not(skip))
                def _(s=s, step=step):
                    home = s if s < K else s + 2

                    def block(t):
                        spot = jnp.where(t < K, t, t + 2)
                        value = tiles[spot >> 1]
                        same = jnp.broadcast_to((spot & 1) == (home & 1), value.shape)
                        return jnp.where(same, value, pltpu.roll(value, BLK, 1))

                    def after(t, step):
                        t = t + step
                        return jnp.where(t >= 2 * K, t - 2 * K, t)

                    def more(carry):
                        return carry[0] != s

                    def add(carry):
                        t, total = carry
                        return after(t, next_ref[n, t]), total + block(t)

                    _, total = lax.while_loop(more, add, (after(s, step), block(jnp.int32(s))))
                    span = slice((s // 2) * LANES, (s // 2 + 1) * LANES)
                    keep = low if s % 2 == 0 else jnp.logical_not(low)
                    stage[n, :, span] = jnp.where(
                        keep, total, stage[n, :, span].astype(jnp.float32)
                    ).astype(jnp.bfloat16)

        save(n).start()
    for n in range(HALF):
        save(n).wait()


def merge(slots, lead, own_labels, parts):
    return pl.pallas_call(
        merge_kernel,
        out_shape=[
            jax.ShapeDtypeStruct((HALF, BLK, 2 * K * BLK), jnp.bfloat16),
            jax.ShapeDtypeStruct((HALF, 2 * K), jnp.int32),
        ],
        in_specs=[SMEM] + [VMEM] * (2 + NG),
        out_specs=[pl.BlockSpec(memory_space=pl.ANY), VMEM],
        scratch_shapes=[
            pltpu.VMEM((2 * NG, BLK, WIDE), jnp.bfloat16),
            pltpu.VMEM((SLOTS, BLK, LANES), jnp.float32),
            pltpu.VMEM((HALF, BLK, 2 * K * BLK), jnp.bfloat16),
            pltpu.SemaphoreType.DMA((HALF,)),
            pltpu.VMEM((HALF, LANES), jnp.int32),
            pltpu.VMEM((HALF, LANES), jnp.int32),
            pltpu.VMEM((HALF, LANES), jnp.int32),
            pltpu.SMEM((HALF, LANES), jnp.int32),
            pltpu.SemaphoreType.DMA,
        ],
        compiler_params=LIMIT,
        name="merge",
    )(slots, lead, own_labels, *parts)


def shift(value, axis, size, by):
    if by == 0:
        return value
    return lax.ppermute(value, axis, [(i, (i + by) % size) for i in range(size)])


def cross(value, b):
    if b == 0:
        return value
    by, flip = b // NC, b % NC
    pairs = [
        (x * NC + c, ((x + by) % NX) * NC + (c ^ flip)) for x in range(NX) for c in range(NC)
    ]
    return lax.ppermute(value, ("x", "core"), pairs)


def per_device(stiffness, prolongator, columns, fetch_rows, send_order, partner_slot):
    g, x, z, c = (lax.axis_index(name) for name in AXES)
    device = x * (NZ * NC) + z * NC + c
    own = prolongator.reshape(ROWS, 32, LANES)

    held = []
    for h in range(CHUNKS):
        piece = own[:, h * CK:(h + 1) * CK]
        got = {0: piece}
        for s in (4, 2, 6, 1, 7):
            got[s] = shift(piece, "z", NZ, s)
        got[5] = shift(got[4], "z", NZ, 1)
        got[3] = shift(got[4], "z", NZ, NZ - 1)
        held.append([got[s] for s in range(NZ)])

    returned = lax.all_to_all(code_rows(partner_slot), "grp", split_axis=0, concat_axis=0, tiled=True)
    lists = fetch_rows.reshape(NX, NZ, NC, C).transpose(0, 2, 1, 3).reshape(NX * NC, 1, NZ * C)
    note = note_rows(send_order, lists, returned)
    wanted = lax.all_to_all(note, ("x", "core"), split_axis=0, concat_axis=0, tiled=True)
    words = slot_words(columns, fetch_rows)
    lane = jnp.arange(LANES, dtype=jnp.int32)
    inner = lane & (BLK - 1)
    source = (lane & BLK) + jnp.where(inner < 32, 2 * inner, 2 * (inner - 32) + 1)
    perm = (lane[:, None] == source[None, :]).astype(jnp.bfloat16)
    y = products(prolongator.reshape(ROWS, BLK, BLK), perm, stiffness)
    wanted, y = lax.optimization_barrier((wanted, y))
    codes = lax.all_to_all(plane_rows(wanted), "z", split_axis=0, concat_axis=0, tiled=True)

    parts = []
    for h in range(CHUNKS):
        chosen = select(wanted, held[h])
        moved = {b: cross(chosen[i], b) for i, b in enumerate(ORDER)}
        parts += [pltpu.with_memory_space_constraint(moved[b], pltpu.HBM) for b in range(NX * NC)]

    *sent, table = followers(words, send_order, codes, own, y, parts)
    arrived = [sent[0]] + [shift(sent[s], "grp", NG, s) for s in range(1, NG)]
    lead, lead_labels = leaders(words, codes, y, table)
    return tuple(merge(partner_slot, lead, lead_labels, arrived))


def solution(mesh):
    grid = Mesh(mesh.devices.reshape(NG, NX, NZ, NC), AXES)
    return jax.shard_map(
        per_device,
        mesh=grid,
        in_specs=(
            P(AXES, None, None),
            P(AXES, None),
            P(AXES, None),
            P(AXES, None),
            P(AXES, None),
            P(AXES, None),
        ),
        out_specs=(P(AXES, None, None), P(AXES, None)),
        check_vma=False,
    )
```

```python
import functools

import jax
import jax.numpy as jnp
from jax import lax
from jax.experimental import pallas as pl
from jax.experimental.pallas import tpu as pltpu
from jax.sharding import Mesh, PartitionSpec as P

BLK = 64
K = 11
C = 4
ROWS = 16
HALF = 8
NG, NX, NZ, NC = 4, 4, 8, 2
N_DEV = NX * NZ * NC
LANES = 128
SLOTS = 12
WIDE = SLOTS * BLK
TABLE = N_DEV * C
SPOTS, LABELS = 512, 4096
CHUNKS = 1
CK = 32 // CHUNKS
AXES = ("grp", "x", "z", "core")
ORDER = ((2, 6, 4, 5, 1), (3, 7), (0,))

VMEM = pl.BlockSpec(memory_space=pltpu.VMEM)
SMEM = pl.BlockSpec(memory_space=pltpu.SMEM)
HBM = pl.BlockSpec(memory_space=pltpu.HBM)
LIMIT = pltpu.CompilerParams(vmem_limit_bytes=12 * 1024 * 1024)


def low_lanes(shape):
    return lax.broadcasted_iota(jnp.int32, shape, 1) < BLK


STEP = 4


def products_kernel(p_ref, perm_ref, a_hbm, y_ref, a_ref, work, sems):
    def load(h):
        rows = pl.ds(h * STEP, STEP)
        return pltpu.make_async_copy(a_hbm.at[rows], a_ref.at[rows], sems.at[h])

    for h in range(ROWS // STEP):
        load(h).start()
    perm = perm_ref[...]
    pad = jnp.zeros((BLK, BLK), jnp.float32)
    for h in range(ROWS // STEP):
        load(h).wait()
        for i in range(STEP):
            y = lax.dot_general(
                p_ref[h * STEP + i], a_ref[h * STEP + i], (((0,), (0,)), ((), ())),
                preferred_element_type=jnp.float32,
            )
            y = jnp.concatenate([y, pad] if h * STEP + i < HALF else [pad, y], axis=1)
            work[h, i * BLK:(i + 1) * BLK] = y.astype(jnp.bfloat16)
        for t in range(WIDE // LANES):
            span = slice(t * LANES, (t + 1) * LANES)
            y_ref[h * STEP:(h + 1) * STEP, :, span] = jnp.dot(
                work[h, :, span], perm, preferred_element_type=jnp.float32
            ).astype(jnp.bfloat16).reshape(STEP, BLK, LANES)


def products(blocks, perm, stiffness):
    return pl.pallas_call(
        products_kernel,
        out_shape=jax.ShapeDtypeStruct((ROWS, BLK, WIDE), jnp.bfloat16),
        in_specs=[VMEM, VMEM, HBM],
        out_specs=VMEM,
        scratch_shapes=[
            pltpu.VMEM((ROWS, BLK, K * BLK), jnp.bfloat16),
            pltpu.VMEM((ROWS // STEP, STEP * BLK, WIDE), jnp.bfloat16),
            pltpu.SemaphoreType.DMA((ROWS // STEP,)),
        ],
        compiler_params=LIMIT,
        cost_estimate=pl.CostEstimate(
            flops=2 * ROWS * BLK * BLK * WIDE * 3, bytes_accessed=3_200_000, transcendentals=0
        ),
        name="products",
    )(blocks, perm, stiffness)


def select_kernel(targets, wanted_ref, *refs):
    n = len(targets)
    held, outs, stage, sems = refs[:NZ], refs[NZ:NZ + n], refs[NZ + n], refs[NZ + n + 1]
    x, z, c = (lax.axis_index(name) for name in AXES[1:])
    copies = []
    for i, b in enumerate(targets):
        target = ((x + b // NC) & (NX - 1)) * NC + (c ^ (b % NC))
        for s in range(NZ):
            home = ((z - s) & (NZ - 1)) * C
            for m in range(C):
                stage[i, home + m] = held[s][wanted_ref[target, 0, home + m]]
        copy = pltpu.make_async_copy(stage.at[i], outs[i], sems.at[i])
        copy.start()
        copies.append(copy)
    for copy in copies:
        copy.wait()


def select(targets, wanted, held):
    n = len(targets)
    shape = (NZ * C, CK, LANES)
    return pl.pallas_call(
        functools.partial(select_kernel, targets),
        out_shape=[jax.ShapeDtypeStruct(shape, jnp.bfloat16)] * n,
        in_specs=[SMEM] + [VMEM] * NZ,
        out_specs=[HBM] * n,
        scratch_shapes=[pltpu.VMEM((n,) + shape, jnp.bfloat16), pltpu.SemaphoreType.DMA((n,))],
        compiler_params=LIMIT,
        name="select",
    )(wanted, *held)


def fill(table, own_ref, parts, sems):
    n = NX * NC
    copies = []
    for h in range(CHUNKS):
        for b in range(n):
            spot = table.at[pl.ds(b * NZ * C, NZ * C), pl.ds(h * CK, CK)]
            copies.append(pltpu.make_async_copy(parts[h * n + b], spot, sems.at[h * n + b]))
    for copy in copies:
        copy.start()
    table[TABLE:TABLE + ROWS] = own_ref[...]
    table[TABLE + ROWS] = jnp.zeros((32, LANES), jnp.bfloat16)
    for copy in copies:
        copy.wait()


def row_tiles(i, late, table, slot_ref, y_ref, emit):
    low = low_lanes((32, LANES))
    zero = jnp.zeros((32, LANES), jnp.bfloat16)
    for t in range(SLOTS // 2):
        a, b = (
            table[slot_ref[i, k] & (SPOTS - 1) if 0 <= k < K else TABLE + ROWS]
            for k in (2 * t - late, 2 * t + 1 - late)
        )
        rhs = jnp.concatenate([
            jnp.where(low, a, zero),
            jnp.where(low, pltpu.roll(a, BLK, 1), zero),
            jnp.where(low, zero, pltpu.roll(b, BLK, 1)),
            jnp.where(low, zero, b),
        ], axis=0)
        span = slice(t * LANES, (t + 1) * LANES)
        emit(span, jnp.dot(
            y_ref[i, :, span], rhs, preferred_element_type=jnp.float32
        ).astype(jnp.bfloat16))


def label_row(i, slot_ref, codes_ref):
    lane = lax.broadcasted_iota(jnp.int32, (1, LANES), 1)
    labels = jnp.full((1, LANES), -1, jnp.int32)
    for k in range(K):
        word = slot_ref[i, k]
        address = (word >> 21) - 1
        spot = jnp.maximum(address, 0)
        code = jnp.where(address < 0, 0, codes_ref[spot >> 6, 0, spot & 63])
        offset = ((word >> 9) & (LABELS - 1)) - 1
        labels = jnp.where(lane == k, offset + code, labels)
    return labels


def follower_kernel(shifts, slot_ref, send_ref, codes_ref, y_ref, *refs):
    outs = refs[len(refs) - len(shifts):]
    table = refs[0]
    for i, s in enumerate(shifts):
        target = (lax.axis_index(AXES[0]) + s) & (NG - 1)
        for q in range(2):
            row = HALF + send_ref[0, target * 2 + q]

            def emit(span, value, i=i, q=q):
                outs[i][q, :, span] = value

            row_tiles(row, 1, table, slot_ref, y_ref, emit)
            labels = label_row(row, slot_ref, codes_ref)[:, 0:BLK]
            outs[i][q, 0:1, 0:BLK] = (labels >> 4).astype(jnp.float32).astype(jnp.bfloat16)
            outs[i][q, 16:17, 0:BLK] = (labels & 15).astype(jnp.float32).astype(jnp.bfloat16)


def first_kernel(shifts, slot_ref, send_ref, codes_ref, y_ref, own_ref, *refs):
    n = NX * NC * CHUNKS
    parts, outs, table, sems = refs[:n], refs[n:n + len(shifts)], refs[-2], refs[-1]
    fill(table, own_ref, parts, sems)
    follower_kernel(shifts, slot_ref, send_ref, codes_ref, y_ref, table, *outs)


def leader_kernel(slot_ref, codes_ref, y_ref, table, out, labels_ref):
    def row(i, carry):
        def emit(span, value):
            out[i, :, span] = value

        row_tiles(i, 0, table, slot_ref, y_ref, emit)
        labels_ref[pl.ds(i, 1), :] = label_row(i, slot_ref, codes_ref)
        return carry

    lax.fori_loop(0, HALF, row, 0)


ROW_COST = pl.CostEstimate(flops=2 * 8 * 6 * BLK * LANES * LANES, bytes_accessed=5_000_000, transcendentals=0)


def first_followers(shifts, slots, send, codes, own, y, parts):
    shape = jax.ShapeDtypeStruct((2, BLK, WIDE), jnp.bfloat16)
    table = jax.ShapeDtypeStruct((TABLE + ROWS + 1, 32, LANES), jnp.bfloat16)
    return pl.pallas_call(
        functools.partial(first_kernel, shifts),
        out_shape=[shape] * len(shifts) + [table],
        in_specs=[SMEM] * 3 + [VMEM] * 2 + [HBM] * len(parts),
        out_specs=[VMEM] * (len(shifts) + 1),
        scratch_shapes=[pltpu.SemaphoreType.DMA((len(parts),))],
        compiler_params=LIMIT,
        cost_estimate=ROW_COST,
        name="first",
    )(slots, send, codes, y, own, *parts)


def followers(shifts, slots, send, codes, y, table):
    shape = jax.ShapeDtypeStruct((2, BLK, WIDE), jnp.bfloat16)
    return pl.pallas_call(
        functools.partial(follower_kernel, shifts),
        out_shape=[shape] * len(shifts),
        in_specs=[SMEM] * 3 + [VMEM] * 2,
        out_specs=[VMEM] * len(shifts),
        compiler_params=LIMIT,
        cost_estimate=ROW_COST,
        name="followers",
    )(slots, send, codes, y, table)


def leaders(slots, codes, y, table):
    return pl.pallas_call(
        leader_kernel,
        out_shape=[
            jax.ShapeDtypeStruct((HALF, BLK, WIDE), jnp.bfloat16),
            jax.ShapeDtypeStruct((HALF, LANES), jnp.int32),
        ],
        in_specs=[SMEM] * 2 + [VMEM] * 2,
        out_specs=[VMEM] * 2,
        compiler_params=LIMIT,
        cost_estimate=ROW_COST,
        name="leaders",
    )(slots, codes, y, table)


def code_kernel(slots_ref, codes_ref):
    g = lax.axis_index(AXES[0])
    shape = (NG, 1, 2)
    spot = lax.broadcasted_iota(jnp.int32, shape, 0) * 2 + lax.broadcasted_iota(jnp.int32, shape, 2)
    codes = jnp.zeros(shape, jnp.int32)
    for i in range(HALF):
        codes = jnp.where(spot == slots_ref[0, i], g * (N_DEV * HALF) + i, codes)
    codes_ref[...] = codes


def code_rows(slots):
    return pl.pallas_call(
        code_kernel,
        out_shape=jax.ShapeDtypeStruct((NG, 1, 2), jnp.int32),
        in_specs=[SMEM],
        out_specs=VMEM,
        name="codes",
    )(slots)


NOTE = NZ * C + HALF


def note_kernel(send_ref, lists_ref, returned_ref, out):
    lane = lax.broadcasted_iota(jnp.int32, (NX * NC, 1, HALF), 2)
    mine = jnp.zeros((NX * NC, 1, HALF), jnp.int32)
    for t in range(NG):
        for q in range(2):
            mine = jnp.where(lane == send_ref[0, 2 * t + q], returned_ref[t:t + 1, :, q:q + 1], mine)
    out[:, :, 0:NZ * C] = lists_ref[...]
    out[:, :, NZ * C:] = mine


def note_rows(send, lists, returned):
    return pl.pallas_call(
        note_kernel,
        out_shape=jax.ShapeDtypeStruct((NX * NC, 1, NOTE), jnp.int32),
        in_specs=[SMEM, VMEM, VMEM],
        out_specs=VMEM,
        name="note",
    )(send, lists, returned)


def plane_kernel(note_ref, out, row_ref):
    for d in range(NX * NC):
        row_ref[:, d * HALF:(d + 1) * HALF] = note_ref[d][:, NZ * C:]
    for z in range(NZ):
        out[z] = row_ref[...]


def plane_rows(note):
    return pl.pallas_call(
        plane_kernel,
        out_shape=jax.ShapeDtypeStruct((NZ, 1, NX * NC * HALF), jnp.int32),
        in_specs=[VMEM],
        out_specs=VMEM,
        scratch_shapes=[pltpu.VMEM((1, NX * NC * HALF), jnp.int32)],
        name="plane",
    )(note)


def slot_kernel(columns_ref, fetch_ref, slot_ref):
    g, x, z, c = (lax.axis_index(name) for name in AXES)
    device = x * (NZ * NC) + z * NC + c

    def row(i, carry):
        for k in range(K):
            column = columns_ref[i, k]
            ghost = jnp.maximum(column - ROWS, 0)
            local = column < ROWS
            asked = ghost >> 2
            peer = jnp.where(local, device, asked)
            row = jnp.where(local, jnp.maximum(column, 0), fetch_ref[asked, ghost & 3])
            px, pz, pc = peer >> 4, (peer >> 1) & (NZ - 1), peer & 1
            way = ((x - px) & (NX - 1)) * NC + (c ^ pc)
            at = jnp.where(local, TABLE + row, way * (NZ * C) + pz * C + (ghost & 3))
            late = row >= HALF
            spot = jnp.where(late, pz * (NX * NC * HALF) + (px * NC + pc) * HALF + row - HALF + 1, 0)
            offset = peer * HALF + 1 + jnp.where(late, 0, g * (N_DEV * HALF) + row)
            word = spot * (LABELS * SPOTS) + offset * SPOTS + at
            slot_ref[i, k] = jnp.where(column >= 0, word, TABLE + ROWS)
        return carry

    lax.fori_loop(0, ROWS, row, 0)


def slot_words(columns, fetch):
    return pl.pallas_call(
        slot_kernel,
        out_shape=jax.ShapeDtypeStruct((ROWS, K), jnp.int32),
        in_specs=[SMEM] * 2,
        out_specs=SMEM,
        cost_estimate=pl.CostEstimate(flops=1_000_000, bytes_accessed=2_000_000, transcendentals=0),
        name="slots",
    )(columns, fetch)


def merge_kernel(slots_ref, lead_ref, own_labels_ref, *refs):
    parts, out, labels_ref = refs[:NG], refs[NG], refs[NG + 1]
    follow, tiles, stage, sems, digits, work, steps_ref, next_ref, next_sem = refs[NG + 2:]
    per = SLOTS // 2

    lane = lax.broadcasted_iota(jnp.int32, (HALF, LANES), 1)
    for s in range(NG):
        for q in range(2):
            high = parts[s][q, 0:1, 0:LANES].astype(jnp.float32)
            rest = parts[s][q, 16:17, 0:LANES].astype(jnp.float32)
            digits[2 * s + q:2 * s + q + 1, :] = (high * 16.0 + rest).astype(jnp.int32)
    spots = []
    for n in range(HALF):
        spot = slots_ref[0, n]
        spots.append(((lax.axis_index(AXES[0]) - (spot >> 1)) & (NG - 1)) * 2 + (spot & 1))
        work[n:n + 1, :] = digits[pl.ds(spots[n], 1), :]
    labels = jnp.where(lane < 2 * K, pltpu.roll(work[...], K, 1), -1)
    work[...] = labels
    work[:, 0:K] = own_labels_ref[:, 0:K]
    labels = work[...]
    labels_ref[...] = work[:, 0:2 * K]
    twice = jnp.where(lane < 2 * K, labels, pltpu.roll(labels, 2 * K, 1))
    steps = jnp.full((HALF, LANES), 2 * K, jnp.int32)
    for d in range(2 * K - 1, 0, -1):
        steps = jnp.where(pltpu.roll(twice, LANES - d, 1) == labels, d, steps)
    steps = jnp.where((lane < 2 * K) & (labels >= 0), steps, 2 * K)
    usual = jnp.where((lane == 0) | (lane == K), K, 2 * K)
    odd = jnp.max(jnp.where(steps != usual, 1, 0), axis=1, keepdims=True)
    steps_ref[...] = jnp.where(lane == 2 * K, odd, steps)
    fetch = pltpu.make_async_copy(steps_ref, next_ref, next_sem)
    fetch.start()

    for s in range(NG):
        follow[2 * s:2 * s + 2] = parts[s][...]
    low = low_lanes((BLK, LANES))

    def save(n):
        return pltpu.make_async_copy(stage.at[n], out.at[n], sems.at[n])

    fetch.wait()
    for n in range(HALF):
        f = spots[n]

        def lead(t):
            return lead_ref[n, :, t * LANES:(t + 1) * LANES]

        def part(t):
            return follow[f, :, t * LANES:(t + 1) * LANES]

        first = lead(0).astype(jnp.float32)
        second = jnp.where(low, 0.0, part(0).astype(jnp.float32))
        stage[n, :, 0:LANES] = (first + pltpu.roll(second, BLK, 1)).astype(jnp.bfloat16)
        middle = lead(per - 1).astype(jnp.float32) + second
        middle = middle + jnp.where(low, 0.0, pltpu.roll(first, BLK, 1))
        stage[n, :, 5 * LANES:6 * LANES] = middle.astype(jnp.bfloat16)
        stage[n, :, LANES:5 * LANES] = lead_ref[n, :, LANES:5 * LANES]
        stage[n, :, 6 * LANES:] = follow[f, :, LANES:]

        @pl.when(next_ref[n, 2 * K] != 0)
        def _(n=n, lead=lead, part=part):
            for t in range(per):
                tiles[t] = lead(t).astype(jnp.float32)
                tiles[per + t] = part(t).astype(jnp.float32)
            plain = (next_ref[n, 0] == K) & (next_ref[n, K] == K)
            for s in range(2 * K):
                step = next_ref[n, s]
                skip = plain if s in (0, K) else step == 2 * K

                @pl.when(jnp.logical_not(skip))
                def _(s=s, step=step):
                    home = s if s < K else s + 2

                    def block(t):
                        spot = jnp.where(t < K, t, t + 2)
                        value = tiles[spot >> 1]
                        same = jnp.broadcast_to((spot & 1) == (home & 1), value.shape)
                        return jnp.where(same, value, pltpu.roll(value, BLK, 1))

                    def after(t, step):
                        t = t + step
                        return jnp.where(t >= 2 * K, t - 2 * K, t)

                    def more(carry):
                        return carry[0] != s

                    def add(carry):
                        t, total = carry
                        return after(t, next_ref[n, t]), total + block(t)

                    _, total = lax.while_loop(more, add, (after(s, step), block(jnp.int32(s))))
                    span = slice((s // 2) * LANES, (s // 2 + 1) * LANES)
                    keep = low if s % 2 == 0 else jnp.logical_not(low)
                    stage[n, :, span] = jnp.where(
                        keep, total, stage[n, :, span].astype(jnp.float32)
                    ).astype(jnp.bfloat16)

        save(n).start()
    for n in range(HALF):
        save(n).wait()


def merge(slots, lead, own_labels, parts):
    return pl.pallas_call(
        merge_kernel,
        out_shape=[
            jax.ShapeDtypeStruct((HALF, BLK, 2 * K * BLK), jnp.bfloat16),
            jax.ShapeDtypeStruct((HALF, 2 * K), jnp.int32),
        ],
        in_specs=[SMEM] + [VMEM] * (2 + NG),
        out_specs=[pl.BlockSpec(memory_space=pl.ANY), VMEM],
        scratch_shapes=[
            pltpu.VMEM((2 * NG, BLK, WIDE), jnp.bfloat16),
            pltpu.VMEM((SLOTS, BLK, LANES), jnp.float32),
            pltpu.VMEM((HALF, BLK, 2 * K * BLK), jnp.bfloat16),
            pltpu.SemaphoreType.DMA((HALF,)),
            pltpu.VMEM((HALF, LANES), jnp.int32),
            pltpu.VMEM((HALF, LANES), jnp.int32),
            pltpu.VMEM((HALF, LANES), jnp.int32),
            pltpu.SMEM((HALF, LANES), jnp.int32),
            pltpu.SemaphoreType.DMA,
        ],
        compiler_params=LIMIT,
        name="merge",
    )(slots, lead, own_labels, *parts)


def shift(value, axis, size, by):
    if by == 0:
        return value
    return lax.ppermute(value, axis, [(i, (i + by) % size) for i in range(size)])


def cross(value, b):
    if b == 0:
        return value
    by, flip = b // NC, b % NC
    pairs = [
        (x * NC + c, ((x + by) % NX) * NC + (c ^ flip)) for x in range(NX) for c in range(NC)
    ]
    return lax.ppermute(value, ("x", "core"), pairs)


def per_device(stiffness, prolongator, columns, fetch_rows, send_order, partner_slot):
    g, x, z, c = (lax.axis_index(name) for name in AXES)
    device = x * (NZ * NC) + z * NC + c
    own = prolongator.reshape(ROWS, 32, LANES)

    held = []
    for h in range(CHUNKS):
        piece = own[:, h * CK:(h + 1) * CK]
        got = {0: piece}
        for s in (4, 2, 6, 1, 7):
            got[s] = shift(piece, "z", NZ, s)
        got[5] = shift(got[4], "z", NZ, 1)
        got[3] = shift(got[4], "z", NZ, NZ - 1)
        held.append([got[s] for s in range(NZ)])

    returned = lax.all_to_all(code_rows(partner_slot), "grp", split_axis=0, concat_axis=0, tiled=True)
    lists = fetch_rows.reshape(NX, NZ, NC, C).transpose(0, 2, 1, 3).reshape(NX * NC, 1, NZ * C)
    note = note_rows(send_order, lists, returned)
    wanted = lax.all_to_all(note, ("x", "core"), split_axis=0, concat_axis=0, tiled=True)
    words = pltpu.with_memory_space_constraint(slot_words(columns, fetch_rows), pltpu.HBM)
    lane = jnp.arange(LANES, dtype=jnp.int32)
    inner = lane & (BLK - 1)
    source = (lane & BLK) + jnp.where(inner < 32, 2 * inner, 2 * (inner - 32) + 1)
    perm = (lane[:, None] == source[None, :]).astype(jnp.bfloat16)
    y = products(prolongator.reshape(ROWS, BLK, BLK), perm, stiffness)
    wanted, y = lax.optimization_barrier((wanted, y))
    codes = lax.all_to_all(plane_rows(wanted), "z", split_axis=0, concat_axis=0, tiled=True)

    parts = []
    for h in range(CHUNKS):
        chosen = []
        for targets in ORDER:
            chosen += select(targets, wanted, held[h])
            wanted, chosen[-1] = lax.optimization_barrier((wanted, chosen[-1]))
        moved = {b: cross(chosen[i], b) for i, b in enumerate(sum(ORDER, ()))}
        parts += [pltpu.with_memory_space_constraint(moved[b], pltpu.HBM) for b in range(NX * NC)]

    sent = {}
    sent[2], table = first_followers((2,), words, send_order, codes, own, y, parts)
    sent[1], sent[3], sent[0] = followers((1, 3, 0), words, send_order, codes, y, table)
    arrived = [shift(sent[s], "grp", NG, s) for s in range(NG)]
    lead, lead_labels = leaders(words, codes, y, table)
    return tuple(merge(partner_slot, lead, lead_labels, arrived))


def solution(mesh):
    grid = Mesh(mesh.devices.reshape(NG, NX, NZ, NC), AXES)
    return jax.shard_map(
        per_device,
        mesh=grid,
        in_specs=(
            P(AXES, None, None),
            P(AXES, None),
            P(AXES, None),
            P(AXES, None),
            P(AXES, None),
            P(AXES, None),
        ),
        out_specs=(P(AXES, None, None), P(AXES, None)),
        check_vma=False,
    )
```

```python
import functools

import jax
import jax.numpy as jnp
from jax import lax
from jax.experimental import pallas as pl
from jax.experimental.pallas import tpu as pltpu
from jax.sharding import Mesh, PartitionSpec as P

BLK = 64
K = 11
C = 4
ROWS = 16
HALF = 8
NG, NX, NZ, NC = 4, 4, 8, 2
N_DEV = NX * NZ * NC
LANES = 128
SLOTS = 12
WIDE = SLOTS * BLK
TABLE = N_DEV * C
SPOTS, LABELS = 512, 4096
CHUNKS = 1
CK = 32 // CHUNKS
AXES = ("grp", "x", "z", "core")
ORDER = ((2, 6, 4, 5, 1), (3, 7), (0,))

VMEM = pl.BlockSpec(memory_space=pltpu.VMEM)
SMEM = pl.BlockSpec(memory_space=pltpu.SMEM)
HBM = pl.BlockSpec(memory_space=pltpu.HBM)
LIMIT = pltpu.CompilerParams(vmem_limit_bytes=12 * 1024 * 1024)


def low_lanes(shape):
    return lax.broadcasted_iota(jnp.int32, shape, 1) < BLK


STEP = 4


def products_kernel(own_ref, perm_ref, a_hbm, y_ref, a_ref, work, sems):
    def load(h):
        rows = pl.ds(h * STEP, STEP)
        return pltpu.make_async_copy(a_hbm.at[rows], a_ref.at[rows], sems.at[h])

    for h in range(ROWS // STEP):
        load(h).start()
    perm = perm_ref[...]
    pad = jnp.zeros((BLK, BLK), jnp.float32)
    for h in range(ROWS // STEP):
        load(h).wait()
        for i in range(STEP):
            block = own_ref[h * STEP + i]
            block = jnp.concatenate([block, pltpu.roll(block, BLK, 1)], axis=0)
            block = jnp.dot(perm[0:BLK, 0:BLK], block, preferred_element_type=jnp.float32)
            block = block[:, 0:BLK].astype(jnp.bfloat16)
            y = lax.dot_general(
                block, a_ref[h * STEP + i], (((0,), (0,)), ((), ())),
                preferred_element_type=jnp.float32,
            )
            y = jnp.concatenate([y, pad] if h * STEP + i < HALF else [pad, y], axis=1)
            work[h, i * BLK:(i + 1) * BLK] = y.astype(jnp.bfloat16)
        for t in range(WIDE // LANES):
            span = slice(t * LANES, (t + 1) * LANES)
            y_ref[h * STEP:(h + 1) * STEP, :, span] = jnp.dot(
                work[h, :, span], perm, preferred_element_type=jnp.float32
            ).astype(jnp.bfloat16).reshape(STEP, BLK, LANES)


def products(own, perm, stiffness):
    return pl.pallas_call(
        products_kernel,
        out_shape=jax.ShapeDtypeStruct((ROWS, BLK, WIDE), jnp.bfloat16),
        in_specs=[VMEM, VMEM, HBM],
        out_specs=VMEM,
        scratch_shapes=[
            pltpu.VMEM((ROWS, BLK, K * BLK), jnp.bfloat16),
            pltpu.VMEM((ROWS // STEP, STEP * BLK, WIDE), jnp.bfloat16),
            pltpu.SemaphoreType.DMA((ROWS // STEP,)),
        ],
        compiler_params=LIMIT,
        cost_estimate=pl.CostEstimate(
            flops=2 * ROWS * BLK * BLK * WIDE * 3, bytes_accessed=3_200_000, transcendentals=0
        ),
        name="products",
    )(own, perm, stiffness)


def select_kernel(targets, wanted_ref, *refs):
    n = len(targets)
    held, outs, stage, sems = refs[:NZ], refs[NZ:NZ + n], refs[NZ + n], refs[NZ + n + 1]
    x, z, c = (lax.axis_index(name) for name in AXES[1:])
    copies = []
    for i, b in enumerate(targets):
        target = ((x + b // NC) & (NX - 1)) * NC + (c ^ (b % NC))
        for s in range(NZ):
            home = ((z - s) & (NZ - 1)) * C
            for m in range(C):
                stage[i, home + m] = held[s][wanted_ref[target, 0, home + m]]
        copy = pltpu.make_async_copy(stage.at[i], outs[i], sems.at[i])
        copy.start()
        copies.append(copy)
    for copy in copies:
        copy.wait()


def select(targets, wanted, held):
    n = len(targets)
    shape = (NZ * C, CK, LANES)
    return pl.pallas_call(
        functools.partial(select_kernel, targets),
        out_shape=[jax.ShapeDtypeStruct(shape, jnp.bfloat16)] * n,
        in_specs=[SMEM] + [VMEM] * NZ,
        out_specs=[HBM] * n,
        scratch_shapes=[pltpu.VMEM((n,) + shape, jnp.bfloat16), pltpu.SemaphoreType.DMA((n,))],
        compiler_params=LIMIT,
        name="select",
    )(wanted, *held)


def fill(table, own_ref, parts, sems):
    n = NX * NC
    copies = []
    for h in range(CHUNKS):
        for b in range(n):
            spot = table.at[pl.ds(b * NZ * C, NZ * C), pl.ds(h * CK, CK)]
            copies.append(pltpu.make_async_copy(parts[h * n + b], spot, sems.at[h * n + b]))
    for copy in copies:
        copy.start()
    table[TABLE:TABLE + ROWS] = own_ref[...]
    table[TABLE + ROWS] = jnp.zeros((32, LANES), jnp.bfloat16)
    for copy in copies:
        copy.wait()


def row_tiles(i, late, table, slot_ref, y_ref, emit):
    low = low_lanes((32, LANES))
    zero = jnp.zeros((32, LANES), jnp.bfloat16)
    for t in range(SLOTS // 2):
        a, b = (
            table[slot_ref[i, k] & (SPOTS - 1) if 0 <= k < K else TABLE + ROWS]
            for k in (2 * t - late, 2 * t + 1 - late)
        )
        rhs = jnp.concatenate([
            jnp.where(low, a, zero),
            jnp.where(low, pltpu.roll(a, BLK, 1), zero),
            jnp.where(low, zero, pltpu.roll(b, BLK, 1)),
            jnp.where(low, zero, b),
        ], axis=0)
        span = slice(t * LANES, (t + 1) * LANES)
        emit(span, jnp.dot(
            y_ref[i, :, span], rhs, preferred_element_type=jnp.float32
        ).astype(jnp.bfloat16))


def label_row(i, slot_ref, codes_ref):
    lane = lax.broadcasted_iota(jnp.int32, (1, LANES), 1)
    labels = jnp.full((1, LANES), -1, jnp.int32)
    for k in range(K):
        word = slot_ref[i, k]
        address = (word >> 21) - 1
        spot = jnp.maximum(address, 0)
        code = jnp.where(address < 0, 0, codes_ref[spot >> 6, 0, spot & 63])
        offset = ((word >> 9) & (LABELS - 1)) - 1
        labels = jnp.where(lane == k, offset + code, labels)
    return labels


def follower_kernel(shifts, slot_ref, send_ref, codes_ref, y_ref, *refs):
    outs = refs[len(refs) - len(shifts):]
    table = refs[0]
    for i, s in enumerate(shifts):
        target = (lax.axis_index(AXES[0]) + s) & (NG - 1)
        for q in range(2):
            row = HALF + send_ref[0, target * 2 + q]

            def emit(span, value, i=i, q=q):
                outs[i][q, :, span] = value

            row_tiles(row, 1, table, slot_ref, y_ref, emit)
            labels = label_row(row, slot_ref, codes_ref)[:, 0:BLK]
            outs[i][q, 0:1, 0:BLK] = (labels >> 4).astype(jnp.float32).astype(jnp.bfloat16)
            outs[i][q, 16:17, 0:BLK] = (labels & 15).astype(jnp.float32).astype(jnp.bfloat16)


def first_kernel(shifts, slot_ref, send_ref, codes_ref, y_ref, own_ref, *refs):
    n = NX * NC * CHUNKS
    parts, outs, table, sems = refs[:n], refs[n:n + len(shifts)], refs[-2], refs[-1]
    fill(table, own_ref, parts, sems)
    follower_kernel(shifts, slot_ref, send_ref, codes_ref, y_ref, table, *outs)


def leader_kernel(slot_ref, codes_ref, y_ref, table, out, labels_ref):
    def row(i, carry):
        def emit(span, value):
            out[i, :, span] = value

        row_tiles(i, 0, table, slot_ref, y_ref, emit)
        labels_ref[pl.ds(i, 1), :] = label_row(i, slot_ref, codes_ref)
        return carry

    lax.fori_loop(0, HALF, row, 0)


ROW_COST = pl.CostEstimate(flops=2 * 8 * 6 * BLK * LANES * LANES, bytes_accessed=5_000_000, transcendentals=0)


def first_followers(shifts, slots, send, codes, own, y, parts):
    shape = jax.ShapeDtypeStruct((2, BLK, WIDE), jnp.bfloat16)
    table = jax.ShapeDtypeStruct((TABLE + ROWS + 1, 32, LANES), jnp.bfloat16)
    return pl.pallas_call(
        functools.partial(first_kernel, shifts),
        out_shape=[shape] * len(shifts) + [table],
        in_specs=[SMEM] * 3 + [VMEM] * 2 + [HBM] * len(parts),
        out_specs=[VMEM] * (len(shifts) + 1),
        scratch_shapes=[pltpu.SemaphoreType.DMA((len(parts),))],
        compiler_params=LIMIT,
        cost_estimate=ROW_COST,
        name="first",
    )(slots, send, codes, y, own, *parts)


def followers(shifts, slots, send, codes, y, table):
    shape = jax.ShapeDtypeStruct((2, BLK, WIDE), jnp.bfloat16)
    return pl.pallas_call(
        functools.partial(follower_kernel, shifts),
        out_shape=[shape] * len(shifts),
        in_specs=[SMEM] * 3 + [VMEM] * 2,
        out_specs=[VMEM] * len(shifts),
        compiler_params=LIMIT,
        cost_estimate=ROW_COST,
        name="followers",
    )(slots, send, codes, y, table)


def leaders(slots, codes, y, table):
    return pl.pallas_call(
        leader_kernel,
        out_shape=[
            jax.ShapeDtypeStruct((HALF, BLK, WIDE), jnp.bfloat16),
            jax.ShapeDtypeStruct((HALF, LANES), jnp.int32),
        ],
        in_specs=[SMEM] * 2 + [VMEM] * 2,
        out_specs=[VMEM] * 2,
        compiler_params=LIMIT,
        cost_estimate=ROW_COST,
        name="leaders",
    )(slots, codes, y, table)


def code_kernel(slots_ref, codes_ref):
    g = lax.axis_index(AXES[0])
    shape = (NG, 1, 2)
    spot = lax.broadcasted_iota(jnp.int32, shape, 0) * 2 + lax.broadcasted_iota(jnp.int32, shape, 2)
    codes = jnp.zeros(shape, jnp.int32)
    for i in range(HALF):
        codes = jnp.where(spot == slots_ref[0, i], g * (N_DEV * HALF) + i, codes)
    codes_ref[...] = codes


def code_rows(slots):
    return pl.pallas_call(
        code_kernel,
        out_shape=jax.ShapeDtypeStruct((NG, 1, 2), jnp.int32),
        in_specs=[SMEM],
        out_specs=VMEM,
        name="codes",
    )(slots)


NOTE = NZ * C + HALF


def note_kernel(send_ref, lists_ref, returned_ref, out):
    lane = lax.broadcasted_iota(jnp.int32, (NX * NC, 1, HALF), 2)
    mine = jnp.zeros((NX * NC, 1, HALF), jnp.int32)
    for t in range(NG):
        for q in range(2):
            mine = jnp.where(lane == send_ref[0, 2 * t + q], returned_ref[t:t + 1, :, q:q + 1], mine)
    out[:, :, 0:NZ * C] = lists_ref[...]
    out[:, :, NZ * C:] = mine


def note_rows(send, lists, returned):
    return pl.pallas_call(
        note_kernel,
        out_shape=jax.ShapeDtypeStruct((NX * NC, 1, NOTE), jnp.int32),
        in_specs=[SMEM, VMEM, VMEM],
        out_specs=VMEM,
        name="note",
    )(send, lists, returned)


def plane_kernel(note_ref, out, row_ref):
    for d in range(NX * NC):
        row_ref[:, d * HALF:(d + 1) * HALF] = note_ref[d][:, NZ * C:]
    for z in range(NZ):
        out[z] = row_ref[...]


def plane_rows(note):
    return pl.pallas_call(
        plane_kernel,
        out_shape=jax.ShapeDtypeStruct((NZ, 1, NX * NC * HALF), jnp.int32),
        in_specs=[VMEM],
        out_specs=VMEM,
        scratch_shapes=[pltpu.VMEM((1, NX * NC * HALF), jnp.int32)],
        name="plane",
    )(note)


def slot_kernel(columns_ref, lists_ref, slot_ref):
    g, x, z, c = (lax.axis_index(name) for name in AXES)
    device = x * (NZ * NC) + z * NC + c

    def row(i, carry):
        for k in range(K):
            column = columns_ref[i, k]
            ghost = jnp.maximum(column - ROWS, 0)
            local = column < ROWS
            asked = ghost >> 2
            peer = jnp.where(local, device, asked)
            wish = lists_ref[(asked >> 4) * NC + (asked & 1), 0, ((asked >> 1) & (NZ - 1)) * C + (ghost & 3)]
            row = jnp.where(local, jnp.maximum(column, 0), wish)
            px, pz, pc = peer >> 4, (peer >> 1) & (NZ - 1), peer & 1
            way = ((x - px) & (NX - 1)) * NC + (c ^ pc)
            at = jnp.where(local, TABLE + row, way * (NZ * C) + pz * C + (ghost & 3))
            late = row >= HALF
            spot = jnp.where(late, pz * (NX * NC * HALF) + (px * NC + pc) * HALF + row - HALF + 1, 0)
            offset = peer * HALF + 1 + jnp.where(late, 0, g * (N_DEV * HALF) + row)
            word = spot * (LABELS * SPOTS) + offset * SPOTS + at
            slot_ref[i, k] = jnp.where(column >= 0, word, TABLE + ROWS)
        return carry

    lax.fori_loop(0, ROWS, row, 0)


def slot_words(columns, lists):
    return pl.pallas_call(
        slot_kernel,
        out_shape=jax.ShapeDtypeStruct((ROWS, K), jnp.int32),
        in_specs=[SMEM] * 2,
        out_specs=SMEM,
        cost_estimate=pl.CostEstimate(flops=1_000_000, bytes_accessed=2_000_000, transcendentals=0),
        name="slots",
    )(columns, lists)


def merge_kernel(slots_ref, lead_ref, own_labels_ref, *refs):
    parts, out, labels_ref = refs[:NG], refs[NG], refs[NG + 1]
    follow, tiles, stage, sems, digits, work, steps_ref, next_ref, next_sem = refs[NG + 2:]
    per = SLOTS // 2

    lane = lax.broadcasted_iota(jnp.int32, (HALF, LANES), 1)
    for s in range(NG):
        for q in range(2):
            high = parts[s][q, 0:1, 0:LANES].astype(jnp.float32)
            rest = parts[s][q, 16:17, 0:LANES].astype(jnp.float32)
            digits[2 * s + q:2 * s + q + 1, :] = (high * 16.0 + rest).astype(jnp.int32)
    spots = []
    for n in range(HALF):
        spot = slots_ref[0, n]
        spots.append(((lax.axis_index(AXES[0]) - (spot >> 1)) & (NG - 1)) * 2 + (spot & 1))
        work[n:n + 1, :] = digits[pl.ds(spots[n], 1), :]
    labels = jnp.where(lane < 2 * K, pltpu.roll(work[...], K, 1), -1)
    work[...] = labels
    work[:, 0:K] = own_labels_ref[:, 0:K]
    labels = work[...]
    labels_ref[...] = work[:, 0:2 * K]
    twice = jnp.where(lane < 2 * K, labels, pltpu.roll(labels, 2 * K, 1))
    steps = jnp.full((HALF, LANES), 2 * K, jnp.int32)
    for d in range(2 * K - 1, 0, -1):
        steps = jnp.where(pltpu.roll(twice, LANES - d, 1) == labels, d, steps)
    steps = jnp.where((lane < 2 * K) & (labels >= 0), steps, 2 * K)
    usual = jnp.where((lane == 0) | (lane == K), K, 2 * K)
    odd = jnp.max(jnp.where(steps != usual, 1, 0), axis=1, keepdims=True)
    steps_ref[...] = jnp.where(lane == 2 * K, odd, steps)
    fetch = pltpu.make_async_copy(steps_ref, next_ref, next_sem)
    fetch.start()

    for s in range(NG):
        follow[2 * s:2 * s + 2] = parts[s][...]
    low = low_lanes((BLK, LANES))

    def save(n):
        return pltpu.make_async_copy(stage.at[n], out.at[n], sems.at[n])

    fetch.wait()
    for n in range(HALF):
        f = spots[n]

        def lead(t):
            return lead_ref[n, :, t * LANES:(t + 1) * LANES]

        def part(t):
            return follow[f, :, t * LANES:(t + 1) * LANES]

        first = lead(0).astype(jnp.float32)
        second = jnp.where(low, 0.0, part(0).astype(jnp.float32))
        stage[n, :, 0:LANES] = (first + pltpu.roll(second, BLK, 1)).astype(jnp.bfloat16)
        middle = lead(per - 1).astype(jnp.float32) + second
        middle = middle + jnp.where(low, 0.0, pltpu.roll(first, BLK, 1))
        stage[n, :, 5 * LANES:6 * LANES] = middle.astype(jnp.bfloat16)
        stage[n, :, LANES:5 * LANES] = lead_ref[n, :, LANES:5 * LANES]
        stage[n, :, 6 * LANES:] = follow[f, :, LANES:]

        @pl.when(next_ref[n, 2 * K] != 0)
        def _(n=n, lead=lead, part=part):
            for t in range(per):
                tiles[t] = lead(t).astype(jnp.float32)
                tiles[per + t] = part(t).astype(jnp.float32)
            plain = (next_ref[n, 0] == K) & (next_ref[n, K] == K)
            for s in range(2 * K):
                step = next_ref[n, s]
                skip = plain if s in (0, K) else step == 2 * K

                @pl.when(jnp.logical_not(skip))
                def _(s=s, step=step):
                    home = s if s < K else s + 2

                    def block(t):
                        spot = jnp.where(t < K, t, t + 2)
                        value = tiles[spot >> 1]
                        same = jnp.broadcast_to((spot & 1) == (home & 1), value.shape)
                        return jnp.where(same, value, pltpu.roll(value, BLK, 1))

                    def after(t, step):
                        t = t + step
                        return jnp.where(t >= 2 * K, t - 2 * K, t)

                    def more(carry):
                        return carry[0] != s

                    def add(carry):
                        t, total = carry
                        return after(t, next_ref[n, t]), total + block(t)

                    _, total = lax.while_loop(more, add, (after(s, step), block(jnp.int32(s))))
                    span = slice((s // 2) * LANES, (s // 2 + 1) * LANES)
                    keep = low if s % 2 == 0 else jnp.logical_not(low)
                    stage[n, :, span] = jnp.where(
                        keep, total, stage[n, :, span].astype(jnp.float32)
                    ).astype(jnp.bfloat16)

        save(n).start()
    for n in range(HALF):
        save(n).wait()


def merge(slots, lead, own_labels, parts):
    return pl.pallas_call(
        merge_kernel,
        out_shape=[
            jax.ShapeDtypeStruct((HALF, BLK, 2 * K * BLK), jnp.bfloat16),
            jax.ShapeDtypeStruct((HALF, 2 * K), jnp.int32),
        ],
        in_specs=[SMEM] + [VMEM] * (2 + NG),
        out_specs=[pl.BlockSpec(memory_space=pl.ANY), VMEM],
        scratch_shapes=[
            pltpu.VMEM((2 * NG, BLK, WIDE), jnp.bfloat16),
            pltpu.VMEM((SLOTS, BLK, LANES), jnp.float32),
            pltpu.VMEM((HALF, BLK, 2 * K * BLK), jnp.bfloat16),
            pltpu.SemaphoreType.DMA((HALF,)),
            pltpu.VMEM((HALF, LANES), jnp.int32),
            pltpu.VMEM((HALF, LANES), jnp.int32),
            pltpu.VMEM((HALF, LANES), jnp.int32),
            pltpu.SMEM((HALF, LANES), jnp.int32),
            pltpu.SemaphoreType.DMA,
        ],
        compiler_params=LIMIT,
        name="merge",
    )(slots, lead, own_labels, *parts)


def shift(value, axis, size, by):
    if by == 0:
        return value
    return lax.ppermute(value, axis, [(i, (i + by) % size) for i in range(size)])


def cross(value, b):
    if b == 0:
        return value
    by, flip = b // NC, b % NC
    pairs = [
        (x * NC + c, ((x + by) % NX) * NC + (c ^ flip)) for x in range(NX) for c in range(NC)
    ]
    return lax.ppermute(value, ("x", "core"), pairs)


def per_device(stiffness, prolongator, columns, fetch_rows, send_order, partner_slot):
    g, x, z, c = (lax.axis_index(name) for name in AXES)
    device = x * (NZ * NC) + z * NC + c
    own = prolongator.reshape(ROWS, 32, LANES)

    held = []
    for h in range(CHUNKS):
        piece = own[:, h * CK:(h + 1) * CK]
        got = {0: piece}
        for s in (4, 2, 6, 1, 7):
            got[s] = shift(piece, "z", NZ, s)
        got[5] = shift(got[4], "z", NZ, 1)
        got[3] = shift(got[4], "z", NZ, NZ - 1)
        held.append([got[s] for s in range(NZ)])

    returned = lax.all_to_all(code_rows(partner_slot), "grp", split_axis=0, concat_axis=0, tiled=True)
    lists = fetch_rows.reshape(NX, NZ, NC, C).transpose(0, 2, 1, 3).reshape(NX * NC, 1, NZ * C)
    note = note_rows(send_order, lists, returned)
    wanted = lax.all_to_all(note, ("x", "core"), split_axis=0, concat_axis=0, tiled=True)
    words = pltpu.with_memory_space_constraint(slot_words(columns, lists), pltpu.HBM)
    lane = jnp.arange(LANES, dtype=jnp.int32)
    inner = lane & (BLK - 1)
    source = (lane & BLK) + jnp.where(inner < 32, 2 * inner, 2 * (inner - 32) + 1)
    perm = (lane[:, None] == source[None, :]).astype(jnp.bfloat16)
    y = products(own, perm, stiffness)
    wanted, y = lax.optimization_barrier((wanted, y))
    codes = lax.all_to_all(plane_rows(wanted), "z", split_axis=0, concat_axis=0, tiled=True)

    parts = []
    for h in range(CHUNKS):
        chosen = []
        for targets in ORDER:
            chosen += select(targets, wanted, held[h])
            wanted, chosen[-1] = lax.optimization_barrier((wanted, chosen[-1]))
        moved = {b: cross(chosen[i], b) for i, b in enumerate(sum(ORDER, ()))}
        parts += [pltpu.with_memory_space_constraint(moved[b], pltpu.HBM) for b in range(NX * NC)]

    sent = {}
    sent[2], table = first_followers((2,), words, send_order, codes, own, y, parts)
    sent[1], sent[3], sent[0] = followers((1, 3, 0), words, send_order, codes, y, table)
    arrived = [shift(sent[s], "grp", NG, s) for s in range(NG)]
    lead, lead_labels = leaders(words, codes, y, table)
    return tuple(merge(partner_slot, lead, lead_labels, arrived))


def solution(mesh):
    grid = Mesh(mesh.devices.reshape(NG, NX, NZ, NC), AXES)
    return jax.shard_map(
        per_device,
        mesh=grid,
        in_specs=(
            P(AXES, None, None),
            P(AXES, None),
            P(AXES, None),
            P(AXES, None),
            P(AXES, None),
            P(AXES, None),
        ),
        out_specs=(P(AXES, None, None), P(AXES, None)),
        check_vma=False,
    )
```

```python
import functools

import jax
import jax.numpy as jnp
from jax import lax
from jax.experimental import pallas as pl
from jax.experimental.pallas import tpu as pltpu
from jax.sharding import Mesh, PartitionSpec as P

BLK = 64
K = 11
C = 4
ROWS = 16
HALF = 8
NG, NX, NZ, NC = 4, 4, 8, 2
N_DEV = NX * NZ * NC
LANES = 128
SLOTS = 12
WIDE = SLOTS * BLK
TABLE = N_DEV * C
SPOTS, LABELS = 512, 4096
CHUNKS = 1
CK = 32 // CHUNKS
AXES = ("grp", "x", "z", "core")
ORDER = ((2, 6, 4, 5, 1), (3, 7), (0,))

VMEM = pl.BlockSpec(memory_space=pltpu.VMEM)
SMEM = pl.BlockSpec(memory_space=pltpu.SMEM)
HBM = pl.BlockSpec(memory_space=pltpu.HBM)
LIMIT = pltpu.CompilerParams(vmem_limit_bytes=12 * 1024 * 1024)


def low_lanes(shape):
    return lax.broadcasted_iota(jnp.int32, shape, 1) < BLK


STEP = 4


def products_kernel(p_ref, perm_ref, a_hbm, y_ref, a_ref, work, sems):
    def load(h):
        rows = pl.ds(h * STEP, STEP)
        return pltpu.make_async_copy(a_hbm.at[rows], a_ref.at[rows], sems.at[h])

    for h in range(ROWS // STEP):
        load(h).start()
    perm = perm_ref[...]
    pad = jnp.zeros((BLK, BLK), jnp.float32)
    for h in range(ROWS // STEP):
        load(h).wait()
        for i in range(STEP):
            y = lax.dot_general(
                p_ref[h * STEP + i], a_ref[h * STEP + i], (((0,), (0,)), ((), ())),
                preferred_element_type=jnp.float32,
            )
            y = jnp.concatenate([y, pad] if h * STEP + i < HALF else [pad, y], axis=1)
            work[h, i * BLK:(i + 1) * BLK] = y.astype(jnp.bfloat16)
        for t in range(WIDE // LANES):
            span = slice(t * LANES, (t + 1) * LANES)
            y_ref[h * STEP:(h + 1) * STEP, :, span] = jnp.dot(
                work[h, :, span], perm, preferred_element_type=jnp.float32
            ).astype(jnp.bfloat16).reshape(STEP, BLK, LANES)


def products(blocks, perm, stiffness):
    return pl.pallas_call(
        products_kernel,
        out_shape=jax.ShapeDtypeStruct((ROWS, BLK, WIDE), jnp.bfloat16),
        in_specs=[VMEM, VMEM, HBM],
        out_specs=VMEM,
        scratch_shapes=[
            pltpu.VMEM((ROWS, BLK, K * BLK), jnp.bfloat16),
            pltpu.VMEM((ROWS // STEP, STEP * BLK, WIDE), jnp.bfloat16),
            pltpu.SemaphoreType.DMA((ROWS // STEP,)),
        ],
        compiler_params=LIMIT,
        cost_estimate=pl.CostEstimate(
            flops=2 * ROWS * BLK * BLK * WIDE * 3, bytes_accessed=3_200_000, transcendentals=0
        ),
        name="products",
    )(blocks, perm, stiffness)


def select_kernel(targets, wanted_ref, *refs):
    n = len(targets)
    held, outs, stage, sems = refs[:NZ], refs[NZ:NZ + n], refs[NZ + n], refs[NZ + n + 1]
    x, z, c = (lax.axis_index(name) for name in AXES[1:])
    copies = []
    for i, b in enumerate(targets):
        target = ((x + b // NC) & (NX - 1)) * NC + (c ^ (b % NC))
        for s in range(NZ):
            home = ((z - s) & (NZ - 1)) * C
            for m in range(C):
                stage[i, home + m] = held[s][wanted_ref[target, 0, home + m]]
        copy = pltpu.make_async_copy(stage.at[i], outs[i], sems.at[i])
        copy.start()
        copies.append(copy)
    for copy in copies:
        copy.wait()


def select(targets, wanted, held):
    n = len(targets)
    shape = (NZ * C, CK, LANES)
    return pl.pallas_call(
        functools.partial(select_kernel, targets),
        out_shape=[jax.ShapeDtypeStruct(shape, jnp.bfloat16)] * n,
        in_specs=[SMEM] + [VMEM] * NZ,
        out_specs=[HBM] * n,
        scratch_shapes=[pltpu.VMEM((n,) + shape, jnp.bfloat16), pltpu.SemaphoreType.DMA((n,))],
        compiler_params=LIMIT,
        name="select",
    )(wanted, *held)


def fill(table, own_ref, parts, sems):
    n = NX * NC
    copies = []
    for h in range(CHUNKS):
        for b in range(n):
            spot = table.at[pl.ds(b * NZ * C, NZ * C), pl.ds(h * CK, CK)]
            copies.append(pltpu.make_async_copy(parts[h * n + b], spot, sems.at[h * n + b]))
    for copy in copies:
        copy.start()
    table[TABLE:TABLE + ROWS] = own_ref[...]
    table[TABLE + ROWS] = jnp.zeros((32, LANES), jnp.bfloat16)
    for copy in copies:
        copy.wait()


def row_tiles(i, late, table, slot_ref, y_ref, emit):
    low = low_lanes((32, LANES))
    zero = jnp.zeros((32, LANES), jnp.bfloat16)
    for t in range(SLOTS // 2):
        a, b = (
            table[slot_ref[i, k] & (SPOTS - 1) if 0 <= k < K else TABLE + ROWS]
            for k in (2 * t - late, 2 * t + 1 - late)
        )
        rhs = jnp.concatenate([
            jnp.where(low, a, zero),
            jnp.where(low, pltpu.roll(a, BLK, 1), zero),
            jnp.where(low, zero, pltpu.roll(b, BLK, 1)),
            jnp.where(low, zero, b),
        ], axis=0)
        span = slice(t * LANES, (t + 1) * LANES)
        emit(span, jnp.dot(
            y_ref[i, :, span], rhs, preferred_element_type=jnp.float32
        ).astype(jnp.bfloat16))


def label_row(i, slot_ref, codes_ref):
    lane = lax.broadcasted_iota(jnp.int32, (1, LANES), 1)
    labels = jnp.full((1, LANES), -1, jnp.int32)
    for k in range(K):
        word = slot_ref[i, k]
        address = (word >> 21) - 1
        spot = jnp.maximum(address, 0)
        code = jnp.where(address < 0, 0, codes_ref[spot >> 6, 0, spot & 63])
        offset = ((word >> 9) & (LABELS - 1)) - 1
        labels = jnp.where(lane == k, offset + code, labels)
    return labels


def follower_kernel(shifts, slot_ref, send_ref, codes_ref, y_ref, *refs):
    outs = refs[len(refs) - len(shifts):]
    table = refs[0]
    for i, s in enumerate(shifts):
        target = (lax.axis_index(AXES[0]) + s) & (NG - 1)
        for q in range(2):
            row = HALF + send_ref[0, target * 2 + q]

            def emit(span, value, i=i, q=q):
                outs[i][q, :, span] = value

            row_tiles(row, 1, table, slot_ref, y_ref, emit)
            labels = label_row(row, slot_ref, codes_ref)[:, 0:BLK]
            outs[i][q, 0:1, 0:BLK] = (labels >> 4).astype(jnp.float32).astype(jnp.bfloat16)
            outs[i][q, 16:17, 0:BLK] = (labels & 15).astype(jnp.float32).astype(jnp.bfloat16)


def first_kernel(shifts, slot_ref, send_ref, codes_ref, y_ref, own_ref, *refs):
    n = NX * NC * CHUNKS
    parts, outs, table, sems = refs[:n], refs[n:n + len(shifts)], refs[-2], refs[-1]
    fill(table, own_ref, parts, sems)
    follower_kernel(shifts, slot_ref, send_ref, codes_ref, y_ref, table, *outs)


def leader_kernel(slot_ref, codes_ref, y_ref, table, out, labels_ref):
    def row(i, carry):
        def emit(span, value):
            out[i, :, span] = value

        row_tiles(i, 0, table, slot_ref, y_ref, emit)
        labels_ref[pl.ds(i, 1), :] = label_row(i, slot_ref, codes_ref)
        return carry

    lax.fori_loop(0, HALF, row, 0)


ROW_COST = pl.CostEstimate(flops=2 * 8 * 6 * BLK * LANES * LANES, bytes_accessed=5_000_000, transcendentals=0)


def first_followers(shifts, slots, send, codes, own, y, parts):
    shape = jax.ShapeDtypeStruct((2, BLK, WIDE), jnp.bfloat16)
    table = jax.ShapeDtypeStruct((TABLE + ROWS + 1, 32, LANES), jnp.bfloat16)
    return pl.pallas_call(
        functools.partial(first_kernel, shifts),
        out_shape=[shape] * len(shifts) + [table],
        in_specs=[SMEM] * 3 + [VMEM] * 2 + [HBM] * len(parts),
        out_specs=[VMEM] * (len(shifts) + 1),
        scratch_shapes=[pltpu.SemaphoreType.DMA((len(parts),))],
        compiler_params=LIMIT,
        cost_estimate=ROW_COST,
        name="first",
    )(slots, send, codes, y, own, *parts)


def followers(shifts, slots, send, codes, y, table):
    shape = jax.ShapeDtypeStruct((2, BLK, WIDE), jnp.bfloat16)
    return pl.pallas_call(
        functools.partial(follower_kernel, shifts),
        out_shape=[shape] * len(shifts),
        in_specs=[SMEM] * 3 + [VMEM] * 2,
        out_specs=[VMEM] * len(shifts),
        compiler_params=LIMIT,
        cost_estimate=ROW_COST,
        name="followers",
    )(slots, send, codes, y, table)


def leaders(slots, codes, y, table):
    return pl.pallas_call(
        leader_kernel,
        out_shape=[
            jax.ShapeDtypeStruct((HALF, BLK, WIDE), jnp.bfloat16),
            jax.ShapeDtypeStruct((HALF, LANES), jnp.int32),
        ],
        in_specs=[SMEM] * 2 + [VMEM] * 2,
        out_specs=[VMEM] * 2,
        compiler_params=LIMIT,
        cost_estimate=ROW_COST,
        name="leaders",
    )(slots, codes, y, table)


def code_kernel(slots_ref, codes_ref):
    g = lax.axis_index(AXES[0])
    shape = (NG, 1, 2)
    spot = lax.broadcasted_iota(jnp.int32, shape, 0) * 2 + lax.broadcasted_iota(jnp.int32, shape, 2)
    codes = jnp.zeros(shape, jnp.int32)
    for i in range(HALF):
        codes = jnp.where(spot == slots_ref[0, i], g * (N_DEV * HALF) + i, codes)
    codes_ref[...] = codes


def code_rows(slots):
    return pl.pallas_call(
        code_kernel,
        out_shape=jax.ShapeDtypeStruct((NG, 1, 2), jnp.int32),
        in_specs=[SMEM],
        out_specs=VMEM,
        name="codes",
    )(slots)


NOTE = NZ * C + HALF


def note_kernel(send_ref, lists_ref, returned_ref, out):
    lane = lax.broadcasted_iota(jnp.int32, (NX * NC, 1, HALF), 2)
    mine = jnp.zeros((NX * NC, 1, HALF), jnp.int32)
    for t in range(NG):
        for q in range(2):
            mine = jnp.where(lane == send_ref[0, 2 * t + q], returned_ref[t:t + 1, :, q:q + 1], mine)
    out[:, :, 0:NZ * C] = lists_ref[...]
    out[:, :, NZ * C:] = mine


def note_rows(send, lists, returned):
    return pl.pallas_call(
        note_kernel,
        out_shape=jax.ShapeDtypeStruct((NX * NC, 1, NOTE), jnp.int32),
        in_specs=[SMEM, VMEM, VMEM],
        out_specs=VMEM,
        name="note",
    )(send, lists, returned)


def plane_kernel(note_ref, out, row_ref):
    for d in range(NX * NC):
        row_ref[:, d * HALF:(d + 1) * HALF] = note_ref[d][:, NZ * C:]
    for z in range(NZ):
        out[z] = row_ref[...]


def plane_rows(note):
    return pl.pallas_call(
        plane_kernel,
        out_shape=jax.ShapeDtypeStruct((NZ, 1, NX * NC * HALF), jnp.int32),
        in_specs=[VMEM],
        out_specs=VMEM,
        scratch_shapes=[pltpu.VMEM((1, NX * NC * HALF), jnp.int32)],
        name="plane",
    )(note)


def slot_kernel(columns_ref, fetch_ref, slot_ref):
    g, x, z, c = (lax.axis_index(name) for name in AXES)
    device = x * (NZ * NC) + z * NC + c

    def row(i, carry):
        for k in range(K):
            column = columns_ref[i, k]
            ghost = jnp.maximum(column - ROWS, 0)
            local = column < ROWS
            asked = ghost >> 2
            peer = jnp.where(local, device, asked)
            row = jnp.where(local, jnp.maximum(column, 0), fetch_ref[asked, ghost & 3])
            px, pz, pc = peer >> 4, (peer >> 1) & (NZ - 1), peer & 1
            way = ((x - px) & (NX - 1)) * NC + (c ^ pc)
            at = jnp.where(local, TABLE + row, way * (NZ * C) + pz * C + (ghost & 3))
            late = row >= HALF
            spot = jnp.where(late, pz * (NX * NC * HALF) + (px * NC + pc) * HALF + row - HALF + 1, 0)
            offset = peer * HALF + 1 + jnp.where(late, 0, g * (N_DEV * HALF) + row)
            word = spot * (LABELS * SPOTS) + offset * SPOTS + at
            slot_ref[i, k] = jnp.where(column >= 0, word, TABLE + ROWS)
        return carry

    lax.fori_loop(0, ROWS, row, 0)


def slot_words(columns, fetch):
    return pl.pallas_call(
        slot_kernel,
        out_shape=jax.ShapeDtypeStruct((ROWS, K), jnp.int32),
        in_specs=[SMEM] * 2,
        out_specs=SMEM,
        cost_estimate=pl.CostEstimate(flops=1_000_000, bytes_accessed=2_000_000, transcendentals=0),
        name="slots",
    )(columns, fetch)


def merge_kernel(slots_ref, lead_ref, own_labels_ref, *refs):
    parts, out, labels_ref = refs[:NG], refs[NG], refs[NG + 1]
    follow, tiles, stage, sems, digits, work, steps_ref, next_ref, next_sem = refs[NG + 2:]
    per = SLOTS // 2

    lane = lax.broadcasted_iota(jnp.int32, (HALF, LANES), 1)
    for s in range(NG):
        for q in range(2):
            high = parts[s][q, 0:1, 0:LANES].astype(jnp.float32)
            rest = parts[s][q, 16:17, 0:LANES].astype(jnp.float32)
            digits[2 * s + q:2 * s + q + 1, :] = (high * 16.0 + rest).astype(jnp.int32)
    spots = []
    for n in range(HALF):
        spot = slots_ref[0, n]
        spots.append(((lax.axis_index(AXES[0]) - (spot >> 1)) & (NG - 1)) * 2 + (spot & 1))
        work[n:n + 1, :] = digits[pl.ds(spots[n], 1), :]
    labels = jnp.where(lane < 2 * K, pltpu.roll(work[...], K, 1), -1)
    work[...] = labels
    work[:, 0:K] = own_labels_ref[:, 0:K]
    labels = work[...]
    labels_ref[...] = work[:, 0:2 * K]
    twice = jnp.where(lane < 2 * K, labels, pltpu.roll(labels, 2 * K, 1))
    steps = jnp.full((HALF, LANES), 2 * K, jnp.int32)
    for d in range(2 * K - 1, 0, -1):
        steps = jnp.where(pltpu.roll(twice, LANES - d, 1) == labels, d, steps)
    steps = jnp.where((lane < 2 * K) & (labels >= 0), steps, 2 * K)
    usual = jnp.where((lane == 0) | (lane == K), K, 2 * K)
    odd = jnp.max(jnp.where(steps != usual, 1, 0), axis=1, keepdims=True)
    steps_ref[...] = jnp.where(lane == 2 * K, odd, steps)
    fetch = pltpu.make_async_copy(steps_ref, next_ref, next_sem)
    fetch.start()

    for s in range(NG):
        follow[2 * s:2 * s + 2] = parts[s][...]
    low = low_lanes((BLK, LANES))

    def save(n):
        return pltpu.make_async_copy(stage.at[n], out.at[n], sems.at[n])

    fetch.wait()
    for n in range(HALF):
        f = spots[n]

        def lead(t):
            return lead_ref[n, :, t * LANES:(t + 1) * LANES]

        def part(t):
            return follow[f, :, t * LANES:(t + 1) * LANES]

        first = lead(0).astype(jnp.float32)
        second = jnp.where(low, 0.0, part(0).astype(jnp.float32))
        stage[n, :, 0:LANES] = (first + pltpu.roll(second, BLK, 1)).astype(jnp.bfloat16)
        middle = lead(per - 1).astype(jnp.float32) + second
        middle = middle + jnp.where(low, 0.0, pltpu.roll(first, BLK, 1))
        stage[n, :, 5 * LANES:6 * LANES] = middle.astype(jnp.bfloat16)
        stage[n, :, LANES:5 * LANES] = lead_ref[n, :, LANES:5 * LANES]
        stage[n, :, 6 * LANES:] = follow[f, :, LANES:]

        @pl.when(next_ref[n, 2 * K] != 0)
        def _(n=n, lead=lead, part=part):
            for t in range(per):
                tiles[t] = lead(t).astype(jnp.float32)
                tiles[per + t] = part(t).astype(jnp.float32)
            plain = (next_ref[n, 0] == K) & (next_ref[n, K] == K)
            for s in range(2 * K):
                step = next_ref[n, s]
                skip = plain if s in (0, K) else step == 2 * K

                @pl.when(jnp.logical_not(skip))
                def _(s=s, step=step):
                    home = s if s < K else s + 2

                    def block(t):
                        spot = jnp.where(t < K, t, t + 2)
                        value = tiles[spot >> 1]
                        same = jnp.broadcast_to((spot & 1) == (home & 1), value.shape)
                        return jnp.where(same, value, pltpu.roll(value, BLK, 1))

                    def after(t, step):
                        t = t + step
                        return jnp.where(t >= 2 * K, t - 2 * K, t)

                    def more(carry):
                        return carry[0] != s

                    def add(carry):
                        t, total = carry
                        return after(t, next_ref[n, t]), total + block(t)

                    _, total = lax.while_loop(more, add, (after(s, step), block(jnp.int32(s))))
                    span = slice((s // 2) * LANES, (s // 2 + 1) * LANES)
                    keep = low if s % 2 == 0 else jnp.logical_not(low)
                    stage[n, :, span] = jnp.where(
                        keep, total, stage[n, :, span].astype(jnp.float32)
                    ).astype(jnp.bfloat16)

        save(n).start()
    for n in range(HALF):
        save(n).wait()


def merge(slots, lead, own_labels, parts):
    return pl.pallas_call(
        merge_kernel,
        out_shape=[
            jax.ShapeDtypeStruct((HALF, BLK, 2 * K * BLK), jnp.bfloat16),
            jax.ShapeDtypeStruct((HALF, 2 * K), jnp.int32),
        ],
        in_specs=[SMEM] + [VMEM] * (2 + NG),
        out_specs=[pl.BlockSpec(memory_space=pl.ANY), VMEM],
        scratch_shapes=[
            pltpu.VMEM((2 * NG, BLK, WIDE), jnp.bfloat16),
            pltpu.VMEM((SLOTS, BLK, LANES), jnp.float32),
            pltpu.VMEM((HALF, BLK, 2 * K * BLK), jnp.bfloat16),
            pltpu.SemaphoreType.DMA((HALF,)),
            pltpu.VMEM((HALF, LANES), jnp.int32),
            pltpu.VMEM((HALF, LANES), jnp.int32),
            pltpu.VMEM((HALF, LANES), jnp.int32),
            pltpu.SMEM((HALF, LANES), jnp.int32),
            pltpu.SemaphoreType.DMA,
        ],
        compiler_params=LIMIT,
        name="merge",
    )(slots, lead, own_labels, *parts)


def shift(value, axis, size, by):
    if by == 0:
        return value
    return lax.ppermute(value, axis, [(i, (i + by) % size) for i in range(size)])


def cross(value, b):
    if b == 0:
        return value
    by, flip = b // NC, b % NC
    pairs = [
        (x * NC + c, ((x + by) % NX) * NC + (c ^ flip)) for x in range(NX) for c in range(NC)
    ]
    return lax.ppermute(value, ("x", "core"), pairs)


def per_device(stiffness, prolongator, columns, fetch_rows, send_order, partner_slot):
    g, x, z, c = (lax.axis_index(name) for name in AXES)
    device = x * (NZ * NC) + z * NC + c
    own = prolongator.reshape(ROWS, 32, LANES)

    held = []
    for h in range(CHUNKS):
        piece = own[:, h * CK:(h + 1) * CK]
        got = {0: piece}
        for s in (4, 2, 6, 1, 7):
            got[s] = shift(piece, "z", NZ, s)
        got[5] = shift(got[4], "z", NZ, 1)
        got[3] = shift(got[4], "z", NZ, NZ - 1)
        held.append([got[s] for s in range(NZ)])

    returned = lax.all_to_all(code_rows(partner_slot), "grp", split_axis=0, concat_axis=0, tiled=True)
    lists = fetch_rows.reshape(NX, NZ, NC, C).transpose(0, 2, 1, 3).reshape(NX * NC, 1, NZ * C)
    note = note_rows(send_order, lists, returned)
    wanted = lax.all_to_all(note, ("x", "core"), split_axis=0, concat_axis=0, tiled=True)
    words = pltpu.with_memory_space_constraint(slot_words(columns, fetch_rows), pltpu.HBM)
    lane = jnp.arange(LANES, dtype=jnp.int32)
    inner = lane & (BLK - 1)
    source = (lane & BLK) + jnp.where(inner < 32, 2 * inner, 2 * (inner - 32) + 1)
    perm = (lane[:, None] == source[None, :]).astype(jnp.bfloat16)
    y = products(prolongator.reshape(ROWS, BLK, BLK), perm, stiffness)
    wanted, y = lax.optimization_barrier((wanted, y))
    codes = lax.all_to_all(plane_rows(wanted), "z", split_axis=0, concat_axis=0, tiled=True)

    parts = []
    for h in range(CHUNKS):
        chosen = []
        for targets in ORDER:
            chosen += select(targets, wanted, held[h])
            wanted, chosen[-1] = lax.optimization_barrier((wanted, chosen[-1]))
        moved = {b: cross(chosen[i], b) for i, b in enumerate(sum(ORDER, ()))}
        parts += [pltpu.with_memory_space_constraint(moved[b], pltpu.HBM) for b in range(NX * NC)]

    sent = {}
    sent[2], sent[1], table = first_followers((2, 1), words, send_order, codes, own, y, parts)
    sent[3], sent[0] = followers((3, 0), words, send_order, codes, y, table)
    arrived = [shift(sent[s], "grp", NG, s) for s in range(NG)]
    lead, lead_labels = leaders(words, codes, y, table)
    return tuple(merge(partner_slot, lead, lead_labels, arrived))


def solution(mesh):
    grid = Mesh(mesh.devices.reshape(NG, NX, NZ, NC), AXES)
    return jax.shard_map(
        per_device,
        mesh=grid,
        in_specs=(
            P(AXES, None, None),
            P(AXES, None),
            P(AXES, None),
            P(AXES, None),
            P(AXES, None),
            P(AXES, None),
        ),
        out_specs=(P(AXES, None, None), P(AXES, None)),
        check_vma=False,
    )
```
